32 devices in a mesh: dp: 8 (over y, x, core), tensor: 4 (over z).
Axes of the slice: x: 2, y: 2, z: 4, core: 2. Of those that a mesh axis runs over, the one named last changes fastest.
Arguments:
- inputs: bfloat16 [16384, 768], P(('dp', 'tensor')), may hold values from -6 to 6
- out_grad: bfloat16 [16384, 768], P(('dp', 'tensor')), may hold values from -6 to 6
- seq_lengths: int32 [8, 3], P('dp'), may hold values from 1 to 1024, 2048 in all within a row
- balance: int32 [8, 2048], P('dp'), may hold values from 0 to 2047, each once within a row
- clusters: int32 [8, 12, 2048], P('dp', 'tensor'), may hold values from 0 to 2047, each once within a row
- query_weight: bfloat16 [768, 768], P('dp', 'tensor'), may hold values from -0.21875 to 0.21875
- query_bias: float32 [768], P('tensor'), may hold values from -3 to 3
- key_weight: bfloat16 [768, 768], P('dp', 'tensor'), may hold values from -0.21875 to 0.21875
- value_weight: bfloat16 [768, 768], P('dp', 'tensor'), may hold values from -0.21875 to 0.21875
- value_bias: float32 [768], P('tensor'), may hold values from -3 to 3
- out_weight: bfloat16 [768, 768], P('tensor', 'dp'), may hold values from -0.875 to 0.875
- out_bias: float32 [768], replicated, may hold values from -3 to 3
- norm1_gain: float32 [768], replicated, may hold values from 0.1 to 1.9
- norm1_bias: float32 [768], replicated, may hold values from -3 to 3
- up_weight: bfloat16 [768, 3072], P('dp', 'tensor'), may hold values from -0.21875 to 0.21875
- up_bias: float32 [3072], P('tensor'), may hold values from -3 to 3
- down_weight: bfloat16 [3072, 768], P('tensor', 'dp'), may hold values from -0.109375 to 0.109375
- down_bias: float32 [768], replicated, may hold values from -3 to 3
- norm2_gain: float32 [768], replicated, may hold values from 0.1 to 1.9
- norm2_bias: float32 [768], replicated, may hold values from -3 to 3
Outputs:
- layer_out: bfloat16 [16384, 768], P(('dp', 'tensor'))
- grad_inputs: float32 [16384, 768], P(('dp', 'tensor'))
- grad_query_weight: float32 [768, 768], P('dp', 'tensor')
- grad_query_bias: float32 [768], P('tensor')
- grad_key_weight: float32 [768, 768], P('dp', 'tensor')
- grad_value_weight: float32 [768, 768], P('dp', 'tensor')
- grad_value_bias: float32 [768], P('tensor')
- grad_out_weight: float32 [768, 768], P('tensor', 'dp')
- grad_out_bias: float32 [768], replicated
- grad_norm1_gain: float32 [768], replicated
- grad_norm1_bias: float32 [768], replicated
- grad_up_weight: float32 [768, 3072], P('dp', 'tensor')
- grad_up_bias: float32 [3072], P('tensor')
- grad_down_weight: float32 [3072, 768], P('tensor', 'dp')
- grad_down_bias: float32 [768], replicated
- grad_norm2_gain: float32 [768], replicated
- grad_norm2_bias: float32 [768], replicated
The draws below stay inside these ranges and needn't reach their ends.
Inputs may be any that keep to these rules, and one draw needn't show every extreme that they name: `seq_lengths`: each group's lengths sum to 2048; the largest in each group is exactly 1024. `balance`: each group's row is a permutation of its 2048 token indices. `clusters`: each head's row of a group is a permutation of the 2048 balanced positions.
All inputs are finite; a program needn't handle non-finite values.
Results may differ from the reference program's by a relative error of at most 0.019.
Values may be sent and summed in bfloat16 or wider, within the bound.
No kernel may reach another device: no remote copies, remote signals or barrier semaphores. Data moves between devices by JAX's collectives and lax.ppermute only.
A program may use at most 128 MiB of HBM per device.

```python
import math
import jax
import jax.numpy as jnp
import numpy as np
from jax import lax

D = 768
H = 12
HD = 64
FF = 3072
SEQS = 3
CL = 128
TOK_G = 2048
MAXLEN = 1024
TOKENS = 16384
N_DP = 8


def level_of(own_key, dims, shards, smallest, largest):
    def one(position, parts):
        draws = jax.random.uniform(jax.random.fold_in(jax.random.fold_in(own_key, 6), position), (parts,), jnp.float32, smallest / len(shards), largest / len(shards))
        return jnp.repeat(jnp.exp(draws), dims[position] // parts).reshape((-1,) + (1,) * (len(dims) - position - 1))

    loudness = one(*shards[0])
    for cut in shards[1:]:
        loudness = loudness * one(*cut)
    return loudness


def profile(number_of, total, bound, skew):
    loads = [(1 << 20) // math.isqrt(grade ** skew) + 1 for grade in range(2, number_of + 1)]
    rest, given = total - bound - (number_of - 1), [1] * (number_of - 1)
    while rest > 0:
        movable = [i for i in range(number_of - 1) if given[i] < bound]
        pool, left = sum([loads[i] for i in movable]), rest
        for i in movable:
            addition = min(bound - given[i], max(1, left * loads[i] // pool), rest)
            given[i] = given[i] + addition
            rest = rest - addition
    return np.array([bound] + given)


def uneven(rng, count, total, reach, skew):
    if count == 2:
        one = jax.random.randint(rng, (), max(1, total - reach), min(reach, total - 1) + 1)
        return jnp.stack([one, total - one])
    sizes = jnp.asarray(profile(count, total, reach, skew), jnp.int32)
    couples = (count - 1) // 2
    giver, receiver = sizes[1:1 + 2 * couples:2], sizes[2:2 + 2 * couples:2]
    room = jnp.minimum(giver - 1, reach - receiver)
    shifted = jax.random.randint(jax.random.fold_in(rng, 1), (couples,), 0, 1 << 20) % (room + 1)
    sizes = sizes.at[1:1 + 2 * couples:2].set(giver - shifted).at[2:2 + 2 * couples:2].set(receiver + shifted)
    return sizes[jax.random.permutation(jax.random.fold_in(rng, 2), count)]


def centred(rng, extent, width, limit, shards=(), kind=jnp.bfloat16):
    drawn = jax.random.normal(rng, extent, jnp.float32) * width
    if len(shards) > 0:
        drawn = level_of(rng, extent, shards, -0.22, 0.18) * drawn
    return jnp.clip(drawn, min=-limit, max=limit).astype(kind)


def setup_inputs(seed: int = 0) -> dict:
    key_list = jax.random.split(jax.random.key(seed), 21)
    return {
        "inputs": centred(key_list[0], (TOKENS, D), 1.0, 6.0, ((0, 32),)),
        "out_grad": centred(key_list[1], (TOKENS, D), 1.0, 6.0, ((0, 32),)),
        "seq_lengths": jax.vmap(lambda own: uneven(own, SEQS, TOK_G, MAXLEN, 2))(jax.random.split(key_list[2], N_DP)).reshape((N_DP, SEQS)).astype(jnp.int32),
        "balance": jax.vmap(lambda own: jax.random.permutation(own, TOK_G))(jax.random.split(key_list[3], N_DP)).reshape((N_DP, TOK_G)).astype(jnp.int32),
        "clusters": jax.vmap(lambda own: jax.random.permutation(own, TOK_G))(jax.random.split(key_list[4], N_DP * H)).reshape((N_DP, H, TOK_G)).astype(jnp.int32),
        "query_weight": centred(key_list[5], (D, D), D ** -0.5, 0.21875, ((0, 8), (1, 4))),
        "query_bias": centred(key_list[6], (D,), 0.5, 3.0, ((0, 4),), jnp.float32),
        "key_weight": centred(key_list[7], (D, D), D ** -0.5, 0.21875, ((0, 8), (1, 4))),
        "value_weight": centred(key_list[8], (D, D), D ** -0.5, 0.21875, ((0, 8), (1, 4))),
        "value_bias": centred(key_list[9], (D,), 0.5, 3.0, ((0, 4),), jnp.float32),
        "out_weight": centred(key_list[10], (D, D), (D // 16) ** -0.5, 0.875, ((0, 4), (1, 8))),
        "out_bias": centred(key_list[11], (D,), 0.5, 3.0, (), jnp.float32),
        "norm1_gain": jnp.clip(1.0 + 0.18 * jax.random.normal(key_list[12], (D,), jnp.float32), 0.1, 1.9),
        "norm1_bias": centred(key_list[13], (D,), 0.5, 3.0, (), jnp.float32),
        "up_weight": centred(key_list[14], (D, FF), D ** -0.5, 0.21875, ((0, 8), (1, 4))),
        "up_bias": centred(key_list[15], (FF,), 0.5, 3.0, ((0, 4),), jnp.float32),
        "down_weight": centred(key_list[16], (FF, D), FF ** -0.5, 0.109375, ((0, 4), (1, 8))),
        "down_bias": centred(key_list[17], (D,), 0.5, 3.0, (), jnp.float32),
        "norm2_gain": jnp.clip(1.0 + 0.18 * jax.random.normal(key_list[18], (D,), jnp.float32), 0.1, 1.9),
        "norm2_bias": centred(key_list[19], (D,), 0.5, 3.0, (), jnp.float32),
    }


@jax.custom_vjp
def low(v):
    return lax.optimization_barrier(v.astype(jnp.bfloat16)).astype(jnp.float32)

@jax.custom_vjp
def low_back(v):
    return v

def low_keep(v):
    return (low(v), None)

def low_pass(kept, grad):
    return (grad,)

def back_keep(v):
    return (v, None)

def back_low(kept, grad):
    return (low(grad),)
low.defvjp(low_keep, low_pass)
low_back.defvjp(back_keep, back_low)

def low_both(values_in):
    return low_back(low(values_in))

def matmul(left, right):
    return jnp.dot(left, right, precision=lax.Precision.HIGHEST)

def layer_norm(values_in, gain, shift):
    center = values_in - lax.optimization_barrier(jnp.mean(values_in, axis=-1, keepdims=True))
    variance = lax.optimization_barrier(jnp.mean(center * center, axis=-1, keepdims=True))
    return center * lax.rsqrt(variance + 1e-06) * gain + shift

def head_block(bundle, segment):
    query_head, key_head, value_head, slot_order, token_place = bundle
    cluster_count = slot_order.shape[0] // CL
    query_slots = jnp.take(query_head, slot_order, axis=0).reshape(cluster_count, CL, HD)
    key_slots = jnp.take(key_head, slot_order, axis=0).reshape(cluster_count, CL, HD)
    value_slots = jnp.take(value_head, slot_order, axis=0).reshape(cluster_count, CL, HD)
    segment_slots = jnp.take(segment, slot_order, axis=0).reshape(cluster_count, CL)
    same_doc = segment_slots[:, :, None] == segment_slots[:, None, :]
    raw_scores = jnp.einsum('cqd,ckd->cqk', query_slots, key_slots, precision=lax.Precision.HIGHEST) * HD ** (-0.5)
    scores = low_back(jnp.where(same_doc, raw_scores, -1e+30))
    prob_low = low(jax.nn.softmax(scores, axis=-1))
    context = jnp.einsum('cqk,ckd->cqd', prob_low, value_slots, precision=lax.Precision.HIGHEST).reshape(-1, HD)
    return jnp.take(context, token_place, axis=0)

def layer_forward(params, inputs, segment, slot_order, token_place):
    query_weight, query_bias, key_weight, value_weight, value_bias, out_weight, out_bias, norm1_gain, norm1_bias, up_weight, up_bias, down_weight, down_bias, norm2_gain, norm2_bias = params
    token_count = inputs.shape[0]
    query_rows = low_both(matmul(inputs, query_weight) + query_bias)
    key_rows = low_both(matmul(inputs, key_weight))
    value_rows = low_both(matmul(inputs, value_weight) + value_bias)

    def split_heads(values_in):
        return values_in.reshape(token_count, H, HD).transpose(1, 0, 2)

    def one_head(bundle):
        return head_block(bundle, segment)
    context = lax.map(jax.checkpoint(one_head), (split_heads(query_rows), split_heads(key_rows), split_heads(value_rows), slot_order, token_place))
    context = low_both(context.transpose(1, 0, 2).reshape(token_count, D))
    attention = low_back(matmul(context, out_weight))
    summed = inputs + attention + out_bias
    normed = layer_norm(summed, norm1_gain, norm1_bias)
    normed_low = low(normed)
    up_value = low_back(matmul(normed_low, up_weight) + up_bias)
    active = low(jax.nn.gelu(up_value, approximate=True))
    feed = low_back(matmul(active, down_weight))
    return layer_norm(normed + feed + down_bias, norm2_gain, norm2_bias)

def reference(inputs, out_grad, seq_lengths, balance, clusters, query_weight, query_bias, key_weight, value_weight, value_bias, out_weight, out_bias, norm1_gain, norm1_bias, up_weight, up_bias, down_weight, down_bias, norm2_gain, norm2_bias):
    params = tuple((item.astype(jnp.float32) for item in (query_weight, query_bias, key_weight, value_weight, value_bias, out_weight, out_bias, norm1_gain, norm1_bias, up_weight, up_bias, down_weight, down_bias, norm2_gain, norm2_bias)))
    positions = jnp.arange(TOK_G, dtype=jnp.int32)
    group_inputs = inputs.reshape(N_DP, TOK_G, D)
    group_grads = out_grad.reshape(N_DP, TOK_G, D)

    def one_group(totals, bundle):
        rows_in, rows_grad, lengths_row, balance_row, cluster_rows = bundle
        bounds = jnp.cumsum(lengths_row).astype(jnp.int32)
        segment = lax.optimization_barrier(jnp.sum((positions[:, None] >= bounds[None, :]).astype(jnp.int32), axis=1)).astype(jnp.int32)
        slot_order = jnp.take(balance_row, cluster_rows, axis=0).astype(jnp.int32)
        token_place = jax.vmap(lambda row_order: jnp.zeros((TOK_G,), jnp.int32).at[row_order].set(positions))(slot_order)

        def forward(param_set, layer_in):
            return layer_forward(param_set, layer_in, segment, slot_order, token_place)
        result, pull = jax.vjp(forward, params, rows_in.astype(jnp.float32))
        grad_params, grad_rows = pull(rows_grad.astype(jnp.float32))
        totals = jax.tree.map(lambda first, second: first + second, totals, grad_params)
        return (totals, (result.astype(jnp.bfloat16), grad_rows))
    start_totals = jax.tree.map(jnp.zeros_like, params)
    totals, (layer_out, grad_inputs) = lax.scan(one_group, start_totals, (group_inputs, group_grads, seq_lengths, balance, clusters))
    return (layer_out.reshape(TOKENS, D), grad_inputs.reshape(TOKENS, D), totals[0], totals[1], totals[2], totals[3], totals[4], totals[5], totals[6], totals[7], totals[8], totals[9], totals[10], totals[11], totals[12], totals[13], totals[14])
```

```python
import functools

import jax
import jax.numpy as jnp
from jax import lax
from jax.experimental import pallas as pl
from jax.experimental.pallas import tpu as pltpu
from jax.sharding import Mesh, PartitionSpec as P

HD = 64
CL = 128
BLK = 256
F32 = jnp.float32
BF16 = jnp.bfloat16
EPS = 1e-06


def nn(left, right):
    return jnp.dot(left, right, preferred_element_type=F32)


def nt(left, right):
    return lax.dot_general(left, right, (((1,), (1,)), ((), ())), preferred_element_type=F32)


def tn(left, right):
    return lax.dot_general(left, right, (((0,), (0,)), ((), ())), preferred_element_type=F32)


def order_kernel(seqs, scal_ref, clusters_ref, balance_ref, order_ref, seg_ref):
    count = balance_ref.shape[1]
    rows = scal_ref[1]
    balance = balance_ref[...]
    high = balance // 64
    low = balance - high * 64
    pick = lax.broadcasted_iota(jnp.int32, (8, count), 0)
    table = jnp.where(pick == 0, high, jnp.where(pick == 1, low, 0)).astype(F32).astype(BF16)
    chosen = clusters_ref[0]
    total = jnp.zeros((8, count), F32)
    for start in range(0, count, BLK):
        place = lax.broadcasted_iota(jnp.int32, (BLK, count), 0) + start
        hot = jnp.where(place == chosen, 1.0, 0.0).astype(BF16)
        total = total + nn(table[:, start : start + BLK], hot)
    token = (total[0:1] * 64.0 + total[1:2]).astype(jnp.int32)
    segment = jnp.zeros_like(token)
    for s in range(seqs):
        segment = segment + jnp.where(token >= scal_ref[2 + s], 1, 0)
    seg_ref[0] = segment.astype(F32)
    shift = scal_ref[0] * rows
    from_own = shift - (token // rows) * rows
    from_own = jnp.where(from_own < 0, from_own + count, from_own)
    order_ref[0] = (from_own + token % rows).astype(F32)


def column(row):
    return jnp.transpose(jnp.broadcast_to(row, (CL, CL)))


def slots_by_tokens(order_ref, start, count):
    lane = lax.broadcasted_iota(jnp.int32, (CL, CL), 1).astype(F32)
    parts = []
    for half in range(BLK // CL):
        gap = column(order_ref[0, :, pl.ds(start + half * CL, CL)]) - lane
        parts.append(
            jnp.concatenate(
                [jnp.where(gap == float(j * CL), 1.0, 0.0).astype(BF16) for j in range(count // CL)],
                axis=1,
            )
        )
    return jnp.concatenate(parts, axis=0)


def tokens_by_slots(order_ref, start, count):
    row = order_ref[0] - jnp.asarray(start, F32)
    place = lax.broadcasted_iota(jnp.int32, (BLK, count), 0).astype(F32)
    return jnp.where(place == row, 1.0, 0.0).astype(BF16)


def softmax_of(first, second, seg_ref, start):
    scores = nt(first, second) * HD ** (-0.5)
    seg_row = seg_ref[0, :, pl.ds(start, CL)]
    scores = jnp.where(column(seg_row) == seg_row, scores, -1e30)
    raised = jnp.exp(scores - jnp.max(scores, axis=1, keepdims=True))
    return raised / jnp.sum(raised, axis=1, keepdims=True)


def upper_half(values):
    lane = lax.broadcasted_iota(jnp.int32, values.shape, 1)
    return jnp.where(lane >= HD, values, 0.0)


def forward_kernel(blocks, order_ref, seg_ref, x_ref, w_ref, b_ref, slots_ref, out_ref, qkv_ref, ctx_ref):
    count = x_ref.shape[0]
    for start in range(0, count, BLK):
        qkv_ref[start : start + BLK] = (nn(x_ref[start : start + BLK], w_ref[0]) + b_ref[0]).astype(BF16)

    def gather(i, carry):
        start = pl.multiple_of(i * BLK, BLK)
        hot = slots_by_tokens(order_ref, start, count)
        picked = nn(hot, qkv_ref[...]).astype(BF16)
        slots_ref[0, pl.ds(start, BLK)] = picked
        for half in range(BLK // CL):
            part = picked[half * CL : (half + 1) * CL]
            first, second = part[:, :CL], part[:, CL:]
            probs = softmax_of(first, second, seg_ref, start + half * CL)
            context = nn(probs.astype(BF16), first)
            ctx_ref[pl.ds(start + half * CL, CL)] = upper_half(context).astype(BF16)
        return carry

    lax.fori_loop(0, count // BLK, gather, 0)
    rows = count // blocks

    def give(i, carry):
        def one(start):
            return nn(tokens_by_slots(order_ref, start, count), ctx_ref[...])

        for r in range(0, rows // 2, BLK):
            base = i * rows + r
            packed = pltpu.roll(one(base), HD, 1) + one(base + rows // 2)
            out_ref[i, r : r + BLK] = packed.astype(BF16)
        return carry

    lax.fori_loop(0, blocks, give, 0)


def backward_kernel(blocks, order_ref, seg_ref, slots_ref, g_ref, out_ref, gctx_ref, grad_ref):
    count = slots_ref.shape[1]
    rows = count // blocks
    half_rows = rows // 2
    for k in range(blocks):
        packed = g_ref[k].astype(F32)
        gctx_ref[k * rows : k * rows + half_rows] = upper_half(pltpu.roll(packed, HD, 1)).astype(BF16)
        gctx_ref[k * rows + half_rows : (k + 1) * rows] = upper_half(packed).astype(BF16)

    def gather(i, carry):
        start = pl.multiple_of(i * BLK, BLK)
        hot = slots_by_tokens(order_ref, start, count)
        picked = nn(hot, gctx_ref[...]).astype(BF16)
        for half in range(BLK // CL):
            at = start + half * CL
            part = slots_ref[0, pl.ds(at, CL)]
            first, second = part[:, :CL], part[:, CL:]
            grad_ctx = picked[half * CL : (half + 1) * CL]
            probs = softmax_of(first, second, seg_ref, at)
            grad_prob = nt(grad_ctx, first)
            inner = jnp.sum(probs * grad_prob, axis=1, keepdims=True)
            grad_scores = (probs * (grad_prob - inner)).astype(BF16)
            grad_query = nn(grad_scores, second) * HD ** (-0.5)
            grad_key = tn(grad_scores, first) * HD ** (-0.5)
            grad_value = tn(probs.astype(BF16), grad_ctx)
            lane = lax.broadcasted_iota(jnp.int32, (CL, CL), 1)
            grad_ref[pl.ds(at, CL), :CL] = jnp.where(lane < HD, grad_query, grad_value).astype(BF16)
            grad_ref[pl.ds(at, CL), CL:] = jnp.where(lane < HD, grad_key, 0.0).astype(BF16)
        return carry

    lax.fori_loop(0, count // BLK, gather, 0)

    def give(i, carry):
        def one(start):
            return nn(tokens_by_slots(order_ref, start, count), grad_ref[...])

        for r in range(0, half_rows, BLK):
            base = i * rows + r
            low, high = one(base), one(base + half_rows)
            out_ref[i, r : r + BLK] = low[:, :CL].astype(BF16)
            out_ref[i, half_rows + r : half_rows + r + BLK] = high[:, :CL].astype(BF16)
            packed = low[:, CL:] + pltpu.roll(high[:, CL:], HD, 1)
            out_ref[i, rows + r : rows + r + BLK] = packed.astype(BF16)
        return carry

    lax.fori_loop(0, blocks, give, 0)


def head_spec(shape, head):
    return pl.BlockSpec((1,) + shape, lambda i: (head,) + (0,) * len(shape))


def full_spec(shape):
    return pl.BlockSpec(shape, lambda i: (0,) * len(shape))


def params():
    return pltpu.CompilerParams(vmem_limit_bytes=48 * 1024 * 1024)


def slot_tokens(seqs, scalars, clusters, balance):
    heads, count = clusters.shape[0], clusters.shape[2]
    return pl.pallas_call(
        functools.partial(order_kernel, seqs),
        grid=(heads,),
        in_specs=[
            pl.BlockSpec(memory_space=pltpu.SMEM),
            pl.BlockSpec((1, 1, count), lambda h: (h, 0, 0)),
            pl.BlockSpec((1, count), lambda h: (0, 0)),
        ],
        out_specs=[pl.BlockSpec((1, 1, count), lambda h: (h, 0, 0))] * 2,
        out_shape=[jax.ShapeDtypeStruct((heads, 1, count), F32)] * 2,
        compiler_params=params(),
        name="slot_tokens",
        cost_estimate=pl.CostEstimate(flops=2 * 8 * heads * count * count, bytes_accessed=heads * count * 16, transcendentals=0),
    )(scalars, clusters, balance)


def attend(blocks, head, order, seg, x_all, weights, biases):
    count = x_all.shape[0]
    width = x_all.shape[1]
    rows = count // blocks
    return pl.pallas_call(
        functools.partial(forward_kernel, blocks),
        grid=(1,),
        in_specs=[
            head_spec((1, count), head),
            head_spec((1, count), head),
            full_spec((count, width)),
            head_spec((width, 2 * CL), head),
            head_spec((1, 2 * CL), head),
        ],
        out_specs=[full_spec((1, count, 2 * CL)), full_spec((blocks, rows // 2, CL))],
        out_shape=[
            jax.ShapeDtypeStruct((1, count, 2 * CL), BF16),
            jax.ShapeDtypeStruct((blocks, rows // 2, CL), BF16),
        ],
        scratch_shapes=[pltpu.VMEM((count, 2 * CL), BF16), pltpu.VMEM((count, CL), BF16)],
        compiler_params=params(),
        name="attend",
        cost_estimate=pl.CostEstimate(
            flops=2 * count * count * 3 * CL + 2 * count * width * 2 * CL, bytes_accessed=count * width * 2 + count * CL * 6, transcendentals=count * CL
        ),
    )(order, seg, x_all, weights, biases)


def attend_back(blocks, head, order, seg, slots, grad_context):
    count = slots.shape[1]
    rows = count // blocks
    return pl.pallas_call(
        functools.partial(backward_kernel, blocks),
        grid=(1,),
        in_specs=[
            head_spec((1, count), head),
            head_spec((1, count), head),
            full_spec((1, count, 2 * CL)),
            full_spec((blocks, rows // 2, CL)),
        ],
        out_specs=full_spec((blocks, rows + rows // 2, CL)),
        out_shape=jax.ShapeDtypeStruct((blocks, rows + rows // 2, CL), BF16),
        scratch_shapes=[pltpu.VMEM((count, CL), BF16), pltpu.VMEM((count, 2 * CL), BF16)],
        compiler_params=params(),
        name="attend_back",
        cost_estimate=pl.CostEstimate(flops=2 * count * count * 3 * CL, bytes_accessed=count * CL * 12, transcendentals=count * CL),
    )(order, seg, slots, grad_context)


def norm_stats(values_in):
    center = values_in - jnp.mean(values_in, axis=-1, keepdims=True)
    inverse = lax.rsqrt(jnp.mean(center * center, axis=-1, keepdims=True) + EPS)
    return center * inverse, inverse


def norm_back(cotangent, gain, hat, inverse):
    scaled = cotangent * gain
    return inverse * (
        scaled
        - jnp.mean(scaled, axis=-1, keepdims=True)
        - hat * jnp.mean(scaled * hat, axis=-1, keepdims=True)
    )


def exchange(parts, size, sign):
    return [parts[0]] + [
        lax.ppermute(parts[k], "tensor", [(i, (i + sign * k) % size) for i in range(size)])
        for k in range(1, size)
    ]


def gather_line(own, size, rank):
    up, down = own, own
    ups, downs = [], []
    for k in range(1, size):
        up = lax.ppermute(up, "tensor", [(i, i + 1) for i in range(k - 1, size - 1)])
        down = lax.ppermute(down, "tensor", [(i + 1, i) for i in range(0, size - k)])
        ups.append(up)
        downs.append(down)
    return [own] + [jnp.where(rank >= k, ups[k - 1], downs[size - 1 - k]) for k in range(1, size)]


def local(
    inputs, out_grad, seq_lengths, balance, clusters, query_weight, query_bias, key_weight,
    value_weight, value_bias, out_weight, out_bias, norm1_gain, norm1_bias, up_weight, up_bias,
    down_weight, down_bias, norm2_gain, norm2_bias,
):
    dp = ("chip", "core")
    everyone = ("chip", "core", "tensor")
    rows, width = inputs.shape
    size = lax.axis_size("tensor")
    rank = lax.axis_index("tensor")
    dp_size = lax.axis_size("chip") * lax.axis_size("core")
    shard = query_weight.shape[0]
    local_width = query_weight.shape[1]
    local_hidden = up_weight.shape[1]
    heads = clusters.shape[1]
    seqs = seq_lengths.shape[1]

    bounds = jnp.cumsum(seq_lengths[0])
    scalars = jnp.concatenate([jnp.stack([rank, jnp.int32(rows)]), bounds]).astype(jnp.int32)
    order, seg = slot_tokens(seqs, scalars, clusters[0][:, None, :], balance)

    own_qkv = lax.all_gather(
        jnp.concatenate([query_weight, key_weight, value_weight], axis=1), dp, axis=0, tiled=True
    )
    pieces = own_qkv.reshape(width, 3, heads, HD)
    head_weights = jnp.concatenate(
        [pieces[:, 0], pieces[:, 2], pieces[:, 1], jnp.zeros_like(pieces[:, 0])], axis=-1
    ).transpose(1, 0, 2)
    no_bias = jnp.zeros((heads, HD), F32)
    head_biases = jnp.concatenate(
        [query_bias.reshape(heads, HD), value_bias.reshape(heads, HD), no_bias, no_bias], axis=-1
    )[:, None, :]
    ff = lax.all_gather(
        jnp.concatenate([up_weight, down_weight.T, out_weight.T], axis=1), everyone, axis=0, tiled=True
    ).reshape(dp_size, size, shard, 2 * local_hidden + local_width)

    def whole(start, stop):
        return ff[:, :, :, start:stop].transpose(0, 2, 1, 3).reshape(width, size * (stop - start))

    up_full = whole(0, local_hidden)
    down_full_t = whole(local_hidden, 2 * local_hidden)
    out_full_t = whole(2 * local_hidden, 2 * local_hidden + local_width)
    up_bias_full = lax.all_gather(up_bias, "tensor", axis=0, tiled=True)

    x_parts = gather_line(inputs, size, rank)
    x_all = jnp.concatenate(x_parts, axis=0)

    slots, contexts = [], []
    for h in range(heads):
        kept, context_h = attend(size, h, order, seg, x_all, head_weights, head_biases)
        slots.append(kept)
        contexts.append(exchange([context_h[k] for k in range(size)], size, -1))
    packed = jnp.stack([jnp.stack([contexts[h][k] for h in range(heads)]) for k in range(size)])
    context = (
        packed.reshape(size, heads, rows // 2, 2, HD)
        .transpose(3, 2, 0, 1, 4)
        .reshape(rows, size, heads * HD)
    )
    doubled = jnp.concatenate([context, context], axis=1)
    context = lax.dynamic_slice_in_dim(doubled, (size - rank) % size, size, 1).reshape(rows, width)

    summed = inputs.astype(F32) + nt(context, out_full_t) + out_bias
    hat1, inverse1 = norm_stats(summed)
    normed = hat1 * norm1_gain + norm1_bias
    normed_low = normed.astype(BF16)
    up_value = nn(normed_low, up_full) + up_bias_full
    curve = 2.0**0.5 * (1.0 / jnp.pi) ** 0.5
    square = up_value * up_value
    tanh = jnp.tanh(curve * (up_value + 0.044715 * square * up_value))
    active = (0.5 * up_value * (1.0 + tanh)).astype(BF16)
    slope = 0.5 * (1.0 + tanh) + 0.5 * up_value * (1.0 - tanh * tanh) * curve * (1.0 + 3 * 0.044715 * square)
    pre_norm = normed + nt(active, down_full_t) + down_bias
    hat2, inverse2 = norm_stats(pre_norm)
    layer_out = (hat2 * norm2_gain + norm2_bias).astype(BF16)
    cot = out_grad.astype(F32)
    grad_pre = norm_back(cot, norm2_gain, hat2, inverse2)
    grad_pre_low = grad_pre.astype(BF16)
    grad_down_t = tn(grad_pre_low, active).astype(BF16)
    grad_up = (nn(grad_pre_low, down_full_t) * slope).astype(BF16)
    grad_up_w = tn(normed_low, grad_up).astype(BF16)
    grad_normed = grad_pre + nt(grad_up, up_full)
    grad_summed = norm_back(grad_normed, norm1_gain, hat1, inverse1)
    grad_summed_low = grad_summed.astype(BF16)
    grad_out_t = tn(grad_summed_low, context).astype(BF16)
    grad_context = nn(grad_summed_low, out_full_t).astype(BF16)

    grad_context = grad_context.reshape(rows, size, heads * HD)
    grad_context = lax.dynamic_slice_in_dim(
        jnp.concatenate([grad_context, grad_context], axis=1), rank, size, 1
    )
    grad_packed = (
        grad_context.reshape(2, rows // 2, size, heads, HD)
        .transpose(2, 3, 1, 0, 4)
        .reshape(size, heads, rows // 2, 2 * HD)
    )

    ffn_a = lax.psum_scatter(grad_down_t, dp, scatter_dimension=0, tiled=True)
    ffn_b = lax.psum_scatter(
        jnp.concatenate([grad_up_w, grad_out_t], axis=1), dp, scatter_dimension=0, tiled=True
    )
    ffn_a = lax.psum_scatter(ffn_a.reshape(shard, size, local_hidden).transpose(1, 0, 2), "tensor", scatter_dimension=0, tiled=False)
    ffn_b = jnp.concatenate(
        [
            ffn_b[:, : size * local_hidden].reshape(shard, size, local_hidden),
            ffn_b[:, size * local_hidden :].reshape(shard, size, local_width),
        ],
        axis=2,
    ).transpose(1, 0, 2)
    ffn_b = lax.psum_scatter(ffn_b, "tensor", scatter_dimension=0, tiled=False)
    grad_down_weight = ffn_a.astype(F32).T
    grad_up_weight = ffn_b[:, :local_hidden].astype(F32)
    grad_out_weight = ffn_b[:, local_hidden:].astype(F32).T

    qkv_all = lax.all_gather(
        jnp.concatenate([query_weight, key_weight, value_weight], axis=1), everyone, axis=0, tiled=True
    ).reshape(dp_size, size, shard, 3, heads, HD)
    qkv_all = jnp.concatenate([qkv_all, qkv_all], axis=1)
    qkv_all = lax.dynamic_slice_in_dim(qkv_all, rank, size, 1)

    total = grad_summed
    weight_grads, bias_grads = [], []
    for h in range(heads):
        arrived = exchange([grad_packed[k, h] for k in range(size)], size, 1)
        grads = attend_back(size, h, order, seg, slots[h], jnp.stack(arrived))
        grad_qv = grads[:, :rows].reshape(size * rows, CL)
        grad_k = grads[:, rows:].reshape(size, rows // 2, 2, HD).transpose(0, 2, 1, 3).reshape(size * rows, HD)
        tokens_h = jnp.concatenate([grad_qv, grad_k], axis=1)
        weight_grads.append(tn(x_all, tokens_h).astype(BF16))
        bias_grads.append(jnp.sum(grad_qv.astype(F32), axis=0))
        back = exchange([grads[k] for k in range(size)], size, -1)
        own_qv = jnp.stack([b[:rows] for b in back])
        own_k = jnp.stack([b[rows:] for b in back]).reshape(size, rows // 2, 2, HD).transpose(0, 2, 1, 3).reshape(size, rows, HD)
        full = jnp.concatenate([own_qv, own_k], axis=2).transpose(1, 0, 2).reshape(rows, size * 3 * HD)
        mat = jnp.concatenate([qkv_all[:, :, :, 0, h], qkv_all[:, :, :, 2, h], qkv_all[:, :, :, 1, h]], axis=-1)
        mat = mat.transpose(0, 2, 1, 3).reshape(width, size * 3 * HD)
        total = total + nt(full, mat)
    grad_inputs = total
    wg = lax.psum_scatter(jnp.concatenate(weight_grads, axis=1), dp, scatter_dimension=0, tiled=True)
    wg = wg.astype(F32).reshape(shard, heads, 3, HD)
    grad_query_weight = wg[:, :, 0].reshape(shard, local_width)
    grad_value_weight = wg[:, :, 1].reshape(shard, local_width)
    grad_key_weight = wg[:, :, 2].reshape(shard, local_width)

    bias = jnp.stack(bias_grads)
    bias = lax.psum(bias, dp)
    grad_query_bias = bias[:, :HD].reshape(local_width)
    grad_value_bias = bias[:, HD:].reshape(local_width)

    small = lax.psum(
        jnp.concatenate(
            [
                jnp.sum(grad_summed, axis=0),
                jnp.sum(grad_normed * hat1, axis=0),
                jnp.sum(grad_normed, axis=0),
                jnp.sum(grad_pre, axis=0),
                jnp.sum(cot * hat2, axis=0),
                jnp.sum(cot, axis=0),
                jnp.sum(grad_up.astype(F32), axis=0),
            ]
        ),
        everyone,
    )
    vec = [small[i * width : (i + 1) * width] for i in range(6)]
    grad_up_bias = lax.dynamic_slice_in_dim(small, 6 * width + rank * local_hidden, local_hidden, 0)
    return (
        layer_out, grad_inputs, grad_query_weight, grad_query_bias, grad_key_weight, grad_value_weight,
        grad_value_bias, grad_out_weight, vec[0], vec[1], vec[2], grad_up_weight, grad_up_bias,
        grad_down_weight, vec[3], vec[4], vec[5],
    )


def solution(mesh):
    devices = mesh.devices
    split = Mesh(devices.reshape(devices.shape[0] // 2, 2, devices.shape[1]), ("chip", "core", "tensor"))
    dp = ("chip", "core")
    rows, weight, turned, vector, same = (
        P(dp + ("tensor",), None),
        P(dp, "tensor"),
        P("tensor", dp),
        P("tensor"),
        P(),
    )
    in_specs = (
        rows, rows, P(dp, None), P(dp, None), P(dp, "tensor", None), weight, vector, weight, weight,
        vector, turned, same, same, same, weight, vector, turned, same, same, same,
    )
    out_specs = (
        rows, rows, weight, vector, weight, weight, vector, turned, same, same, same, weight, vector,
        turned, same, same, same,
    )
    return jax.shard_map(local, mesh=split, in_specs=in_specs, out_specs=out_specs, check_vma=False)
```

```python
import functools

import jax
import jax.numpy as jnp
from jax import lax
from jax.experimental import pallas as pl
from jax.experimental.pallas import tpu as pltpu
from jax.sharding import Mesh, PartitionSpec as P

HD = 64
CL = 128
PAIR = 2 * HD
WIDE = 4 * HD
F32 = jnp.float32
BF16 = jnp.bfloat16
EPS = 1e-06
PEAK_PER_MICRO = 1.15e9


def nn(left, right):
    return jnp.dot(left, right, preferred_element_type=F32)


def nt(left, right):
    return lax.dot_general(left, right, (((1,), (1,)), ((), ())), preferred_element_type=F32)


def tn(left, right):
    return lax.dot_general(left, right, (((0,), (0,)), ((), ())), preferred_element_type=F32)


def one_hot(hits):
    return jnp.where(hits, 1.0, 0.0).astype(BF16)


def head_lane(shape, dim, part):
    lane = lax.broadcasted_iota(jnp.int32, shape, dim)
    column = (lane // WIDE) * HD + lane % HD
    return jnp.where((lane % WIDE) // HD == part, column, -1)


def prepare_kernel(q_ref, k_ref, v_ref, o_ref, up_ref, dn_ref, heads_ref, ff_ref):
    shape = (q_ref.shape[1], heads_ref.shape[1])
    column = lax.broadcasted_iota(jnp.int32, shape, 0)
    total = jnp.zeros(heads_ref.shape, F32)
    for part, ref in ((0, q_ref), (1, v_ref), (2, k_ref)):
        total = total + nn(ref[...], one_hot(head_lane(shape, 1, part) == column))
    heads_ref[...] = total.astype(BF16)
    hidden = up_ref.shape[1]
    ff_ref[:, :hidden] = up_ref[...]
    ff_ref[:, hidden : 2 * hidden] = dn_ref[...]
    shape = (ff_ref.shape[1] - 2 * hidden, o_ref.shape[0])
    spread = one_hot(lax.broadcasted_iota(jnp.int32, shape, 0) == lax.broadcasted_iota(jnp.int32, shape, 1))
    padded = nn(spread, o_ref[...]).astype(BF16)
    rows = o_ref.shape[1]
    same = lax.broadcasted_iota(jnp.int32, (rows, rows), 0) == lax.broadcasted_iota(jnp.int32, (rows, rows), 1)
    ff_ref[:, 2 * hidden :] = nt(one_hot(same), padded).astype(BF16)


def unmix_kernel(grads_ref, q_ref, k_ref, v_ref):
    shape = (q_ref.shape[1], grads_ref.shape[1])
    column = lax.broadcasted_iota(jnp.int32, shape, 0)
    for part, ref in ((0, q_ref), (1, v_ref), (2, k_ref)):
        ref[...] = nt(grads_ref[...], one_hot(head_lane(shape, 1, part) == column))


def order_kernel(seqs, scal_ref, clusters_ref, balance_ref, order_ref, seg_ref):
    count = balance_ref.shape[1]
    step = 2 * CL
    rows = scal_ref[2]
    balance = balance_ref[...]
    high = balance // HD
    low = balance - high * HD
    pick = lax.broadcasted_iota(jnp.int32, (8, count), 0)
    table = jnp.where(pick == 0, high, jnp.where(pick == 1, low, 0)).astype(F32).astype(BF16)
    chosen = clusters_ref[0]
    total = jnp.zeros((8, count), F32)
    for start in range(0, count, step):
        place = lax.broadcasted_iota(jnp.int32, (step, count), 0) + start
        total = total + nn(table[:, start : start + step], one_hot(place == chosen))
    token = (total[0:1] * float(HD) + total[1:2]).astype(jnp.int32)
    segment = jnp.zeros_like(token)
    for s in range(seqs):
        segment = segment + jnp.where(token >= scal_ref[3 + s], 1, 0)
    seg_ref[0] = segment.astype(F32)
    from_own = scal_ref[0] * rows - (token // rows) * rows
    from_own = jnp.where(from_own < 0, from_own + count, from_own)
    order_ref[0] = (from_own + token % rows).astype(F32)


def column_of(row):
    return jnp.transpose(jnp.broadcast_to(row, (CL, CL)))


def slots_by_tokens(order_ref, start, span, count):
    lane = lax.broadcasted_iota(jnp.int32, (CL, CL), 1).astype(F32)
    parts = []
    for at in range(0, span, CL):
        gap = column_of(order_ref[0, :, pl.ds(start + at, CL)]) - lane
        parts.append(jnp.concatenate([one_hot(gap == float(j)) for j in range(0, count, CL)], axis=1))
    return jnp.concatenate(parts, axis=0)


def tokens_by_slots(order_ref, start, span, count):
    row = order_ref[0] - jnp.asarray(start, F32)
    return one_hot(lax.broadcasted_iota(jnp.int32, (span, count), 0).astype(F32) == row)


def softmax_of(first, second, seg_ref, start):
    scores = nt(first, second) * HD ** (-0.5)
    seg_row = seg_ref[0, :, pl.ds(start, CL)]
    scores = jnp.where(column_of(seg_row) == seg_row, scores, -1e30)
    raised = jnp.exp(scores - jnp.max(scores, axis=1, keepdims=True))
    return raised / jnp.sum(raised, axis=1, keepdims=True)


def upper_half(values):
    lane = lax.broadcasted_iota(jnp.int32, values.shape, 1)
    return jnp.where(lane >= HD, values, 0.0)


def project_kernel(size, heads, scal_ref, own_ref, w_ref, b_ref, *refs):
    ups, downs = refs[: size - 1], refs[size - 1 : 2 * size - 2]
    x_out, qkv_out, x_ref, qkv_ref, in_sem, x_sem, qkv_sem = refs[2 * size - 2 :]
    rows = own_ref.shape[0]
    rank = scal_ref[0]

    def place(k):
        return pl.ds(k * rows, rows)

    def landing(k, source):
        return pltpu.make_async_copy(source, x_ref.at[place(k)], in_sem.at[k])

    landing(0, own_ref).start()
    for k in range(1, size):

        @pl.when(rank >= k)
        def _(k=k):
            landing(k, ups[k - 1]).start()

        @pl.when(rank < k)
        def _(k=k):
            landing(k, downs[size - 1 - k]).start()

    leaving = []
    for k in range(size):
        landing(k, own_ref).wait()
        leaving.append(pltpu.make_async_copy(x_ref.at[place(k)], x_out.at[place(k)], x_sem.at[k]))
        leaving[-1].start()
        for h in range(heads):
            lanes = slice(h * WIDE, (h + 1) * WIDE)
            qkv_ref[h, place(k)] = (nn(x_ref[place(k)], w_ref[:, lanes]) + b_ref[:, lanes]).astype(BF16)
            leaving.append(
                pltpu.make_async_copy(qkv_ref.at[h, place(k)], qkv_out.at[h, place(k)], qkv_sem.at[h, k])
            )
            leaving[-1].start()
    for copy in leaving:
        copy.wait()


def forward_kernel(size, heads, span, scal_ref, order_ref, seg_ref, qkv_ref, extra_ref, slots_ref, out_ref, ctx_ref):
    head = pl.program_id(0)
    count = qkv_ref.shape[1]
    rows = count // size
    half = rows // 2
    for k in range(size):
        out_ref[k, pl.ds(heads * half, extra_ref.shape[0])] = extra_ref[...]

    def gather(i, carry):
        start = pl.multiple_of(i * span, span)
        picked = nn(slots_by_tokens(order_ref, start, span, count), qkv_ref[0]).astype(BF16)
        slots_ref[0, pl.ds(start, span)] = picked
        for at in range(0, span, CL):
            first, second = picked[at : at + CL, :PAIR], picked[at : at + CL, PAIR:]
            probs = softmax_of(first, second, seg_ref, start + at)
            ctx_ref[pl.ds(start + at, CL)] = upper_half(nn(probs.astype(BF16), first)).astype(BF16)
        return carry

    lax.fori_loop(0, count // span, gather, 0)
    at = pl.ds(pl.multiple_of(head * half, half), half)
    for k in range(size):
        given = nn(tokens_by_slots(order_ref, k * rows, rows, count), ctx_ref[...])
        to = lax.rem(scal_ref[0] - k + size, size)
        out_ref[to, at] = (pltpu.roll(given[:half], HD, 1) + given[half:]).astype(BF16)


def backward_kernel(size, span, order_ref, seg_ref, slots_ref, turned_ref, *refs):
    g_refs, outs = refs[:size], refs[size : 2 * size]
    mine_ref, other_ref, bias_ref, gctx_ref, grad_ref, tok_ref = refs[2 * size :]
    count = slots_ref.shape[1]
    rows = count // size
    half = rows // 2
    for k in range(size):
        packed = g_refs[k][...].astype(F32)
        gctx_ref[k * rows : k * rows + half] = upper_half(pltpu.roll(packed, HD, 1)).astype(BF16)
        gctx_ref[k * rows + half : (k + 1) * rows] = upper_half(packed).astype(BF16)

    def gather(i, sums):
        start = pl.multiple_of(i * span, span)
        picked = nn(slots_by_tokens(order_ref, start, span, count), gctx_ref[...]).astype(BF16)
        lane = lax.broadcasted_iota(jnp.int32, (CL, PAIR), 1)
        for offset in range(0, span, CL):
            at = pl.ds(start + offset, CL)
            part = slots_ref[0, at]
            first, second = part[:, :PAIR], part[:, PAIR:]
            grad_ctx = picked[offset : offset + CL]
            probs = softmax_of(first, second, seg_ref, start + offset)
            grad_prob = nt(grad_ctx, first)
            inner = jnp.sum(probs * grad_prob, axis=1, keepdims=True)
            grad_scores = (probs * (grad_prob - inner)).astype(BF16)
            grad_query = nn(grad_scores, second) * HD ** (-0.5)
            grad_key = tn(grad_scores, first) * HD ** (-0.5)
            grad_value = tn(probs.astype(BF16), grad_ctx)
            grad_qv = jnp.where(lane < HD, grad_query, grad_value).astype(BF16)
            sums = sums + jnp.sum(grad_qv.astype(F32), axis=0, keepdims=True)
            grad_ref[at, :PAIR] = grad_qv
            grad_ref[at, PAIR:] = jnp.where(lane < HD, grad_key, 0.0).astype(BF16)
        return sums

    bias_ref[...] = lax.fori_loop(0, count // span, gather, jnp.zeros((1, PAIR), F32))
    for k in range(size):
        given = nn(tokens_by_slots(order_ref, k * rows, rows, count), grad_ref[...])
        low = given.astype(BF16)
        tok_ref[k * rows : (k + 1) * rows] = low
        outs[k][:rows] = low[:, :PAIR]
        outs[k][rows:] = (given[:half, PAIR:] + pltpu.roll(given[half:, PAIR:], HD, 1)).astype(BF16)
    cut = turned_ref.shape[0] // 2
    mine_ref[...] = nn(turned_ref[:cut], tok_ref[...]).astype(BF16)
    other_ref[...] = nn(turned_ref[cut:], tok_ref[...]).astype(BF16)


def row_stats(values_in):
    center = values_in - jnp.mean(values_in, axis=-1, keepdims=True)
    inverse = lax.rsqrt(jnp.mean(center * center, axis=-1, keepdims=True) + EPS)
    return center * inverse, inverse


def norm_back(cotangent, gain, hat, inverse):
    scaled = cotangent * gain
    return inverse * (
        scaled
        - jnp.mean(scaled, axis=-1, keepdims=True)
        - hat * jnp.mean(scaled * hat, axis=-1, keepdims=True)
    )


def column_sum(values_in):
    return jnp.sum(values_in, axis=0, keepdims=True)


def row_copies(ref, layout, start, lanes, held, sem):
    size, groups, shard = layout
    if groups == 1:
        shard = held.shape[0]
    return [
        pltpu.make_async_copy(
            ref.at[pl.ds((group * size + k) * shard, shard), pl.ds(start, lanes)],
            held.at[pl.ds(group * shard, shard), pl.ds(k * lanes, lanes)],
            sem,
        )
        for group in range(groups)
        for k in range(size)
    ]


def all_of(held, sem):
    return pltpu.make_async_copy(held, held, sem)


def layer_kernel(heads, layout, scal_ref, x_ref, og_ref, vec_ref, recv_ref, *refs):
    size = layout[0]
    ff_ref, refs = refs[0], refs[1:]
    layer_ref, sum_ref, act_out, gup_out, nlow_ref, plow_ref, slow_ref, ctx_ref, small_ref = refs[:9]
    gctx_refs = refs[9 : 9 + size]
    wup_ref, wdn_ref, wo_ref, act_ref, gup_ref, slope_ref, total_ref = refs[9 + size : 16 + size]
    sem, out_sem = refs[16 + size :]
    rows, width = x_ref.shape
    hidden = wup_ref.shape[1] // size
    head_lanes = wo_ref.shape[1] // size
    rank = scal_ref[0]

    for kind, (start, lanes, held) in enumerate(
        ((2 * hidden, head_lanes, wo_ref), (0, hidden, wup_ref), (hidden, hidden, wdn_ref))
    ):
        for copy in row_copies(ff_ref, layout, start, lanes, held, sem.at[kind]):
            copy.start()

    half = rows // 2
    lower = lax.broadcasted_iota(jnp.int32, (half, PAIR), 1) < HD
    source = [lax.rem(rank - k + size, size) for k in range(size)]
    for k in range(size):
        for h in range(0, heads, 2):
            first = recv_ref[source[k], h * half : (h + 1) * half].astype(F32)
            second = jnp.zeros((half, PAIR), F32)
            if h + 1 < heads:
                second = recv_ref[source[k], (h + 1) * half : (h + 2) * half].astype(F32)
            lanes = slice(k * head_lanes + h * HD, k * head_lanes + h * HD + PAIR)
            ctx_ref[:half, lanes] = jnp.where(lower, first, pltpu.roll(second, HD, 1)).astype(BF16)
            ctx_ref[half:, lanes] = jnp.where(lower, pltpu.roll(first, HD, 1), second).astype(BF16)
    all_of(wo_ref, sem.at[0]).wait()
    summed = x_ref[...].astype(F32) + nt(ctx_ref[...], wo_ref[...]) + vec_ref[0:1]
    hat1, inverse1 = row_stats(summed)
    normed = hat1 * vec_ref[1:2] + vec_ref[2:3]
    nlow_ref[...] = normed.astype(BF16)
    all_of(wup_ref, sem.at[1]).wait()

    total_ref[...] = normed + vec_ref[3:4]
    curve = (2.0 / 3.141592653589793) ** 0.5
    cut = hidden // PAIR
    all_of(wdn_ref, sem.at[2]).wait()

    def leave(kept, out, kind, lanes):
        return pltpu.make_async_copy(kept.at[:, lanes], out.at[:, lanes], out_sem.at[kind])

    def span(k):
        return pl.ds(pl.multiple_of(k * hidden, hidden), hidden)

    def forward(k, carry):
        lanes = span(k)
        parts = recv_ref[lax.rem(rank - k + size, size), heads * half :].astype(F32)
        bias = parts[:cut] + parts[cut : 2 * cut] + parts[2 * cut : 3 * cut]
        bias = jnp.concatenate([bias[i : i + 1] for i in range(cut)], axis=1)
        up = nn(nlow_ref[...], wup_ref[:, lanes]) + bias
        square = up * up
        tanh = jnp.tanh(up * (curve + (0.044715 * curve) * square))
        gate = 0.5 + 0.5 * tanh
        act_ref[:, lanes] = (up * gate).astype(BF16)
        slope_ref[:, lanes] = gate + (0.5 * up) * (1.0 - tanh * tanh) * (curve + (3 * 0.044715 * curve) * square)
        leave(act_ref, act_out, 0, lanes).start()
        total_ref[...] += nt(act_ref[:, lanes], wdn_ref[:, lanes])
        return carry

    lax.fori_loop(0, size, forward, 0)
    hat2, inverse2 = row_stats(total_ref[...])
    gain2 = vec_ref[4:5]
    layer_ref[...] = (hat2 * gain2 + vec_ref[5:6]).astype(BF16)
    cot = og_ref[...].astype(F32)
    grad_pre = norm_back(cot, gain2, hat2, inverse2)
    plow_ref[...] = grad_pre.astype(BF16)
    small_ref[3:4] = column_sum(grad_pre)
    small_ref[4:5] = column_sum(cot * hat2)
    small_ref[5:6] = column_sum(cot)
    small_ref[6:8] = jnp.zeros((2, width), F32)
    total_ref[...] = grad_pre

    def backward(k, carry):
        lanes = span(k)
        grad_up = (nn(plow_ref[...], wdn_ref[:, lanes]) * slope_ref[:, lanes]).astype(BF16)
        gup_ref[:, lanes] = grad_up
        leave(gup_ref, gup_out, 1, lanes).start()
        small_ref[pl.ds(8 + lax.rem(rank - k + size, size), 1)] = column_sum(grad_up.astype(F32))
        total_ref[...] += nt(gup_ref[:, lanes], wup_ref[:, lanes])
        return carry

    lax.fori_loop(0, size, backward, 0)
    grad_normed = total_ref[...]
    small_ref[1:2] = column_sum(grad_normed * hat1)
    small_ref[2:3] = column_sum(grad_normed)
    grad_summed = norm_back(grad_normed, vec_ref[1:2], hat1, inverse1)
    small_ref[0:1] = column_sum(grad_summed)
    sum_ref[...] = grad_summed
    slow_ref[...] = grad_summed.astype(BF16)
    grad_ctx = nn(slow_ref[...], wo_ref[...])
    for k in range(size):
        for h in range(0, heads, 2):
            lanes = slice(k * head_lanes + h * HD, k * head_lanes + h * HD + PAIR)
            top, bottom = grad_ctx[:half, lanes], grad_ctx[half:, lanes]
            gctx_refs[k][h * half : (h + 1) * half] = jnp.where(lower, top, pltpu.roll(bottom, HD, 1)).astype(BF16)
            if h + 1 < heads:
                gctx_refs[k][(h + 1) * half : (h + 2) * half] = jnp.where(
                    lower, pltpu.roll(top, HD, 1), bottom
                ).astype(BF16)
    pltpu.make_async_copy(act_ref, act_out, out_sem.at[0]).wait()
    pltpu.make_async_copy(gup_ref, gup_out, out_sem.at[1]).wait()


def turned_kernel(pairs, *refs):
    lefts, rights = refs[:pairs], refs[pairs : 2 * pairs]
    out_ref, turned_ref = refs[2 * pairs :]
    width = out_ref.shape[0]

    @pl.when(pl.program_id(0) == 0)
    def _():
        row = lax.broadcasted_iota(jnp.int32, (width, width), 0)
        same = one_hot(row == lax.broadcasted_iota(jnp.int32, (width, width), 1))
        for i in range(pairs):
            turned_ref[i] = nt(same, lefts[i][...]).astype(BF16)

    at = 0
    for i in range(pairs):
        lanes = slice(at, at + rights[i].shape[1])
        at = lanes.stop
        out_ref[:, lanes] = nn(turned_ref[i], rights[i][...]).astype(BF16)


def flip_kernel(pick_ref, left_ref, turned_ref):
    turned_ref[...] = nt(pick_ref[...], left_ref[...]).astype(BF16)


def finish_kernel(head, layout, acc_ref, w_ref, *refs):
    size = layout[0]
    out_ref, held_ref, grads_ref, sem = refs[-4:]
    g_refs = refs[:size]
    rows = acc_ref.shape[0]
    half = rows // 2
    for copy in row_copies(w_ref, layout, head * WIDE, WIDE, held_ref, sem):
        copy.start()
    lower = lax.broadcasted_iota(jnp.int32, (half, PAIR), 1) < HD
    for k in range(size):
        at = k * WIDE
        grads_ref[:, at : at + PAIR] = g_refs[k][:rows]
        packed = g_refs[k][rows:].astype(F32)
        grads_ref[:half, at + PAIR : at + WIDE] = jnp.where(lower, packed, 0.0).astype(BF16)
        grads_ref[half:, at + PAIR : at + WIDE] = jnp.where(lower, pltpu.roll(packed, HD, 1), 0.0).astype(BF16)
    all_of(held_ref, sem).wait()
    out_ref[...] = acc_ref[...] + nt(grads_ref[...], held_ref[...])


def cost(micros, exps=0):
    return pl.CostEstimate(flops=int(micros * PEAK_PER_MICRO), bytes_accessed=0, transcendentals=int(exps))


def head_spec(shape, head):
    return pl.BlockSpec((1,) + shape, lambda i: (head,) + (0,) * len(shape))


def full(shape):
    return pl.BlockSpec(tuple(shape), lambda i: (0,) * len(shape))


def held():
    return pl.BlockSpec(memory_space=pl.ANY)


def scalars_spec():
    return pl.BlockSpec(memory_space=pltpu.SMEM)


def shape_of(shape, dtype=BF16):
    return jax.ShapeDtypeStruct(tuple(shape), dtype)


def call(kernel, name, in_specs, out_specs, out_shape, scratch, estimate, mib, grid=(1,), after=()):
    count = len(in_specs)

    def body(*refs):
        kernel(*refs[:count], *refs[count + len(after) :])

    run = pl.pallas_call(
        body,
        grid=grid,
        in_specs=list(in_specs) + [held()] * len(after),
        out_specs=out_specs,
        out_shape=out_shape,
        scratch_shapes=scratch,
        compiler_params=pltpu.CompilerParams(vmem_limit_bytes=mib * 1024 * 1024),
        name=name,
        cost_estimate=estimate,
    )
    return lambda *args: run(*args, *after)


def prepare(query, key, value, out, up, down_t, heads):
    shard, hidden = up.shape
    lanes = 2 * hidden + -(-out.shape[0] // CL) * CL
    args = (query, key, value, out, up, down_t)
    shapes = [shape_of((shard, heads * WIDE)), shape_of((shard, lanes))]
    return call(
        prepare_kernel, "prepare", [full(a.shape) for a in args], [full(s.shape) for s in shapes], shapes, [],
        cost(1), 16,
    )(*args)


def unmix(grads, local_width):
    shard = grads.shape[0]
    shapes = [shape_of((shard, local_width), F32)] * 3
    return call(
        unmix_kernel, "unmix", [full(grads.shape)], [full(s.shape) for s in shapes], shapes, [],
        cost(1), 16,
    )(grads)


def slot_tokens(seqs, scalars, clusters, balance):
    heads, count = clusters.shape[0], clusters.shape[2]
    row = pl.BlockSpec((1, 1, count), lambda h: (h, 0, 0))
    return call(
        functools.partial(order_kernel, seqs), "slot_tokens",
        [scalars_spec(), row, full(balance.shape)], [row] * 2, [shape_of((heads, 1, count), F32)] * 2, [],
        cost(8), 16, grid=(heads,),
    )(scalars, clusters, balance)


def project(size, heads, scalars, own, weights, biases, ups, downs, after):
    rows, width = own.shape
    lanes = heads * WIDE
    shapes = [shape_of((size * rows, width)), shape_of((heads, size * rows, WIDE))]
    return call(
        functools.partial(project_kernel, size, heads), "project",
        [scalars_spec(), held(), full(weights.shape), full(biases.shape)] + [held()] * (2 * size - 2),
        [held()] * 2, shapes,
        [pltpu.VMEM(s.shape, BF16) for s in shapes]
        + [pltpu.SemaphoreType.DMA((size,)), pltpu.SemaphoreType.DMA((size,)), pltpu.SemaphoreType.DMA((heads, size))],
        cost(6), 24, after=after,
    )(scalars, own, weights, biases, *ups, *downs)


def attend(size, scalars, order, seg, qkv, extra):
    heads, count = qkv.shape[:2]
    half = count // size // 2
    row = pl.BlockSpec((1, 1, count), lambda h: (h, 0, 0))
    block = pl.BlockSpec((1, count, WIDE), lambda h: (h, 0, 0))
    shapes = [shape_of((heads, count, WIDE)), shape_of((size, heads * half + extra.shape[0], PAIR))]
    return call(
        functools.partial(forward_kernel, size, heads, count // 2), "attend",
        [scalars_spec(), row, row, block, full(extra.shape)],
        [block, full(shapes[1].shape)], shapes,
        [pltpu.VMEM((count, PAIR), BF16)],
        cost(30), 32, grid=(heads,),
    )(scalars, order, seg, qkv, extra)


def attend_back(size, head, order, seg, slots, turned_x, grad_context, after):
    count = slots.shape[1]
    rows = count // size
    cut = turned_x.shape[0] // 2
    shapes = (
        [shape_of((rows + rows // 2, PAIR))] * size + [shape_of((cut, WIDE))] * 2 + [shape_of((1, PAIR), F32)]
    )
    return call(
        functools.partial(backward_kernel, size, count // 2), "attend_back",
        [head_spec((1, count), head), head_spec((1, count), head), head_spec((count, WIDE), head), full(turned_x.shape)]
        + [pl.BlockSpec((rows // 2, PAIR), lambda i: (head, 0))] * size,
        [full(s.shape) for s in shapes], shapes,
        [pltpu.VMEM((count, PAIR), BF16), pltpu.VMEM((count, WIDE), BF16), pltpu.VMEM((count, WIDE), BF16)],
        cost(3), 40, after=after,
    )(order, seg, slots, turned_x, *grad_context)


def layer(heads, layout, hidden, scalars, inputs, out_grad, vectors, received, ff, after):
    size = layout[0]
    rows, width = inputs.shape
    head_lanes = ff.shape[1] - 2 * hidden
    shapes = [
        shape_of((rows, width)),
        shape_of((rows, width), F32),
        shape_of((rows, size * hidden)),
        shape_of((rows, size * hidden)),
        shape_of((rows, width)),
        shape_of((rows, width)),
        shape_of((rows, width)),
        shape_of((rows, size * head_lanes)),
        shape_of((8 + size, width), F32),
    ] + [shape_of((heads * (rows // 2), PAIR))] * size
    args = (inputs, out_grad, vectors, received)
    return call(
        functools.partial(layer_kernel, heads, layout), "layer",
        [scalars_spec()] + [full(a.shape) for a in args] + [held()],
        [full(s.shape) if i not in (2, 3) else held() for i, s in enumerate(shapes)], shapes,
        [
            pltpu.VMEM((width, size * hidden), BF16),
            pltpu.VMEM((width, size * hidden), BF16),
            pltpu.VMEM((width, size * head_lanes), BF16),
            pltpu.VMEM((rows, size * hidden), BF16),
            pltpu.VMEM((rows, size * hidden), BF16),
            pltpu.VMEM((rows, size * hidden), F32),
            pltpu.VMEM((rows, width), F32),
            pltpu.SemaphoreType.DMA((3,)),
            pltpu.SemaphoreType.DMA((2,)),
        ],
        cost(24), 56, after=after,
    )(scalars, *args, ff)


def turned(size, lefts, rights):
    rows, width = lefts[0].shape
    columns = sum(right.shape[1] for right in rights)
    return call(
        functools.partial(turned_kernel, len(lefts)), "turned",
        [full(left.shape) for left in lefts]
        + [pl.BlockSpec((rows, right.shape[1] // size), lambda i: (0, i)) for right in rights],
        pl.BlockSpec((width, columns // size), lambda i: (0, i)), shape_of((width, columns)),
        [pltpu.VMEM((len(lefts), width, rows), BF16)],
        cost(1), 32, grid=(size,),
    )(*lefts, *rights)


def flip(size, pick, left):
    count, width = left.shape
    rows = count // size
    return call(
        flip_kernel, "flip",
        [full(pick.shape), pl.BlockSpec((rows, width), lambda i: (i, 0))],
        pl.BlockSpec((width, rows), lambda i: (0, i)), shape_of((width, count)), [],
        cost(1), 16, grid=(size,),
    )(pick, left)


def finish(head, layout, total, weights, grads, after):
    size = layout[0]
    rows, width = total.shape
    return call(
        functools.partial(finish_kernel, head, layout), "finish",
        [full(total.shape), held()] + [full(g.shape) for g in grads],
        full(total.shape), shape_of(total.shape, F32),
        [
            pltpu.VMEM((width, size * WIDE), BF16),
            pltpu.VMEM((rows, size * WIDE), BF16),
            pltpu.SemaphoreType.DMA(()),
        ],
        cost(1), 24, after=after,
    )(total, weights, *grads)


def shift(values, size, k):
    return lax.ppermute(values, "tensor", [(i, (i + k) % size) for i in range(size)])


def exchange(parts, size):
    return [parts[0]] + [shift(parts[size - k], size, k) for k in range(1, size)]


def gather_line(own, size):
    up, down = own, own
    ups, downs = [], []
    for k in range(1, size):
        up = lax.ppermute(up, "tensor", [(i, i + 1) for i in range(k - 1, size - 1)])
        down = lax.ppermute(down, "tensor", [(i + 1, i) for i in range(0, size - k)])
        ups.append(up)
        downs.append(down)
    return ups, downs


def swap(values, axis, bit):
    return lax.ppermute(values, axis, [(i, i ^ bit) for i in range(lax.axis_size(axis))])


def bits_of(size):
    return [1 << b for b in range(size.bit_length() - 1)]


def add_low(left, right):
    return (left.astype(F32) + right.astype(F32)).astype(BF16)


def halves(mine, arrived):
    cut = mine.shape[0] // 2
    return add_low(mine[:cut], arrived[:cut]), add_low(mine[cut:], arrived[cut:])


def total_of(parts):
    result = parts[0].astype(F32)
    for part in parts[1:]:
        result = result + part.astype(F32)
    return result


def tie(*groups):
    return lax.optimization_barrier(groups)


def local(
    inputs, out_grad, seq_lengths, balance, clusters, query_weight, query_bias, key_weight,
    value_weight, value_bias, out_weight, out_bias, norm1_gain, norm1_bias, up_weight, up_bias,
    down_weight, down_bias, norm2_gain, norm2_bias,
):
    dp = ("chip", "core")
    rows, width = inputs.shape
    size = lax.axis_size("tensor")
    chips = lax.axis_size("chip")
    rank, chip, core = (lax.axis_index(axis) for axis in ("tensor", "chip", "core"))
    shard = query_weight.shape[0]
    local_width = query_weight.shape[1]
    heads = clusters.shape[1]
    seqs = seq_lengths.shape[1]
    bits = bits_of(chips)

    bounds = jnp.cumsum(seq_lengths[0])
    scalars = jnp.concatenate([jnp.stack([rank, core, jnp.int32(rows)]), bounds]).astype(jnp.int32)
    direct = shard % 16 == 0
    layout = (size, 2 * chips if direct else 1, shard)
    hidden = up_weight.shape[1]

    def near_of(own):
        ups, downs = gather_line(own, size)
        return jnp.concatenate(
            [own] + [jnp.where(rank >= k, ups[k - 1], downs[size - 1 - k]) for k in range(1, size)], axis=0
        )

    def whole(near):
        rows_in = lax.all_gather(near, dp, axis=0, tiled=True)
        if direct:
            return rows_in
        lanes = near.shape[1]
        return rows_in.reshape(2 * chips, size, shard, lanes).transpose(1, 0, 2, 3).reshape(size * width, lanes)

    head_weights, ff_own = prepare(
        query_weight, key_weight, value_weight, out_weight, up_weight, down_weight.T, heads
    )
    ups, downs = gather_line(inputs, size)
    own_qkv = lax.all_gather(head_weights, dp, axis=0, tiled=True)
    near, own_qkv, ups[0], downs[0] = tie(near_of(ff_own), own_qkv, ups[0], downs[0])
    ff = whole(near)
    blank = jnp.zeros((heads, HD), F32)
    head_biases = jnp.concatenate(
        [query_bias.reshape(heads, HD), value_bias.reshape(heads, HD), blank, blank], axis=-1
    ).reshape(1, heads * WIDE)
    terms, rest = [], up_bias
    for _ in range(3):
        term = lax.reduce_precision(rest, 8, 7)
        terms.append(term.astype(BF16))
        rest = rest - term
    extra = jnp.concatenate(terms).reshape(-1, PAIR)
    extra = jnp.pad(extra, ((0, -extra.shape[0] % 16), (0, 0)))
    vectors = jnp.stack([out_bias, norm1_gain, norm1_bias, down_bias, norm2_gain, norm2_bias])

    def row_pick(order_bits):
        place = jnp.arange(width, dtype=jnp.int32)
        block = place // shard
        away = jnp.zeros_like(block)
        for depth, bit in enumerate(order_bits):
            away = away + ((block >> (len(order_bits) - 1 - depth)) & 1) * bit
        near = chip ^ away
        owner = near * 2 + (core ^ (block // chips))
        return one_hot((owner * shard + place % shard)[:, None] == place[None, :])

    pick = row_pick(bits)
    order, seg = slot_tokens(seqs, scalars, clusters[0][:, None, :], balance)
    x_all, qkv = project(size, heads, scalars, inputs, own_qkv, head_biases, ups, downs, [order])
    later_weights, qkv = tie(head_weights, qkv)
    later = whole(jnp.concatenate([later_weights] + [shift(later_weights, size, k) for k in range(1, size)], axis=0))

    slots, sent = attend(size, scalars, order, seg, qkv, extra)
    received = lax.all_to_all(sent, "tensor", 0, 0, tiled=True)
    turned_x = flip(size, pick, x_all)
    (layer_out, grad_summed, active, grad_up, normed_low, pre_low, summed_low, context, small, *grad_ctx) = layer(
        heads, layout, hidden, scalars, inputs, out_grad, vectors, received, ff, []
    )
    arrived = exchange(grad_ctx, size)

    grads = turned(size, [normed_low, pre_low, summed_low], [grad_up, active, context])
    first = [grads]
    grads = lax.psum_scatter(grads, dp, scatter_dimension=0, tiled=True)

    backs, head_mine, head_other, bias_sums = [], [], [], []
    for h in range(heads):
        after = backs[h - 2][1:] if h >= 2 else first
        outs = attend_back(size, h, order, seg, slots, turned_x, arrived, after)
        backs.append(exchange(outs[:size], size))
        head_mine.append(outs[size])
        head_other.append(outs[size + 1])
        bias_sums.append(outs[size + 2])
        if h < len(bits_of(size)):
            small = small + swap(small, "tensor", bits_of(size)[h])
            arrived, small = tie(arrived, small)
    mine = jnp.concatenate(head_mine, axis=1)
    far = swap(jnp.concatenate(head_other, axis=1), "core", 1)
    sums = jnp.concatenate([small, jnp.pad(jnp.concatenate(bias_sums, axis=0), ((0, 0), (0, width - PAIR)))], axis=0)
    sums = sums + swap(sums, "core", 1)
    for bit in bits:
        mine, sent = halves(mine, far)
        far = swap(sent, "chip", bit)
        sums = sums + swap(sums, "chip", bit)
    head_sum = add_low(mine, far)
    grad_inputs = grad_summed
    for h in range(heads):
        grad_inputs = finish(h, layout, grad_inputs, later, backs[h], [grads])
    grad_query_weight, grad_key_weight, grad_value_weight = unmix(head_sum, local_width)
    bias = sums[small.shape[0] :]
    grad_query_bias = bias[:, :HD].reshape(local_width)
    grad_value_bias = bias[:, HD:PAIR].reshape(local_width)
    grad_up_bias = lax.dynamic_index_in_dim(sums, 8 + rank, 0, keepdims=False)
    lanes = grads.shape[1] // size
    grads = total_of(exchange([grads[:, k * lanes : (k + 1) * lanes] for k in range(size)], size))
    grad_up_weight = grads[:, :hidden]
    grad_down_weight = grads[:, hidden : 2 * hidden].T
    grad_out_weight = grads[:, 2 * hidden : 2 * hidden + local_width].T
    return (
        layer_out, grad_inputs, grad_query_weight, grad_query_bias, grad_key_weight, grad_value_weight,
        grad_value_bias, grad_out_weight, sums[0], sums[1], sums[2], grad_up_weight, grad_up_bias,
        grad_down_weight, sums[3], sums[4], sums[5],
    )


def solution(mesh):
    devices = mesh.devices
    split = Mesh(devices.reshape(devices.shape[0] // 2, 2, devices.shape[1]), ("chip", "core", "tensor"))
    dp = ("chip", "core")
    rows, weight, turned_weight, vector, same = (
        P(dp + ("tensor",), None),
        P(dp, "tensor"),
        P("tensor", dp),
        P("tensor"),
        P(),
    )
    in_specs = (
        rows, rows, P(dp, None), P(dp, None), P(dp, "tensor", None), weight, vector, weight, weight,
        vector, turned_weight, same, same, same, weight, vector, turned_weight, same, same, same,
    )
    out_specs = (
        rows, rows, weight, vector, weight, weight, vector, turned_weight, same, same, same, weight, vector,
        turned_weight, same, same, same,
    )
    return jax.shard_map(local, mesh=split, in_specs=in_specs, out_specs=out_specs, check_vma=False)
```

```python
import functools

import jax
import jax.numpy as jnp
from jax import lax
from jax.experimental import pallas as pl
from jax.experimental.pallas import tpu as pltpu
from jax.sharding import Mesh, PartitionSpec as P

HD = 64
CL = 128
PAIR = 2 * HD
WIDE = 4 * HD
F32 = jnp.float32
BF16 = jnp.bfloat16
EPS = 1e-06
PEAK_PER_MICRO = 1.15e9


def nn(left, right):
    return jnp.dot(left, right, preferred_element_type=F32)


def nt(left, right):
    return lax.dot_general(left, right, (((1,), (1,)), ((), ())), preferred_element_type=F32)


def tn(left, right):
    return lax.dot_general(left, right, (((0,), (0,)), ((), ())), preferred_element_type=F32)


def one_hot(hits):
    return jnp.where(hits, 1.0, 0.0).astype(BF16)


def head_lane(shape, dim, part):
    lane = lax.broadcasted_iota(jnp.int32, shape, dim)
    column = (lane // WIDE) * HD + lane % HD
    return jnp.where((lane % WIDE) // HD == part, column, -1)


def prepare_kernel(q_ref, k_ref, v_ref, o_ref, up_ref, dn_ref, heads_ref, ff_ref):
    shape = (q_ref.shape[1], heads_ref.shape[1])
    column = lax.broadcasted_iota(jnp.int32, shape, 0)
    total = jnp.zeros(heads_ref.shape, F32)
    for part, ref in ((0, q_ref), (1, v_ref), (2, k_ref)):
        total = total + nn(ref[...], one_hot(head_lane(shape, 1, part) == column))
    heads_ref[...] = total.astype(BF16)
    hidden = up_ref.shape[1]
    ff_ref[:, :hidden] = up_ref[...]
    ff_ref[:, hidden : 2 * hidden] = dn_ref[...]
    shape = (ff_ref.shape[1] - 2 * hidden, o_ref.shape[0])
    spread = one_hot(lax.broadcasted_iota(jnp.int32, shape, 0) == lax.broadcasted_iota(jnp.int32, shape, 1))
    padded = nn(spread, o_ref[...]).astype(BF16)
    rows = o_ref.shape[1]
    same = lax.broadcasted_iota(jnp.int32, (rows, rows), 0) == lax.broadcasted_iota(jnp.int32, (rows, rows), 1)
    ff_ref[:, 2 * hidden :] = nt(one_hot(same), padded).astype(BF16)


def unmix_kernel(grads_ref, q_ref, k_ref, v_ref):
    shape = (q_ref.shape[1], grads_ref.shape[1])
    column = lax.broadcasted_iota(jnp.int32, shape, 0)
    for part, ref in ((0, q_ref), (1, v_ref), (2, k_ref)):
        ref[...] = nt(grads_ref[...], one_hot(head_lane(shape, 1, part) == column))


def column_of(row):
    return jnp.transpose(jnp.broadcast_to(row, (CL, CL)))


def order_kernel(seqs, scal_ref, clusters_ref, balance_ref, order_ref, wide_ref, mask_ref):
    count = balance_ref.shape[1]
    step = 2 * CL
    rows = scal_ref[2]
    balance = balance_ref[...]
    high = balance // HD
    low = balance - high * HD
    pick = lax.broadcasted_iota(jnp.int32, (8, count), 0)
    table = jnp.where(pick == 0, high, jnp.where(pick == 1, low, 0)).astype(F32).astype(BF16)
    chosen = clusters_ref[0]
    total = jnp.zeros((8, count), F32)
    for start in range(0, count, step):
        place = lax.broadcasted_iota(jnp.int32, (step, count), 0) + start
        total = total + nn(table[:, start : start + step], one_hot(place == chosen))
    token = (total[0:1] * float(HD) + total[1:2]).astype(jnp.int32)
    segment = jnp.zeros_like(token)
    for s in range(seqs):
        segment = segment + jnp.where(token >= scal_ref[3 + s], 1, 0)
    segment = segment.astype(F32)
    from_own = scal_ref[0] * rows - (token // rows) * rows
    from_own = jnp.where(from_own < 0, from_own + count, from_own)
    order = (from_own + token % rows).astype(F32)
    order_ref[0] = order
    for at in range(0, count, CL):
        wide_ref[0, at : at + CL] = column_of(order[:, at : at + CL])
        row = segment[:, at : at + CL]
        mask_ref[0, at : at + CL] = jnp.where(column_of(row) == row, 0.0, -1e30).astype(BF16)


def slots_by_tokens(wide_ref, start, span, count):
    lane = lax.broadcasted_iota(jnp.int32, (span, CL), 1).astype(F32)
    gap = wide_ref[0, pl.ds(start, span)] - lane
    return jnp.concatenate([one_hot(gap == float(j)) for j in range(0, count, CL)], axis=1)


def tokens_by_slots(order_ref, start, span, count):
    row = order_ref[0] - jnp.asarray(start, F32)
    return one_hot(lax.broadcasted_iota(jnp.int32, (span, count), 0).astype(F32) == row)


def by_cluster(product, left, right):
    return jnp.concatenate(
        [product(left[at : at + CL], right[at : at + CL]) for at in range(0, left.shape[0], CL)], axis=0
    )


def softmax_of(first, second, mask):
    scores = by_cluster(nt, first, second) * HD ** (-0.5) + mask.astype(F32)
    raised = jnp.exp(scores - jnp.max(scores, axis=1, keepdims=True))
    return raised * (1.0 / jnp.sum(raised, axis=1, keepdims=True))


def upper_half(values):
    lane = lax.broadcasted_iota(jnp.int32, values.shape, 1)
    return jnp.where(lane >= HD, values, 0.0)


def project_kernel(size, heads, step, scal_ref, w_ref, b_ref, *refs):
    pieces = refs[: 1 if step == 0 else 2]
    x_out, qkv_out, x_ref, qkv_ref, sem, out_sem = refs[-6:]
    rows = x_ref.shape[0]
    rank = scal_ref[0]

    def block(piece, k):
        incoming = pltpu.make_async_copy(piece, x_ref, sem)
        incoming.start()
        incoming.wait()
        place = pl.ds(k * rows, rows)
        leaving = [pltpu.make_async_copy(x_ref, x_out.at[place], out_sem.at[heads])]
        leaving[0].start()
        for h in range(heads):
            lanes = slice(h * WIDE, (h + 1) * WIDE)
            qkv_ref[h] = (nn(x_ref[...], w_ref[:, lanes]) + b_ref[:, lanes]).astype(BF16)
            leaving.append(pltpu.make_async_copy(qkv_ref.at[h], qkv_out.at[h, place], out_sem.at[h]))
            leaving[-1].start()
        for copy in leaving:
            copy.wait()

    if step == 0:
        block(pieces[0], 0)
        return

    @pl.when(rank >= step)
    def _():
        block(pieces[0], step)

    @pl.when(rank < size - step)
    def _():
        block(pieces[1], size - step)


def forward_kernel(size, heads, span, order_ref, wide_ref, mask_ref, qkv_ref, extra_ref, slots_ref, *refs):
    outs, ctx_ref = refs[:size], refs[size]
    head = pl.program_id(0)
    count = qkv_ref.shape[1]
    rows = count // size
    half = rows // 2
    for k in range(size):
        outs[k][heads * half :] = extra_ref[...]

    def gather(i, carry):
        start = pl.multiple_of(i * span, span)
        here = pl.ds(start, span)
        picked = nn(slots_by_tokens(wide_ref, start, span, count), qkv_ref[0]).astype(BF16)
        slots_ref[0, here] = picked
        first = picked[:, :PAIR]
        probs = softmax_of(first, picked[:, PAIR:], mask_ref[0, here])
        ctx_ref[here] = upper_half(by_cluster(nn, probs.astype(BF16), first)).astype(BF16)
        return carry

    lax.fori_loop(0, count // span, gather, 0)
    at = pl.ds(pl.multiple_of(head * half, half), half)
    for k in range(size):
        given = nn(tokens_by_slots(order_ref, k * rows, rows, count), ctx_ref[...])
        outs[k][at] = (pltpu.roll(given[:half], HD, 1) + given[half:]).astype(BF16)


def backward_kernel(size, span, order_ref, wide_ref, mask_ref, slots_ref, turned_ref, *refs):
    g_refs, outs = refs[:size], refs[size : 2 * size]
    mine_ref, other_ref, bias_ref, gctx_ref, grad_ref, tok_ref = refs[2 * size :]
    count = slots_ref.shape[1]
    rows = count // size
    half = rows // 2
    for k in range(size):
        packed = g_refs[k][...].astype(F32)
        gctx_ref[k * rows : k * rows + half] = upper_half(pltpu.roll(packed, HD, 1)).astype(BF16)
        gctx_ref[k * rows + half : (k + 1) * rows] = upper_half(packed).astype(BF16)

    def gather(i, sums):
        start = pl.multiple_of(i * span, span)
        here = pl.ds(start, span)
        grad_ctx = nn(slots_by_tokens(wide_ref, start, span, count), gctx_ref[...]).astype(BF16)
        part = slots_ref[0, here]
        first, second = part[:, :PAIR], part[:, PAIR:]
        probs = softmax_of(first, second, mask_ref[0, here])
        grad_prob = by_cluster(nt, grad_ctx, first)
        inner = jnp.sum(probs * grad_prob, axis=1, keepdims=True)
        grad_scores = (probs * (grad_prob - inner)).astype(BF16)
        grad_query = by_cluster(nn, grad_scores, second) * HD ** (-0.5)
        grad_key = by_cluster(tn, grad_scores, first) * HD ** (-0.5)
        grad_value = by_cluster(tn, probs.astype(BF16), grad_ctx)
        lane = lax.broadcasted_iota(jnp.int32, (span, PAIR), 1)
        grad_qv = jnp.where(lane < HD, grad_query, grad_value).astype(BF16)
        grad_ref[here, :PAIR] = grad_qv
        grad_ref[here, PAIR:] = jnp.where(lane < HD, grad_key, 0.0).astype(BF16)
        return sums + jnp.sum(grad_qv.astype(F32), axis=0, keepdims=True)

    bias_ref[...] = lax.fori_loop(0, count // span, gather, jnp.zeros((1, PAIR), F32))
    for k in range(size):
        given = nn(tokens_by_slots(order_ref, k * rows, rows, count), grad_ref[...])
        low = given.astype(BF16)
        tok_ref[k * rows : (k + 1) * rows] = low
        outs[k][:rows] = low[:, :PAIR]
        outs[k][rows:] = (given[:half, PAIR:] + pltpu.roll(given[half:, PAIR:], HD, 1)).astype(BF16)
    cut = turned_ref.shape[0] // 2
    mine_ref[...] = nn(turned_ref[:cut], tok_ref[...]).astype(BF16)
    other_ref[...] = nn(turned_ref[cut:], tok_ref[...]).astype(BF16)


def row_stats(values_in):
    center = values_in - jnp.mean(values_in, axis=-1, keepdims=True)
    inverse = lax.rsqrt(jnp.mean(center * center, axis=-1, keepdims=True) + EPS)
    return center * inverse, inverse


def norm_back(cotangent, gain, hat, inverse):
    scaled = cotangent * gain
    return inverse * (
        scaled
        - jnp.mean(scaled, axis=-1, keepdims=True)
        - hat * jnp.mean(scaled * hat, axis=-1, keepdims=True)
    )


def column_sum(values_in):
    return jnp.sum(values_in, axis=0, keepdims=True)


def row_copies(ref, layout, start, lanes, held, sem):
    size, groups, shard = layout
    if groups == 1:
        shard = held.shape[0]
    return [
        pltpu.make_async_copy(
            ref.at[pl.ds((group * size + k) * shard, shard), pl.ds(start, lanes)],
            held.at[pl.ds(group * shard, shard), pl.ds(k * lanes, lanes)],
            sem,
        )
        for group in range(groups)
        for k in range(size)
    ]


def all_of(held, sem):
    return pltpu.make_async_copy(held, held, sem)


def layer_kernel(heads, layout, scal_ref, x_ref, og_ref, vec_ref, ff_ref, *refs):
    size = layout[0]
    recv_refs, refs = refs[: 2 * size], refs[2 * size :]
    layer_ref, sum_ref, small_ref, grads_out = refs[:4]
    gctx_refs = refs[4 : 4 + size]
    (
        wup_ref, wdn_ref, wo_ref, act_ref, slope_ref, total_ref, gup_ref, nlow_ref, plow_ref, slow_ref, ctx_ref,
        nturn_ref, pturn_ref, stage_ref, sem, out_sem,
    ) = refs[4 + size :]
    rows, width = x_ref.shape
    hidden = wup_ref.shape[1] // size
    head_lanes = wo_ref.shape[1] // size
    block = 2 * hidden + head_lanes
    rank = scal_ref[0]

    for kind, (start, lanes, held) in enumerate(
        ((2 * hidden, head_lanes, wo_ref), (0, hidden, wup_ref), (hidden, hidden, wdn_ref))
    ):
        for copy in row_copies(ff_ref, layout, start, lanes, held, sem.at[kind]):
            copy.start()

    half = rows // 2
    lower = lax.broadcasted_iota(jnp.int32, (half, PAIR), 1) < HD

    def piece(k, h):
        if h >= heads:
            return jnp.zeros((half, PAIR), F32)
        if h == heads - 1:
            return recv_refs[size + k][:half].astype(F32)
        return recv_refs[k][h * half : (h + 1) * half].astype(F32)

    for k in range(size):
        for h in range(0, heads, 2):
            first, second = piece(k, h), piece(k, h + 1)
            lanes = slice(k * head_lanes + h * HD, k * head_lanes + h * HD + PAIR)
            ctx_ref[:half, lanes] = jnp.where(lower, first, pltpu.roll(second, HD, 1)).astype(BF16)
            ctx_ref[half:, lanes] = jnp.where(lower, pltpu.roll(first, HD, 1), second).astype(BF16)
    row = lax.broadcasted_iota(jnp.int32, (width, width), 0)
    same = one_hot(row == lax.broadcasted_iota(jnp.int32, (width, width), 1))
    all_of(wo_ref, sem.at[0]).wait()
    summed = x_ref[...].astype(F32) + nt(ctx_ref[...], wo_ref[...]) + vec_ref[0:1]
    hat1, inverse1 = row_stats(summed)
    normed = hat1 * vec_ref[1:2] + vec_ref[2:3]
    nlow_ref[...] = normed.astype(BF16)
    total_ref[...] = normed + vec_ref[3:4]
    curve = (2.0 / 3.141592653589793) ** 0.5
    cut = hidden // PAIR
    biases = []
    for k in range(size):
        parts = recv_refs[k][(heads - 1) * half :].astype(F32)
        bias = parts[:cut] + parts[cut : 2 * cut] + parts[2 * cut : 3 * cut]
        biases.append(jnp.concatenate([bias[i : i + 1] for i in range(cut)], axis=1))
        small_ref[8 + k : 9 + k] = biases[-1]
    all_of(wup_ref, sem.at[1]).wait()
    all_of(wdn_ref, sem.at[2]).wait()

    def span(k):
        return pl.ds(pl.multiple_of(k * hidden, hidden), hidden)

    def forward(k, carry):
        lanes = span(k)
        up = nn(nlow_ref[...], wup_ref[:, lanes]) + small_ref[pl.ds(8 + k, 1)]
        square = up * up
        tanh = jnp.tanh(up * (curve + (0.044715 * curve) * square))
        gate = 0.5 + 0.5 * tanh
        act_ref[:, lanes] = (up * gate).astype(BF16)
        slope_ref[:, lanes] = gate + (0.5 * up) * (1.0 - tanh * tanh) * (curve + (3 * 0.044715 * curve) * square)
        total_ref[...] += nt(act_ref[:, lanes], wdn_ref[:, lanes])
        return carry

    lax.fori_loop(0, size, forward, 0)
    nturn_ref[...] = nt(same, nlow_ref[...]).astype(BF16)
    hat2, inverse2 = row_stats(total_ref[...])
    gain2 = vec_ref[4:5]
    layer_ref[...] = (hat2 * gain2 + vec_ref[5:6]).astype(BF16)
    cot = og_ref[...].astype(F32)
    grad_pre = norm_back(cot, gain2, hat2, inverse2)
    plow_ref[...] = grad_pre.astype(BF16)
    pturn_ref[...] = nt(same, plow_ref[...]).astype(BF16)
    small_ref[3:4] = column_sum(grad_pre)
    small_ref[4:5] = column_sum(cot * hat2)
    small_ref[5:6] = column_sum(cot)
    small_ref[6:8] = jnp.zeros((2, width), F32)
    total_ref[...] = grad_pre

    def leave(k):
        at = pl.multiple_of(k * block, block)
        return pltpu.make_async_copy(stage_ref, grads_out.at[:, pl.ds(at, 2 * hidden)], out_sem.at[0])

    def backward(k, carry):
        lanes = span(k)
        grad_up = (nn(plow_ref[...], wdn_ref[:, lanes]) * slope_ref[:, lanes]).astype(BF16)
        gup_ref[...] = grad_up
        small_ref[pl.ds(8 + lax.rem(rank - k + size, size), 1)] = column_sum(grad_up.astype(F32))
        total_ref[...] += nt(gup_ref[...], wup_ref[:, lanes])

        @pl.when(k > 0)
        def _():
            leave(k - 1).wait()

        stage_ref[:, :hidden] = nn(nturn_ref[...], gup_ref[...]).astype(BF16)
        stage_ref[:, hidden:] = nn(pturn_ref[...], act_ref[:, lanes]).astype(BF16)
        leave(k).start()
        return carry

    lax.fori_loop(0, size, backward, 0)
    grad_normed = total_ref[...]
    small_ref[1:2] = column_sum(grad_normed * hat1)
    small_ref[2:3] = column_sum(grad_normed)
    grad_summed = norm_back(grad_normed, vec_ref[1:2], hat1, inverse1)
    small_ref[0:1] = column_sum(grad_summed)
    sum_ref[...] = grad_summed
    slow_ref[...] = grad_summed.astype(BF16)
    grad_ctx = nn(slow_ref[...], wo_ref[...])
    for k in range(size):
        for h in range(0, heads, 2):
            lanes = slice(k * head_lanes + h * HD, k * head_lanes + h * HD + PAIR)
            top, bottom = grad_ctx[:half, lanes], grad_ctx[half:, lanes]
            gctx_refs[k][h * half : (h + 1) * half] = jnp.where(lower, top, pltpu.roll(bottom, HD, 1)).astype(BF16)
            if h + 1 < heads:
                gctx_refs[k][(h + 1) * half : (h + 2) * half] = jnp.where(
                    lower, pltpu.roll(top, HD, 1), bottom
                ).astype(BF16)
    leave(size - 1).wait()
    nturn_ref[...] = nt(same, slow_ref[...]).astype(BF16)
    leaving = []
    for k in range(size):
        kept = stage_ref.at[:, pl.ds(k * head_lanes, head_lanes)]
        stage_ref[:, k * head_lanes : (k + 1) * head_lanes] = nn(
            nturn_ref[...], ctx_ref[:, k * head_lanes : (k + 1) * head_lanes]
        ).astype(BF16)
        leaving.append(
            pltpu.make_async_copy(kept, grads_out.at[:, pl.ds(k * block + 2 * hidden, head_lanes)], out_sem.at[1 + k])
        )
        leaving[-1].start()
    for copy in leaving:
        copy.wait()


def flip_kernel(pick_ref, left_ref, turned_ref):
    turned_ref[...] = nt(pick_ref[...], left_ref[...]).astype(BF16)


def finish_kernel(head, layout, acc_ref, w_ref, *refs):
    size = layout[0]
    out_ref, held_ref, grads_ref, sem = refs[-4:]
    g_refs = refs[:size]
    rows = acc_ref.shape[0]
    half = rows // 2
    for copy in row_copies(w_ref, layout, head * WIDE, WIDE, held_ref, sem):
        copy.start()
    lower = lax.broadcasted_iota(jnp.int32, (half, PAIR), 1) < HD
    for k in range(size):
        at = k * WIDE
        grads_ref[:, at : at + PAIR] = g_refs[k][:rows]
        packed = g_refs[k][rows:].astype(F32)
        grads_ref[:half, at + PAIR : at + WIDE] = jnp.where(lower, packed, 0.0).astype(BF16)
        grads_ref[half:, at + PAIR : at + WIDE] = jnp.where(lower, pltpu.roll(packed, HD, 1), 0.0).astype(BF16)
    all_of(held_ref, sem).wait()
    out_ref[...] = acc_ref[...] + nt(grads_ref[...], held_ref[...])


def cost(micros, exps=0):
    return pl.CostEstimate(flops=int(micros * PEAK_PER_MICRO), bytes_accessed=0, transcendentals=int(exps))


def head_spec(shape, head):
    return pl.BlockSpec((1,) + shape, lambda i: (head,) + (0,) * len(shape))


def full(shape):
    return pl.BlockSpec(tuple(shape), lambda i: (0,) * len(shape))


def held():
    return pl.BlockSpec(memory_space=pl.ANY)


def scalars_spec():
    return pl.BlockSpec(memory_space=pltpu.SMEM)


def shape_of(shape, dtype=BF16):
    return jax.ShapeDtypeStruct(tuple(shape), dtype)


def call(kernel, name, in_specs, out_specs, out_shape, scratch, estimate, mib, grid=(1,), after=()):
    count = len(in_specs)

    def body(*refs):
        kernel(*refs[:count], *refs[count + len(after) :])

    run = pl.pallas_call(
        body,
        grid=grid,
        in_specs=list(in_specs) + [held()] * len(after),
        out_specs=out_specs,
        out_shape=out_shape,
        scratch_shapes=scratch,
        compiler_params=pltpu.CompilerParams(vmem_limit_bytes=mib * 1024 * 1024),
        name=name,
        cost_estimate=estimate,
    )
    return lambda *args: run(*args, *after)


def prepare(query, key, value, out, up, down_t, heads):
    shard, hidden = up.shape
    lanes = 2 * hidden + -(-out.shape[0] // CL) * CL
    args = (query, key, value, out, up, down_t)
    shapes = [shape_of((shard, heads * WIDE)), shape_of((shard, lanes))]
    return call(
        prepare_kernel, "prepare", [full(a.shape) for a in args], [full(s.shape) for s in shapes], shapes, [],
        cost(1), 60,
    )(*args)


def unmix(grads, local_width):
    shard = grads.shape[0]
    shapes = [shape_of((shard, local_width), F32)] * 3
    return call(
        unmix_kernel, "unmix", [full(grads.shape)], [full(s.shape) for s in shapes], shapes, [],
        cost(1), 16,
    )(grads)


def slot_tokens(seqs, scalars, clusters, balance):
    heads, count = clusters.shape[0], clusters.shape[2]
    row = pl.BlockSpec((1, 1, count), lambda h: (h, 0, 0))
    wide = pl.BlockSpec((1, count, CL), lambda h: (h, 0, 0))
    return call(
        functools.partial(order_kernel, seqs), "slot_tokens",
        [scalars_spec(), row, full(balance.shape)], [row, wide, wide],
        [shape_of((heads, 1, count), F32), shape_of((heads, count, CL), F32), shape_of((heads, count, CL))], [],
        cost(10), 16, grid=(heads,),
    )(scalars, clusters, balance)


def project(size, heads, step, scalars, weights, biases, pieces, held_before):
    rows, width = pieces[0].shape
    shapes = [shape_of((size * rows, width)), shape_of((heads, size * rows, WIDE))]
    first = 3 + len(pieces)
    return pl.pallas_call(
        functools.partial(project_kernel, size, heads, step),
        grid=(1,),
        in_specs=[scalars_spec(), full(weights.shape), full(biases.shape)]
        + [held()] * (len(pieces) + len(held_before)),
        out_specs=[held()] * 2,
        out_shape=shapes,
        scratch_shapes=[
            pltpu.VMEM((rows, width), BF16),
            pltpu.VMEM((heads, rows, WIDE), BF16),
            pltpu.SemaphoreType.DMA(()),
            pltpu.SemaphoreType.DMA((heads + 1,)),
        ],
        input_output_aliases={first: 0, first + 1: 1} if step else {},
        compiler_params=pltpu.CompilerParams(vmem_limit_bytes=24 * 1024 * 1024),
        name="project",
        cost_estimate=cost(2),
    )(scalars, weights, biases, *pieces, *held_before)


def attend(size, first, heads, order, wide, mask, qkv, extra, after):
    count = qkv.shape[1]
    half = count // size // 2
    row = pl.BlockSpec((1, 1, count), lambda h: (h + first, 0, 0))
    block = pl.BlockSpec((1, count, WIDE), lambda h: (h + first, 0, 0))
    column = pl.BlockSpec((1, count, CL), lambda h: (h + first, 0, 0))
    shapes = [shape_of((heads, count, WIDE))] + [shape_of((heads * half + extra.shape[0], PAIR))] * size
    return call(
        functools.partial(forward_kernel, size, heads, count // 2), "attend",
        [row, column, column, block, full(extra.shape)],
        [pl.BlockSpec((1, count, WIDE), lambda h: (h, 0, 0))] + [full(s.shape) for s in shapes[1:]], shapes,
        [pltpu.VMEM((count, PAIR), BF16)],
        cost(6.5 * heads), 40, grid=(heads,), after=after,
    )(order, wide, mask, qkv, extra)


def attend_back(size, head, order, wide, mask, slots, place, turned_x, grad_context, after):
    count = slots.shape[1]
    rows = count // size
    cut = turned_x.shape[0] // 2
    shapes = (
        [shape_of((rows + rows // 2, PAIR))] * size + [shape_of((cut, WIDE))] * 2 + [shape_of((1, PAIR), F32)]
    )
    return call(
        functools.partial(backward_kernel, size, count // 2), "attend_back",
        [head_spec((1, count), head), head_spec((count, CL), head), head_spec((count, CL), head)]
        + [head_spec((count, WIDE), place), full(turned_x.shape)]
        + [pl.BlockSpec((rows // 2, PAIR), lambda i: (head, 0))] * size,
        [full(s.shape) for s in shapes], shapes,
        [pltpu.VMEM((count, PAIR), BF16), pltpu.VMEM((count, WIDE), BF16), pltpu.VMEM((count, WIDE), BF16)],
        cost(3), 40, after=after,
    )(order, wide, mask, slots, turned_x, *grad_context)


def layer(heads, layout, hidden, scalars, inputs, out_grad, vectors, received, ff):
    size = layout[0]
    rows, width = inputs.shape
    block = ff.shape[1]
    head_lanes = block - 2 * hidden
    shapes = [
        shape_of((rows, width)),
        shape_of((rows, width), F32),
        shape_of((8 + size, width), F32),
        shape_of((width, size * block)),
    ] + [shape_of((heads * (rows // 2), PAIR))] * size
    args = (inputs, out_grad, vectors)

    def kept(shape, dtype=BF16):
        return pltpu.VMEM(shape, dtype)

    return call(
        functools.partial(layer_kernel, heads, layout), "layer",
        [scalars_spec()] + [full(a.shape) for a in args] + [held()] + [full(r.shape) for r in received],
        [full(s.shape) if i != 3 else held() for i, s in enumerate(shapes)], shapes,
        [
            kept((width, size * hidden)),
            kept((width, size * hidden)),
            kept((width, size * head_lanes)),
            kept((rows, size * hidden)),
            kept((rows, size * hidden), F32),
            kept((rows, width), F32),
            kept((rows, hidden)),
            kept((rows, width)),
            kept((rows, width)),
            kept((rows, width)),
            kept((rows, size * head_lanes)),
            kept((width, rows)),
            kept((width, rows)),
            kept((width, 2 * hidden)),
            pltpu.SemaphoreType.DMA((3,)),
            pltpu.SemaphoreType.DMA((1 + size,)),
        ],
        cost(33), 58,
    )(scalars, *args, ff, *received)


def flip(size, pick, left):
    count, width = left.shape
    rows = count // size
    return call(
        flip_kernel, "flip",
        [full(pick.shape), pl.BlockSpec((rows, width), lambda i: (i, 0))],
        pl.BlockSpec((width, rows), lambda i: (0, i)), shape_of((width, count)), [],
        cost(0.05), 16, grid=(size,),
    )(pick, left)


def finish(head, layout, total, weights, grads, after):
    size = layout[0]
    rows, width = total.shape
    return call(
        functools.partial(finish_kernel, head, layout), "finish",
        [full(total.shape), held()] + [full(g.shape) for g in grads],
        full(total.shape), shape_of(total.shape, F32),
        [
            pltpu.VMEM((width, size * WIDE), BF16),
            pltpu.VMEM((rows, size * WIDE), BF16),
            pltpu.SemaphoreType.DMA(()),
        ],
        cost(1), 24, after=after,
    )(total, weights, *grads)


def shift(values, size, k):
    return lax.ppermute(values, "tensor", [(i, (i + k) % size) for i in range(size)])


def exchange(parts, size):
    return [parts[0]] + [shift(parts[size - k], size, k) for k in range(1, size)]


def gather_line(own, size):
    up, down = own, own
    ups, downs = [], []
    for k in range(1, size):
        up = lax.ppermute(up, "tensor", [(i, i + 1) for i in range(k - 1, size - 1)])
        down = lax.ppermute(down, "tensor", [(i + 1, i) for i in range(0, size - k)])
        ups.append(up)
        downs.append(down)
    return ups, downs


def swap(values, axis, bit):
    return lax.ppermute(values, axis, [(i, i ^ bit) for i in range(lax.axis_size(axis))])


def bits_of(size):
    return [1 << b for b in range(size.bit_length() - 1)]


def add_low(left, right):
    return (left.astype(F32) + right.astype(F32)).astype(BF16)


def halves(mine, arrived):
    cut = mine.shape[0] // 2
    return add_low(mine[:cut], arrived[:cut]), add_low(mine[cut:], arrived[cut:])


def total_of(parts):
    result = parts[0].astype(F32)
    for part in parts[1:]:
        result = result + part.astype(F32)
    return result


def tie(*groups):
    return lax.optimization_barrier(groups)


def local(
    inputs, out_grad, seq_lengths, balance, clusters, query_weight, query_bias, key_weight,
    value_weight, value_bias, out_weight, out_bias, norm1_gain, norm1_bias, up_weight, up_bias,
    down_weight, down_bias, norm2_gain, norm2_bias,
):
    dp = ("chip", "core")
    rows, width = inputs.shape
    size = lax.axis_size("tensor")
    chips = lax.axis_size("chip")
    rank, chip, core = (lax.axis_index(axis) for axis in ("tensor", "chip", "core"))
    shard = query_weight.shape[0]
    local_width = query_weight.shape[1]
    heads = clusters.shape[1]
    seqs = seq_lengths.shape[1]
    bits = bits_of(chips)

    bounds = jnp.cumsum(seq_lengths[0])
    scalars = jnp.concatenate([jnp.stack([rank, core, jnp.int32(rows)]), bounds]).astype(jnp.int32)
    direct = shard % 16 == 0
    layout = (size, 2 * chips if direct else 1, shard)
    hidden = up_weight.shape[1]

    def near_of(own):
        ups, downs = gather_line(own, size)
        return jnp.concatenate(
            [own] + [jnp.where(rank >= k, ups[k - 1], downs[size - 1 - k]) for k in range(1, size)], axis=0
        )

    def whole(near):
        rows_in = lax.all_gather(near, dp, axis=0, tiled=True)
        if direct:
            return rows_in
        lanes = near.shape[1]
        return rows_in.reshape(2 * chips, size, shard, lanes).transpose(1, 0, 2, 3).reshape(size * width, lanes)

    head_weights, ff_own = prepare(
        query_weight, key_weight, value_weight, out_weight, up_weight, down_weight.T, heads
    )
    ups, downs = gather_line(inputs, size)
    own_qkv = lax.all_gather(head_weights, dp, axis=0, tiled=True)
    near, own_qkv, ups[0], downs[0] = tie(near_of(ff_own), own_qkv, ups[0], downs[0])
    ff = whole(near)
    blank = jnp.zeros((heads, HD), F32)
    head_biases = jnp.concatenate(
        [query_bias.reshape(heads, HD), value_bias.reshape(heads, HD), blank, blank], axis=-1
    ).reshape(1, heads * WIDE)
    terms, rest = [], up_bias
    for _ in range(3):
        term = lax.reduce_precision(rest, 8, 7)
        terms.append(term.astype(BF16))
        rest = rest - term
    extra = jnp.concatenate(terms).reshape(-1, PAIR)
    extra = jnp.pad(extra, ((0, -extra.shape[0] % 16), (0, 0)))
    vectors = jnp.stack([out_bias, norm1_gain, norm1_bias, down_bias, norm2_gain, norm2_bias])

    def row_pick(order_bits):
        place = jnp.arange(width, dtype=jnp.int32)
        block = place // shard
        away = jnp.zeros_like(block)
        for depth, bit in enumerate(order_bits):
            away = away + ((block >> (len(order_bits) - 1 - depth)) & 1) * bit
        near = chip ^ away
        owner = near * 2 + (core ^ (block // chips))
        return one_hot((owner * shard + place % shard)[:, None] == place[None, :])

    pick = row_pick(bits)
    order, wide, mask = slot_tokens(seqs, scalars, clusters[0][:, None, :], balance)
    whole_rows = []
    for step in range(size):
        pieces = [ups[step - 1], downs[step - 1]] if step else [inputs]
        whole_rows = project(size, heads, step, scalars, own_qkv, head_biases, pieces, whole_rows)
    x_all, qkv = whole_rows
    later_weights, qkv = tie(head_weights, qkv)
    later_near = jnp.concatenate([later_weights] + [shift(later_weights, size, k) for k in range(1, size)], axis=0)

    kept_a, *context_a = attend(size, 0, heads - 1, order, wide, mask, qkv, extra, [])
    context_a, later_near = tie(context_a, later_near)
    later = whole(later_near)
    kept_b, *context_b = attend(size, heads - 1, 1, order, wide, mask, qkv, extra[:16], [context_a[0]])
    received = exchange(context_a, size) + exchange(context_b, size)
    slots = [(kept_a, h) for h in range(heads - 1)] + [(kept_b, 0)]
    turned_x = flip(size, pick, x_all)
    layer_out, grad_summed, small, grads, *grad_ctx = layer(
        heads, layout, hidden, scalars, inputs, out_grad, vectors, received, ff
    )
    arrived = exchange(grad_ctx, size)
    grads, later = tie(grads, later)
    grads = lax.psum_scatter(grads, dp, scatter_dimension=0, tiled=True)

    backs, head_mine, head_other, bias_sums = [], [], [], []
    for h in range(heads):
        after = backs[h - 2][1:] if h >= 2 else []
        outs = attend_back(size, h, order, wide, mask, *slots[h], turned_x, arrived, after)
        backs.append(exchange(outs[:size], size))
        head_mine.append(outs[size])
        head_other.append(outs[size + 1])
        bias_sums.append(outs[size + 2])
        if h < len(bits_of(size)):
            small = small + swap(small, "tensor", bits_of(size)[h])
            arrived, small = tie(arrived, small)
    backs[heads - 2], head_other = tie(backs[heads - 2], head_other)
    mine = jnp.concatenate(head_mine, axis=1)
    far = swap(jnp.concatenate(head_other, axis=1), "core", 1)
    sums = jnp.concatenate([small, jnp.pad(jnp.concatenate(bias_sums, axis=0), ((0, 0), (0, width - PAIR)))], axis=0)
    sums = sums + swap(sums, "core", 1)
    for bit in bits:
        mine, sent = halves(mine, far)
        far = swap(sent, "chip", bit)
        sums = sums + swap(sums, "chip", bit)
    head_sum = add_low(mine, far)
    grad_query_weight, grad_key_weight, grad_value_weight = unmix(head_sum, local_width)
    bias = sums[small.shape[0] :]
    grad_query_bias = bias[:, :HD].reshape(local_width)
    grad_value_bias = bias[:, HD:PAIR].reshape(local_width)
    grad_up_bias = lax.dynamic_index_in_dim(sums, 8 + rank, 0, keepdims=False)
    backs[heads - 1], grads = tie(backs[heads - 1], grads)
    lanes = grads.shape[1] // size
    grads = total_of(exchange([grads[:, k * lanes : (k + 1) * lanes] for k in range(size)], size))
    grad_inputs = grad_summed
    for h in range(heads):
        grad_inputs = finish(h, layout, grad_inputs, later, backs[h], [])
    grad_up_weight = grads[:, :hidden]
    grad_down_weight = grads[:, hidden : 2 * hidden].T
    grad_out_weight = grads[:, 2 * hidden : 2 * hidden + local_width].T
    return (
        layer_out, grad_inputs, grad_query_weight, grad_query_bias, grad_key_weight, grad_value_weight,
        grad_value_bias, grad_out_weight, sums[0], sums[1], sums[2], grad_up_weight, grad_up_bias,
        grad_down_weight, sums[3], sums[4], sums[5],
    )


def solution(mesh):
    devices = mesh.devices
    split = Mesh(devices.reshape(devices.shape[0] // 2, 2, devices.shape[1]), ("chip", "core", "tensor"))
    dp = ("chip", "core")
    rows, weight, turned_weight, vector, same = (
        P(dp + ("tensor",), None),
        P(dp, "tensor"),
        P("tensor", dp),
        P("tensor"),
        P(),
    )
    in_specs = (
        rows, rows, P(dp, None), P(dp, None), P(dp, "tensor", None), weight, vector, weight, weight,
        vector, turned_weight, same, same, same, weight, vector, turned_weight, same, same, same,
    )
    out_specs = (
        rows, rows, weight, vector, weight, weight, vector, turned_weight, same, same, same, weight, vector,
        turned_weight, same, same, same,
    )
    return jax.shard_map(local, mesh=split, in_specs=in_specs, out_specs=out_specs, check_vma=False)
```

```python
import functools

import jax
import jax.numpy as jnp
from jax import lax
from jax.experimental import pallas as pl
from jax.experimental.pallas import tpu as pltpu
from jax.sharding import Mesh, PartitionSpec as P

HD = 64
CL = 128
PAIR = 2 * HD
WIDE = 4 * HD
F32 = jnp.float32
BF16 = jnp.bfloat16
EPS = 1e-06
PEAK_PER_MICRO = 1.15e9


def nn(left, right):
    return jnp.dot(left, right, preferred_element_type=F32)


def nt(left, right):
    return lax.dot_general(left, right, (((1,), (1,)), ((), ())), preferred_element_type=F32)


def tn(left, right):
    return lax.dot_general(left, right, (((0,), (0,)), ((), ())), preferred_element_type=F32)


def one_hot(hits):
    return jnp.where(hits, 1.0, 0.0).astype(BF16)


def head_lane(shape, dim, part):
    lane = lax.broadcasted_iota(jnp.int32, shape, dim)
    column = (lane // WIDE) * HD + lane % HD
    return jnp.where((lane % WIDE) // HD == part, column, -1)


def prepare_kernel(q_ref, k_ref, v_ref, o_ref, up_ref, dn_ref, heads_ref, ff_ref):
    shape = (q_ref.shape[1], heads_ref.shape[1])
    column = lax.broadcasted_iota(jnp.int32, shape, 0)
    total = jnp.zeros(heads_ref.shape, F32)
    for part, ref in ((0, q_ref), (1, v_ref), (2, k_ref)):
        total = total + nn(ref[...], one_hot(head_lane(shape, 1, part) == column))
    heads_ref[...] = total.astype(BF16)
    hidden = up_ref.shape[1]
    ff_ref[:, :hidden] = up_ref[...]
    ff_ref[:, hidden : 2 * hidden] = dn_ref[...]
    shape = (ff_ref.shape[1] - 2 * hidden, o_ref.shape[0])
    spread = one_hot(lax.broadcasted_iota(jnp.int32, shape, 0) == lax.broadcasted_iota(jnp.int32, shape, 1))
    padded = nn(spread, o_ref[...]).astype(BF16)
    rows = o_ref.shape[1]
    same = lax.broadcasted_iota(jnp.int32, (rows, rows), 0) == lax.broadcasted_iota(jnp.int32, (rows, rows), 1)
    ff_ref[:, 2 * hidden :] = nt(one_hot(same), padded).astype(BF16)


def unmix_kernel(grads_ref, q_ref, k_ref, v_ref):
    shape = (q_ref.shape[1], grads_ref.shape[1])
    column = lax.broadcasted_iota(jnp.int32, shape, 0)
    for part, ref in ((0, q_ref), (1, v_ref), (2, k_ref)):
        ref[...] = nt(grads_ref[...], one_hot(head_lane(shape, 1, part) == column))


def column_of(row):
    return jnp.transpose(jnp.broadcast_to(row, (CL, CL)))


def order_kernel(seqs, scal_ref, clusters_ref, balance_ref, order_ref, wide_ref, mask_ref, table_ref):
    count = balance_ref.shape[1]
    step = 2 * CL
    rows = scal_ref[2]
    balance = balance_ref[...]
    high = balance // HD
    low = balance - high * HD
    pick = lax.broadcasted_iota(jnp.int32, (8, count), 0)
    table = jnp.where(pick == 0, high, jnp.where(pick == 1, low, 0)).astype(F32).astype(BF16)
    chosen = clusters_ref[0]
    table_ref[...] = table

    def pick_block(i, total):
        start = pl.multiple_of(i * step, step)
        place = lax.broadcasted_iota(jnp.int32, (step, count), 0) + start
        return total + nn(table_ref[:, pl.ds(start, step)], one_hot(place == chosen))

    total = lax.fori_loop(0, count // step, pick_block, jnp.zeros((8, count), F32))
    token = (total[0:1] * float(HD) + total[1:2]).astype(jnp.int32)
    segment = jnp.zeros_like(token)
    for s in range(seqs):
        segment = segment + jnp.where(token >= scal_ref[3 + s], 1, 0)
    segment = segment.astype(F32)
    from_own = scal_ref[0] * rows - (token // rows) * rows
    from_own = jnp.where(from_own < 0, from_own + count, from_own)
    order = (from_own + token % rows).astype(F32)
    order_ref[0] = order
    for at in range(0, count, CL):
        wide_ref[0, at : at + CL] = column_of(order[:, at : at + CL])
        row = segment[:, at : at + CL]
        mask_ref[0, at : at + CL] = jnp.where(column_of(row) == row, 0.0, -1e30).astype(BF16)


def slots_by_tokens(wide_ref, start, span, count):
    lane = lax.broadcasted_iota(jnp.int32, (span, CL), 1).astype(F32)
    gap = wide_ref[0, pl.ds(start, span)] - lane
    return jnp.concatenate([one_hot(gap == float(j)) for j in range(0, count, CL)], axis=1)


def tokens_by_slots(order_ref, start, span, count):
    row = order_ref[0] - jnp.asarray(start, F32)
    return one_hot(lax.broadcasted_iota(jnp.int32, (span, count), 0).astype(F32) == row)


def by_cluster(product, left, right):
    return jnp.concatenate(
        [product(left[at : at + CL], right[at : at + CL]) for at in range(0, left.shape[0], CL)], axis=0
    )


def softmax_of(first, second, mask):
    scores = by_cluster(nt, first, second) * HD ** (-0.5) + mask.astype(F32)
    raised = jnp.exp(scores - jnp.max(scores, axis=1, keepdims=True))
    return raised * (1.0 / jnp.sum(raised, axis=1, keepdims=True))


def upper_half(values):
    lane = lax.broadcasted_iota(jnp.int32, values.shape, 1)
    return jnp.where(lane >= HD, values, 0.0)


def project_kernel(size, heads, step, scal_ref, w_ref, b_ref, *refs):
    pieces = refs[: 1 if step == 0 else 2]
    x_out, qkv_out, x_ref, qkv_ref, sem, out_sem = refs[-6:]
    rows = x_ref.shape[0]
    rank = scal_ref[0]

    def block(piece, k):
        incoming = pltpu.make_async_copy(piece, x_ref, sem)
        incoming.start()
        incoming.wait()
        place = pl.ds(k * rows, rows)
        leaving = [pltpu.make_async_copy(x_ref, x_out.at[place], out_sem.at[heads])]
        leaving[0].start()
        for h in range(heads):
            lanes = slice(h * WIDE, (h + 1) * WIDE)
            qkv_ref[h] = (nn(x_ref[...], w_ref[:, lanes]) + b_ref[:, lanes]).astype(BF16)
            leaving.append(pltpu.make_async_copy(qkv_ref.at[h], qkv_out.at[h, place], out_sem.at[h]))
            leaving[-1].start()
        for copy in leaving:
            copy.wait()

    if step == 0:
        block(pieces[0], 0)
        return

    @pl.when(rank >= step)
    def _():
        block(pieces[0], step)

    @pl.when(rank < size - step)
    def _():
        block(pieces[1], size - step)


def forward_kernel(size, heads, span, order_ref, wide_ref, mask_ref, qkv_ref, extra_ref, slots_ref, *refs):
    outs, ctx_ref = refs[:size], refs[size]
    head = pl.program_id(0)
    count = qkv_ref.shape[1]
    rows = count // size
    half = rows // 2
    for k in range(size):
        outs[k][heads * half :] = extra_ref[...]

    def gather(i, carry):
        start = pl.multiple_of(i * span, span)
        here = pl.ds(start, span)
        picked = nn(slots_by_tokens(wide_ref, start, span, count), qkv_ref[0]).astype(BF16)
        slots_ref[0, here] = picked
        first = picked[:, :PAIR]
        probs = softmax_of(first, picked[:, PAIR:], mask_ref[0, here])
        ctx_ref[here] = upper_half(by_cluster(nn, probs.astype(BF16), first)).astype(BF16)
        return carry

    lax.fori_loop(0, count // span, gather, 0)
    at = pl.ds(pl.multiple_of(head * half, half), half)
    for k in range(size):
        given = nn(tokens_by_slots(order_ref, k * rows, rows, count), ctx_ref[...])
        outs[k][at] = (pltpu.roll(given[:half], HD, 1) + given[half:]).astype(BF16)


def backward_kernel(size, span, order_ref, wide_ref, mask_ref, slots_ref, turned_ref, *refs):
    g_refs, outs = refs[:size], refs[size : 2 * size]
    mine_ref, other_ref, bias_ref, gctx_ref, grad_ref, tok_ref = refs[2 * size :]
    count = slots_ref.shape[1]
    rows = count // size
    half = rows // 2
    for k in range(size):
        packed = g_refs[k][...].astype(F32)
        gctx_ref[k * rows : k * rows + half] = upper_half(pltpu.roll(packed, HD, 1)).astype(BF16)
        gctx_ref[k * rows + half : (k + 1) * rows] = upper_half(packed).astype(BF16)

    def gather(i, sums):
        start = pl.multiple_of(i * span, span)
        here = pl.ds(start, span)
        grad_ctx = nn(slots_by_tokens(wide_ref, start, span, count), gctx_ref[...]).astype(BF16)
        part = slots_ref[0, here]
        first, second = part[:, :PAIR], part[:, PAIR:]
        probs = softmax_of(first, second, mask_ref[0, here])
        grad_prob = by_cluster(nt, grad_ctx, first)
        inner = jnp.sum(probs * grad_prob, axis=1, keepdims=True)
        grad_scores = (probs * (grad_prob - inner)).astype(BF16)
        grad_query = by_cluster(nn, grad_scores, second) * HD ** (-0.5)
        grad_key = by_cluster(tn, grad_scores, first) * HD ** (-0.5)
        grad_value = by_cluster(tn, probs.astype(BF16), grad_ctx)
        lane = lax.broadcasted_iota(jnp.int32, (span, PAIR), 1)
        grad_qv = jnp.where(lane < HD, grad_query, grad_value).astype(BF16)
        grad_ref[here, :PAIR] = grad_qv
        grad_ref[here, PAIR:] = jnp.where(lane < HD, grad_key, 0.0).astype(BF16)
        return sums + jnp.sum(grad_qv.astype(F32), axis=0, keepdims=True)

    bias_ref[...] = lax.fori_loop(0, count // span, gather, jnp.zeros((1, PAIR), F32))
    for k in range(size):
        given = nn(tokens_by_slots(order_ref, k * rows, rows, count), grad_ref[...])
        low = given.astype(BF16)
        tok_ref[k * rows : (k + 1) * rows] = low
        outs[k][:rows] = low[:, :PAIR]
        outs[k][rows:] = (given[:half, PAIR:] + pltpu.roll(given[half:, PAIR:], HD, 1)).astype(BF16)
    cut = turned_ref.shape[0] // 2
    mine_ref[...] = nn(turned_ref[:cut], tok_ref[...]).astype(BF16)
    other_ref[...] = nn(turned_ref[cut:], tok_ref[...]).astype(BF16)


def row_stats(values_in):
    center = values_in - jnp.mean(values_in, axis=-1, keepdims=True)
    inverse = lax.rsqrt(jnp.mean(center * center, axis=-1, keepdims=True) + EPS)
    return center * inverse, inverse


def norm_back(cotangent, gain, hat, inverse):
    scaled = cotangent * gain
    return inverse * (
        scaled
        - jnp.mean(scaled, axis=-1, keepdims=True)
        - hat * jnp.mean(scaled * hat, axis=-1, keepdims=True)
    )


def column_sum(values_in):
    return jnp.sum(values_in, axis=0, keepdims=True)


def row_copies(ref, layout, blocks, start, lanes, held, sem):
    size, groups, shard = layout
    if groups == 1:
        shard = held.shape[0]

    def rows_of(group, k):
        at = (group * size + blocks[k]) * shard
        return pl.ds(at if isinstance(at, int) else pl.multiple_of(at, shard), shard)

    return [
        pltpu.make_async_copy(
            ref.at[rows_of(group, k), pl.ds(start, lanes)],
            held.at[pl.ds(group * shard, shard), pl.ds(k * lanes, lanes)],
            sem,
        )
        for group in range(groups)
        for k in range(size)
    ]


def all_of(held, sem):
    return pltpu.make_async_copy(held, held, sem)


def layer_kernel(heads, layout, scal_ref, x_ref, og_ref, vec_ref, ff_ref, *refs):
    size = layout[0]
    recv_refs, refs = refs[: 2 * size], refs[2 * size :]
    layer_ref, sum_ref, small_ref, grads_out = refs[:4]
    gctx_refs = refs[4 : 4 + size]
    (
        wup_ref, wdn_ref, wo_ref, act_ref, slope_ref, total_ref, gup_ref, nlow_ref, plow_ref, slow_ref, ctx_ref,
        nturn_ref, pturn_ref, stage_ref, sem, out_sem,
    ) = refs[4 + size :]
    rows, width = x_ref.shape
    hidden = wup_ref.shape[1] // size
    head_lanes = wo_ref.shape[1] // size
    block = 2 * hidden + head_lanes
    rank = scal_ref[0]

    for kind, (start, lanes, held) in enumerate(
        ((2 * hidden, head_lanes, wo_ref), (0, hidden, wup_ref), (hidden, hidden, wdn_ref))
    ):
        for copy in row_copies(ff_ref, layout, range(size), start, lanes, held, sem.at[kind]):
            copy.start()

    half = rows // 2
    lower = lax.broadcasted_iota(jnp.int32, (half, PAIR), 1) < HD

    def piece(k, h):
        if h >= heads:
            return jnp.zeros((half, PAIR), F32)
        if h == heads - 1:
            return recv_refs[size + k][:half].astype(F32)
        return recv_refs[k][h * half : (h + 1) * half].astype(F32)

    for k in range(size):
        for h in range(0, heads, 2):
            first, second = piece(k, h), piece(k, h + 1)
            lanes = slice(k * head_lanes + h * HD, k * head_lanes + h * HD + PAIR)
            ctx_ref[:half, lanes] = jnp.where(lower, first, pltpu.roll(second, HD, 1)).astype(BF16)
            ctx_ref[half:, lanes] = jnp.where(lower, pltpu.roll(first, HD, 1), second).astype(BF16)
    row = lax.broadcasted_iota(jnp.int32, (width, width), 0)
    same = one_hot(row == lax.broadcasted_iota(jnp.int32, (width, width), 1))
    all_of(wo_ref, sem.at[0]).wait()
    summed = x_ref[...].astype(F32) + nt(ctx_ref[...], wo_ref[...]) + vec_ref[0:1]
    hat1, inverse1 = row_stats(summed)
    normed = hat1 * vec_ref[1:2] + vec_ref[2:3]
    nlow_ref[...] = normed.astype(BF16)
    total_ref[...] = normed + vec_ref[3:4]
    curve = (2.0 / 3.141592653589793) ** 0.5
    cut = hidden // PAIR
    biases = []
    for k in range(size):
        parts = recv_refs[k][(heads - 1) * half :].astype(F32)
        bias = parts[:cut] + parts[cut : 2 * cut] + parts[2 * cut : 3 * cut]
        biases.append(jnp.concatenate([bias[i : i + 1] for i in range(cut)], axis=1))
        small_ref[8 + k : 9 + k] = biases[-1]
    all_of(wup_ref, sem.at[1]).wait()
    all_of(wdn_ref, sem.at[2]).wait()

    def span(k):
        return pl.ds(pl.multiple_of(k * hidden, hidden), hidden)

    def forward(k, carry):
        lanes = span(k)
        up = nn(nlow_ref[...], wup_ref[:, lanes]) + small_ref[pl.ds(8 + k, 1)]
        square = up * up
        tanh = jnp.tanh(up * (curve + (0.044715 * curve) * square))
        gate = 0.5 + 0.5 * tanh
        act_ref[:, lanes] = (up * gate).astype(BF16)
        slope_ref[:, lanes] = gate + (0.5 * up) * (1.0 - tanh * tanh) * (curve + (3 * 0.044715 * curve) * square)
        total_ref[...] += nt(act_ref[:, lanes], wdn_ref[:, lanes])
        return carry

    lax.fori_loop(0, size, forward, 0)
    nturn_ref[...] = nt(same, nlow_ref[...]).astype(BF16)
    hat2, inverse2 = row_stats(total_ref[...])
    gain2 = vec_ref[4:5]
    layer_ref[...] = (hat2 * gain2 + vec_ref[5:6]).astype(BF16)
    cot = og_ref[...].astype(F32)
    grad_pre = norm_back(cot, gain2, hat2, inverse2)
    plow_ref[...] = grad_pre.astype(BF16)
    pturn_ref[...] = nt(same, plow_ref[...]).astype(BF16)
    small_ref[3:4] = column_sum(grad_pre)
    small_ref[4:5] = column_sum(cot * hat2)
    small_ref[5:6] = column_sum(cot)
    small_ref[6:8] = jnp.zeros((2, width), F32)
    total_ref[...] = grad_pre

    def leave(k):
        at = pl.multiple_of(k * block, block)
        return pltpu.make_async_copy(stage_ref, grads_out.at[:, pl.ds(at, 2 * hidden)], out_sem.at[0])

    def backward(k, carry):
        lanes = span(k)
        grad_up = (nn(plow_ref[...], wdn_ref[:, lanes]) * slope_ref[:, lanes]).astype(BF16)
        gup_ref[...] = grad_up
        small_ref[pl.ds(8 + lax.rem(rank - k + size, size), 1)] = column_sum(grad_up.astype(F32))
        total_ref[...] += nt(gup_ref[...], wup_ref[:, lanes])

        @pl.when(k > 0)
        def _():
            leave(k - 1).wait()

        stage_ref[:, :hidden] = nn(nturn_ref[...], gup_ref[...]).astype(BF16)
        stage_ref[:, hidden:] = nn(pturn_ref[...], act_ref[:, lanes]).astype(BF16)
        leave(k).start()
        return carry

    lax.fori_loop(0, size, backward, 0)
    grad_normed = total_ref[...]
    small_ref[1:2] = column_sum(grad_normed * hat1)
    small_ref[2:3] = column_sum(grad_normed)
    grad_summed = norm_back(grad_normed, vec_ref[1:2], hat1, inverse1)
    small_ref[0:1] = column_sum(grad_summed)
    sum_ref[...] = grad_summed
    slow_ref[...] = grad_summed.astype(BF16)
    grad_ctx = nn(slow_ref[...], wo_ref[...])
    for k in range(size):
        for h in range(0, heads, 2):
            lanes = slice(k * head_lanes + h * HD, k * head_lanes + h * HD + PAIR)
            top, bottom = grad_ctx[:half, lanes], grad_ctx[half:, lanes]
            gctx_refs[k][h * half : (h + 1) * half] = jnp.where(lower, top, pltpu.roll(bottom, HD, 1)).astype(BF16)
            if h + 1 < heads:
                gctx_refs[k][(h + 1) * half : (h + 2) * half] = jnp.where(
                    lower, pltpu.roll(top, HD, 1), bottom
                ).astype(BF16)
    leave(size - 1).wait()
    nturn_ref[...] = nt(same, slow_ref[...]).astype(BF16)
    leaving = []
    for k in range(size):
        kept = stage_ref.at[:, pl.ds(k * head_lanes, head_lanes)]
        stage_ref[:, k * head_lanes : (k + 1) * head_lanes] = nn(
            nturn_ref[...], ctx_ref[:, k * head_lanes : (k + 1) * head_lanes]
        ).astype(BF16)
        leaving.append(
            pltpu.make_async_copy(kept, grads_out.at[:, pl.ds(k * block + 2 * hidden, head_lanes)], out_sem.at[1 + k])
        )
        leaving[-1].start()
    for copy in leaving:
        copy.wait()


def flip_kernel(pick_ref, left_ref, turned_ref):
    turned_ref[...] = nt(pick_ref[...], left_ref[...]).astype(BF16)


def finish_kernel(head, layout, scal_ref, acc_ref, w_ref, *refs):
    size = layout[0]
    out_ref, held_ref, grads_ref, sem = refs[-4:]
    g_refs = refs[:size]
    rows = acc_ref.shape[0]
    half = rows // 2
    for copy in row_copies(w_ref, layout, range(size), head * WIDE, WIDE, held_ref, sem):
        copy.start()
    lower = lax.broadcasted_iota(jnp.int32, (half, PAIR), 1) < HD
    for k in range(size):
        at = k * WIDE
        grads_ref[:, at : at + PAIR] = g_refs[k][:rows]
        packed = g_refs[k][rows:].astype(F32)
        grads_ref[:half, at + PAIR : at + WIDE] = jnp.where(lower, packed, 0.0).astype(BF16)
        grads_ref[half:, at + PAIR : at + WIDE] = jnp.where(lower, pltpu.roll(packed, HD, 1), 0.0).astype(BF16)
    all_of(held_ref, sem).wait()
    out_ref[...] = acc_ref[...] + nt(grads_ref[...], held_ref[...])


def cost(micros, exps=0):
    return pl.CostEstimate(flops=int(micros * PEAK_PER_MICRO), bytes_accessed=0, transcendentals=int(exps))


def head_spec(shape, head):
    return pl.BlockSpec((1,) + shape, lambda i: (head,) + (0,) * len(shape))


def full(shape):
    return pl.BlockSpec(tuple(shape), lambda i: (0,) * len(shape))


def held():
    return pl.BlockSpec(memory_space=pl.ANY)


def scalars_spec():
    return pl.BlockSpec(memory_space=pltpu.SMEM)


def shape_of(shape, dtype=BF16):
    return jax.ShapeDtypeStruct(tuple(shape), dtype)


def call(kernel, name, in_specs, out_specs, out_shape, scratch, estimate, mib, grid=(1,), after=()):
    count = len(in_specs)

    def body(*refs):
        kernel(*refs[:count], *refs[count + len(after) :])

    run = pl.pallas_call(
        body,
        grid=grid,
        in_specs=list(in_specs) + [held()] * len(after),
        out_specs=out_specs,
        out_shape=out_shape,
        scratch_shapes=scratch,
        compiler_params=pltpu.CompilerParams(vmem_limit_bytes=mib * 1024 * 1024),
        name=name,
        cost_estimate=estimate,
    )
    return lambda *args: run(*args, *after)


def prepare(query, key, value, out, up, down_t, heads):
    shard, hidden = up.shape
    lanes = 2 * hidden + -(-out.shape[0] // CL) * CL
    args = (query, key, value, out, up, down_t)
    shapes = [shape_of((shard, heads * WIDE)), shape_of((shard, lanes))]
    return call(
        prepare_kernel, "prepare", [full(a.shape) for a in args], [full(s.shape) for s in shapes], shapes, [],
        cost(1), 60,
    )(*args)


def unmix(grads, local_width):
    shard = grads.shape[0]
    shapes = [shape_of((shard, local_width), F32)] * 3
    return call(
        unmix_kernel, "unmix", [full(grads.shape)], [full(s.shape) for s in shapes], shapes, [],
        cost(1), 16,
    )(grads)


def slot_tokens(seqs, scalars, clusters, balance):
    heads, count = clusters.shape[0], clusters.shape[2]
    row = pl.BlockSpec((1, 1, count), lambda h: (h, 0, 0))
    wide = pl.BlockSpec((1, count, CL), lambda h: (h, 0, 0))
    return call(
        functools.partial(order_kernel, seqs), "slot_tokens",
        [scalars_spec(), row, full(balance.shape)], [row, wide, wide],
        [shape_of((heads, 1, count), F32), shape_of((heads, count, CL), F32), shape_of((heads, count, CL))],
        [pltpu.VMEM((8, count), BF16)],
        cost(10), 16, grid=(heads,),
    )(scalars, clusters, balance)


def project(size, heads, step, scalars, weights, biases, pieces, held_before):
    rows, width = pieces[0].shape
    shapes = [shape_of((size * rows, width)), shape_of((heads, size * rows, WIDE))]
    first = 3 + len(pieces)
    return pl.pallas_call(
        functools.partial(project_kernel, size, heads, step),
        grid=(1,),
        in_specs=[scalars_spec(), full(weights.shape), full(biases.shape)]
        + [held()] * (len(pieces) + len(held_before)),
        out_specs=[held()] * 2,
        out_shape=shapes,
        scratch_shapes=[
            pltpu.VMEM((rows, width), BF16),
            pltpu.VMEM((heads, rows, WIDE), BF16),
            pltpu.SemaphoreType.DMA(()),
            pltpu.SemaphoreType.DMA((heads + 1,)),
        ],
        input_output_aliases={first: 0, first + 1: 1} if step else {},
        compiler_params=pltpu.CompilerParams(vmem_limit_bytes=24 * 1024 * 1024),
        name="project",
        cost_estimate=cost(2),
    )(scalars, weights, biases, *pieces, *held_before)


def attend(size, first, heads, order, wide, mask, qkv, extra, after):
    count = qkv.shape[1]
    half = count // size // 2
    row = pl.BlockSpec((1, 1, count), lambda h: (h + first, 0, 0))
    block = pl.BlockSpec((1, count, WIDE), lambda h: (h + first, 0, 0))
    column = pl.BlockSpec((1, count, CL), lambda h: (h + first, 0, 0))
    shapes = [shape_of((heads, count, WIDE))] + [shape_of((heads * half + extra.shape[0], PAIR))] * size
    return call(
        functools.partial(forward_kernel, size, heads, count // 2), "attend",
        [row, column, column, block, full(extra.shape)],
        [pl.BlockSpec((1, count, WIDE), lambda h: (h, 0, 0))] + [full(s.shape) for s in shapes[1:]], shapes,
        [pltpu.VMEM((count, PAIR), BF16)],
        cost(6.5 * heads), 60, grid=(heads,), after=after,
    )(order, wide, mask, qkv, extra)


def attend_back(size, head, order, wide, mask, slots, place, turned_x, grad_context, after):
    count = slots.shape[1]
    rows = count // size
    cut = turned_x.shape[0] // 2
    shapes = (
        [shape_of((rows + rows // 2, PAIR))] * size + [shape_of((cut, WIDE))] * 2 + [shape_of((1, PAIR), F32)]
    )
    return call(
        functools.partial(backward_kernel, size, count // 2), "attend_back",
        [head_spec((1, count), head), head_spec((count, CL), head), head_spec((count, CL), head)]
        + [head_spec((count, WIDE), place), full(turned_x.shape)]
        + [pl.BlockSpec((rows // 2, PAIR), lambda i: (head, 0))] * size,
        [full(s.shape) for s in shapes], shapes,
        [pltpu.VMEM((count, PAIR), BF16), pltpu.VMEM((count, WIDE), BF16), pltpu.VMEM((count, WIDE), BF16)],
        cost(3), 40, after=after,
    )(order, wide, mask, slots, turned_x, *grad_context)


def layer(heads, layout, hidden, scalars, inputs, out_grad, vectors, received, ff):
    size = layout[0]
    rows, width = inputs.shape
    block = ff.shape[1]
    head_lanes = block - 2 * hidden
    shapes = [
        shape_of((rows, width)),
        shape_of((rows, width), F32),
        shape_of((8 + size, width), F32),
        shape_of((width, size * block)),
    ] + [shape_of((heads * (rows // 2), PAIR))] * size
    args = (inputs, out_grad, vectors)

    def kept(shape, dtype=BF16):
        return pltpu.VMEM(shape, dtype)

    return call(
        functools.partial(layer_kernel, heads, layout), "layer",
        [scalars_spec()] + [full(a.shape) for a in args] + [held()] + [full(r.shape) for r in received],
        [full(s.shape) if i != 3 else held() for i, s in enumerate(shapes)], shapes,
        [
            kept((width, size * hidden)),
            kept((width, size * hidden)),
            kept((width, size * head_lanes)),
            kept((rows, size * hidden)),
            kept((rows, size * hidden), F32),
            kept((rows, width), F32),
            kept((rows, hidden)),
            kept((rows, width)),
            kept((rows, width)),
            kept((rows, width)),
            kept((rows, size * head_lanes)),
            kept((width, rows)),
            kept((width, rows)),
            kept((width, 2 * hidden)),
            pltpu.SemaphoreType.DMA((3,)),
            pltpu.SemaphoreType.DMA((1 + size,)),
        ],
        cost(33), 58,
    )(scalars, *args, ff, *received)


def flip(size, pick, left):
    count, width = left.shape
    rows = count // size
    return call(
        flip_kernel, "flip",
        [full(pick.shape), pl.BlockSpec((rows, width), lambda i: (i, 0))],
        pl.BlockSpec((width, rows), lambda i: (0, i)), shape_of((width, count)), [],
        cost(0.05), 16, grid=(size,),
    )(pick, left)


def finish(head, layout, scalars, total, weights, grads, after):
    size = layout[0]
    rows, width = total.shape
    return call(
        functools.partial(finish_kernel, head, layout), "finish",
        [scalars_spec(), full(total.shape), held()] + [full(g.shape) for g in grads],
        full(total.shape), shape_of(total.shape, F32),
        [
            pltpu.VMEM((width, size * WIDE), BF16),
            pltpu.VMEM((rows, size * WIDE), BF16),
            pltpu.SemaphoreType.DMA(()),
        ],
        cost(1), 24, after=after,
    )(scalars, total, weights, *grads)


def shift(values, size, k):
    return lax.ppermute(values, "tensor", [(i, (i + k) % size) for i in range(size)])


def exchange(parts, size):
    return [parts[0]] + [shift(parts[size - k], size, k) for k in range(1, size)]


def line_step(up, down, k, size):
    return (
        lax.ppermute(up, "tensor", [(i, i + 1) for i in range(k - 1, size - 1)]),
        lax.ppermute(down, "tensor", [(i + 1, i) for i in range(0, size - k)]),
    )


def gather_line(own, size):
    ups, downs = [own], [own]
    for k in range(1, size):
        up, down = line_step(ups[-1], downs[-1], k, size)
        ups.append(up)
        downs.append(down)
    return ups[1:], downs[1:]


def swap(values, axis, bit):
    return lax.ppermute(values, axis, [(i, i ^ bit) for i in range(lax.axis_size(axis))])


def bits_of(size):
    return [1 << b for b in range(size.bit_length() - 1)]


def add_low(left, right):
    return (left.astype(F32) + right.astype(F32)).astype(BF16)


def halves(mine, arrived):
    cut = mine.shape[0] // 2
    return add_low(mine[:cut], arrived[:cut]), add_low(mine[cut:], arrived[cut:])


def total_of(parts):
    result = parts[0].astype(F32)
    for part in parts[1:]:
        result = result + part.astype(F32)
    return result


def tie(*groups):
    return lax.optimization_barrier(groups)


def local(
    inputs, out_grad, seq_lengths, balance, clusters, query_weight, query_bias, key_weight,
    value_weight, value_bias, out_weight, out_bias, norm1_gain, norm1_bias, up_weight, up_bias,
    down_weight, down_bias, norm2_gain, norm2_bias,
):
    dp = ("chip", "core")
    rows, width = inputs.shape
    size = lax.axis_size("tensor")
    chips = lax.axis_size("chip")
    rank, chip, core = (lax.axis_index(axis) for axis in ("tensor", "chip", "core"))
    shard = query_weight.shape[0]
    local_width = query_weight.shape[1]
    heads = clusters.shape[1]
    seqs = seq_lengths.shape[1]
    bits = bits_of(chips)

    bounds = jnp.cumsum(seq_lengths[0])
    scalars = jnp.concatenate([jnp.stack([rank, core, jnp.int32(rows)]), bounds]).astype(jnp.int32)
    direct = shard % 16 == 0
    layout = (size, 2 * chips if direct else 1, shard)
    hidden = up_weight.shape[1]

    def whole(near):
        rows_in = lax.all_gather(near, dp, axis=0, tiled=True)
        if direct:
            return rows_in
        lanes = near.shape[1]
        return rows_in.reshape(2 * chips, size, shard, lanes).transpose(1, 0, 2, 3).reshape(size * width, lanes)

    head_weights, ff_own = prepare(
        query_weight, key_weight, value_weight, out_weight, up_weight, down_weight.T, heads
    )
    ups, downs = gather_line(inputs, size)
    ff_ups, ff_downs = [ff_own], [ff_own]
    for k in range(1, size):
        if k == size - 1:
            ff_ups[-1], ff_downs[-1], ups[0], downs[0] = tie(ff_ups[-1], ff_downs[-1], ups[0], downs[0])
        one_up, one_down = line_step(ff_ups[-1], ff_downs[-1], k, size)
        ff_ups.append(one_up)
        ff_downs.append(one_down)
    near = jnp.concatenate(
        [ff_own] + [jnp.where(rank >= k, ff_ups[k], ff_downs[size - k]) for k in range(1, size)], axis=0
    )
    own_qkv = lax.all_gather(head_weights, dp, axis=0, tiled=True)
    near, own_qkv = tie(near, own_qkv)
    ff = whole(near)
    blank = jnp.zeros((heads, HD), F32)
    head_biases = jnp.concatenate(
        [query_bias.reshape(heads, HD), value_bias.reshape(heads, HD), blank, blank], axis=-1
    ).reshape(1, heads * WIDE)
    terms, rest = [], up_bias
    for _ in range(3):
        term = lax.reduce_precision(rest, 8, 7)
        terms.append(term.astype(BF16))
        rest = rest - term
    extra = jnp.concatenate(terms).reshape(-1, PAIR)
    extra = jnp.pad(extra, ((0, -extra.shape[0] % 16), (0, 0)))
    vectors = jnp.stack([out_bias, norm1_gain, norm1_bias, down_bias, norm2_gain, norm2_bias])

    def row_pick(order_bits):
        place = jnp.arange(width, dtype=jnp.int32)
        block = place // shard
        away = jnp.zeros_like(block)
        for depth, bit in enumerate(order_bits):
            away = away + ((block >> (len(order_bits) - 1 - depth)) & 1) * bit
        near = chip ^ away
        owner = near * 2 + (core ^ (block // chips))
        return one_hot((owner * shard + place % shard)[:, None] == place[None, :])

    pick = row_pick(bits)
    order, wide, mask = slot_tokens(seqs, scalars, clusters[0][:, None, :], balance)
    whole_rows = []
    for step in range(size):
        pieces = [ups[step - 1], downs[step - 1]] if step else [inputs]
        whole_rows = project(size, heads, step, scalars, own_qkv, head_biases, pieces, whole_rows)
    x_all, qkv = whole_rows
    later_weights, qkv = tie(head_weights, qkv)
    later_near = jnp.concatenate([later_weights] + [shift(later_weights, size, k) for k in range(1, size)], axis=0)

    kept_a, *context_a = attend(size, 0, heads - 1, order, wide, mask, qkv, extra, [])
    context_a, later_near = tie(context_a, later_near)
    later = whole(later_near)
    received = exchange(context_a, size)
    kept_b, *context_b = attend(size, heads - 1, 1, order, wide, mask, qkv, extra[:16], [context_a[0]])
    received, context_b = tie(received, context_b)
    received = received + exchange(context_b, size)
    slots = [(kept_a, h) for h in range(heads - 1)] + [(kept_b, 0)]
    turned_x = flip(size, pick, x_all)
    layer_out, grad_summed, small, grads, *grad_ctx = layer(
        heads, layout, hidden, scalars, inputs, out_grad, vectors, received, ff
    )
    arrived = exchange(grad_ctx, size)
    grads, later = tie(grads, later)
    grads = lax.psum_scatter(grads, dp, scatter_dimension=0, tiled=True)

    backs, head_mine, head_other, bias_sums = [], [], [], []
    for h in range(heads):
        after = backs[h - 2][1:] if h >= 2 else []
        outs = attend_back(size, h, order, wide, mask, *slots[h], turned_x, arrived, after)
        backs.append(exchange(outs[:size], size))
        head_mine.append(outs[size])
        head_other.append(outs[size + 1])
        bias_sums.append(outs[size + 2])
        if h < len(bits_of(size)):
            small = small + swap(small, "tensor", bits_of(size)[h])
            arrived, small = tie(arrived, small)
    backs[heads - 2], head_other = tie(backs[heads - 2], head_other)
    mine = jnp.concatenate(head_mine, axis=1)
    far = swap(jnp.concatenate(head_other, axis=1), "core", 1)
    sums = jnp.concatenate([small, jnp.pad(jnp.concatenate(bias_sums, axis=0), ((0, 0), (0, width - PAIR)))], axis=0)
    sums = sums + swap(sums, "core", 1)
    grad_inputs = grad_summed
    for h in range(heads - 1):
        grad_inputs = finish(h, layout, scalars, grad_inputs, later, backs[h], [])
    for bit in bits:
        mine, sent = halves(mine, far)
        far = swap(sent, "chip", bit)
        sums = sums + swap(sums, "chip", bit)
    head_sum = add_low(mine, far)
    bias = sums[small.shape[0] :]
    grad_query_bias = bias[:, :HD].reshape(local_width)
    grad_value_bias = bias[:, HD:PAIR].reshape(local_width)
    grad_up_bias = lax.dynamic_index_in_dim(sums, 8 + rank, 0, keepdims=False)
    lanes = grads.shape[1] // size
    parts = [grads[:, k * lanes : (k + 1) * lanes] for k in range(size)]
    parts, grad_inputs, back_last, head_sum = tie(parts, grad_inputs, backs[heads - 1], head_sum)
    backs[heads - 1] = back_last
    moved = exchange(parts, size)
    grad_query_weight, grad_key_weight, grad_value_weight = unmix(head_sum, local_width)
    grads = total_of(moved)
    grad_inputs = finish(heads - 1, layout, scalars, grad_inputs, later, backs[heads - 1], [])
    grad_up_weight = grads[:, :hidden]
    grad_down_weight = grads[:, hidden : 2 * hidden].T
    grad_out_weight = grads[:, 2 * hidden : 2 * hidden + local_width].T
    return (
        layer_out, grad_inputs, grad_query_weight, grad_query_bias, grad_key_weight, grad_value_weight,
        grad_value_bias, grad_out_weight, sums[0], sums[1], sums[2], grad_up_weight, grad_up_bias,
        grad_down_weight, sums[3], sums[4], sums[5],
    )


def solution(mesh):
    devices = mesh.devices
    split = Mesh(devices.reshape(devices.shape[0] // 2, 2, devices.shape[1]), ("chip", "core", "tensor"))
    dp = ("chip", "core")
    rows, weight, turned_weight, vector, same = (
        P(dp + ("tensor",), None),
        P(dp, "tensor"),
        P("tensor", dp),
        P("tensor"),
        P(),
    )
    in_specs = (
        rows, rows, P(dp, None), P(dp, None), P(dp, "tensor", None), weight, vector, weight, weight,
        vector, turned_weight, same, same, same, weight, vector, turned_weight, same, same, same,
    )
    out_specs = (
        rows, rows, weight, vector, weight, weight, vector, turned_weight, same, same, same, weight, vector,
        turned_weight, same, same, same,
    )
    return jax.shard_map(local, mesh=split, in_specs=in_specs, out_specs=out_specs, check_vma=False)
```

```python
import functools

import jax
import jax.numpy as jnp
from jax import lax
from jax.experimental import pallas as pl
from jax.experimental.pallas import tpu as pltpu
from jax.sharding import Mesh, PartitionSpec as P

HD = 64
CL = 128
PAIR = 2 * HD
WIDE = 4 * HD
F32 = jnp.float32
BF16 = jnp.bfloat16
EPS = 1e-06
PEAK_PER_MICRO = 1.15e9


def nn(left, right):
    return jnp.dot(left, right, preferred_element_type=F32)


def nt(left, right):
    return lax.dot_general(left, right, (((1,), (1,)), ((), ())), preferred_element_type=F32)


def tn(left, right):
    return lax.dot_general(left, right, (((0,), (0,)), ((), ())), preferred_element_type=F32)


def one_hot(hits):
    return jnp.where(hits, 1.0, 0.0).astype(BF16)


def head_lane(shape, dim, part):
    lane = lax.broadcasted_iota(jnp.int32, shape, dim)
    column = (lane // WIDE) * HD + lane % HD
    return jnp.where((lane % WIDE) // HD == part, column, -1)


def prepare_kernel(q_ref, k_ref, v_ref, o_ref, up_ref, dn_ref, heads_ref, ff_ref):
    shape = (q_ref.shape[1], heads_ref.shape[1])
    column = lax.broadcasted_iota(jnp.int32, shape, 0)
    total = jnp.zeros(heads_ref.shape, F32)
    for part, ref in ((0, q_ref), (1, v_ref), (2, k_ref)):
        total = total + nn(ref[...], one_hot(head_lane(shape, 1, part) == column))
    heads_ref[...] = total.astype(BF16)
    hidden = up_ref.shape[1]
    ff_ref[:, :hidden] = up_ref[...]
    ff_ref[:, hidden : 2 * hidden] = dn_ref[...]
    shape = (ff_ref.shape[1] - 2 * hidden, o_ref.shape[0])
    spread = one_hot(lax.broadcasted_iota(jnp.int32, shape, 0) == lax.broadcasted_iota(jnp.int32, shape, 1))
    padded = nn(spread, o_ref[...]).astype(BF16)
    rows = o_ref.shape[1]
    same = lax.broadcasted_iota(jnp.int32, (rows, rows), 0) == lax.broadcasted_iota(jnp.int32, (rows, rows), 1)
    ff_ref[:, 2 * hidden :] = nt(one_hot(same), padded).astype(BF16)


def unmix_kernel(grads_ref, q_ref, k_ref, v_ref):
    shape = (q_ref.shape[1], grads_ref.shape[1])
    column = lax.broadcasted_iota(jnp.int32, shape, 0)
    for part, ref in ((0, q_ref), (1, v_ref), (2, k_ref)):
        ref[...] = nt(grads_ref[...], one_hot(head_lane(shape, 1, part) == column))


def column_of(row):
    return jnp.transpose(jnp.broadcast_to(row, (CL, CL)))


def order_kernel(seqs, scal_ref, clusters_ref, balance_ref, order_ref, wide_ref, mask_ref, table_ref):
    count = balance_ref.shape[1]
    step = 2 * CL
    rows = scal_ref[2]
    balance = balance_ref[...]
    high = balance // HD
    low = balance - high * HD
    pick = lax.broadcasted_iota(jnp.int32, (8, count), 0)
    table = jnp.where(pick == 0, high, jnp.where(pick == 1, low, 0)).astype(F32).astype(BF16)
    chosen = clusters_ref[0]
    table_ref[...] = table

    def pick_block(i, total):
        start = pl.multiple_of(i * step, step)
        place = lax.broadcasted_iota(jnp.int32, (step, count), 0) + start
        return total + nn(table_ref[:, pl.ds(start, step)], one_hot(place == chosen))

    total = lax.fori_loop(0, count // step, pick_block, jnp.zeros((8, count), F32))
    token = (total[0:1] * float(HD) + total[1:2]).astype(jnp.int32)
    segment = jnp.zeros_like(token)
    for s in range(seqs):
        segment = segment + jnp.where(token >= scal_ref[3 + s], 1, 0)
    segment = segment.astype(F32)
    from_own = scal_ref[0] * rows - (token // rows) * rows
    from_own = jnp.where(from_own < 0, from_own + count, from_own)
    order = (from_own + token % rows).astype(F32)
    order_ref[0] = order
    for at in range(0, count, CL):
        wide_ref[0, at : at + CL] = column_of(order[:, at : at + CL])
        row = segment[:, at : at + CL]
        mask_ref[0, at : at + CL] = jnp.where(column_of(row) == row, 0.0, -1e30).astype(BF16)


def slots_by_tokens(wide_ref, start, span, count):
    lane = lax.broadcasted_iota(jnp.int32, (span, CL), 1).astype(F32)
    gap = wide_ref[0, pl.ds(start, span)] - lane
    return jnp.concatenate([one_hot(gap == float(j)) for j in range(0, count, CL)], axis=1)


def tokens_by_slots(order_ref, start, span, count):
    row = order_ref[0] - jnp.asarray(start).astype(F32)
    return one_hot(lax.broadcasted_iota(jnp.int32, (span, count), 0).astype(F32) == row)


def by_cluster(product, left, right):
    return jnp.concatenate(
        [product(left[at : at + CL], right[at : at + CL]) for at in range(0, left.shape[0], CL)], axis=0
    )


def softmax_of(first, second, mask):
    scores = by_cluster(nt, first, second) * HD ** (-0.5) + mask.astype(F32)
    raised = jnp.exp(scores - jnp.max(scores, axis=1, keepdims=True))
    return raised * (1.0 / jnp.sum(raised, axis=1, keepdims=True))


def upper_half(values):
    lane = lax.broadcasted_iota(jnp.int32, values.shape, 1)
    return jnp.where(lane >= HD, values, 0.0)


def project_kernel(size, heads, step, scal_ref, w_ref, b_ref, *refs):
    pieces = refs[: 1 if step == 0 else 2]
    x_out, qkv_out, x_ref, qkv_ref, sem, out_sem = refs[-6:]
    rows = x_ref.shape[0]
    rank = scal_ref[0]

    def block(piece, k):
        incoming = pltpu.make_async_copy(piece, x_ref, sem)
        incoming.start()
        incoming.wait()
        place = pl.ds(k * rows, rows)
        leaving = [pltpu.make_async_copy(x_ref, x_out.at[place], out_sem.at[heads])]
        leaving[0].start()
        for h in range(heads):
            lanes = slice(h * WIDE, (h + 1) * WIDE)
            qkv_ref[h] = (nn(x_ref[...], w_ref[:, lanes]) + b_ref[:, lanes]).astype(BF16)
            leaving.append(pltpu.make_async_copy(qkv_ref.at[h], qkv_out.at[h, place], out_sem.at[h]))
            leaving[-1].start()
        for copy in leaving:
            copy.wait()

    if step == 0:
        block(pieces[0], 0)
        return

    @pl.when(rank >= step)
    def _():
        block(pieces[0], step)

    @pl.when(rank < size - step)
    def _():
        block(pieces[1], size - step)


def forward_kernel(size, heads, span, order_ref, wide_ref, mask_ref, qkv_ref, extra_ref, slots_ref, *refs):
    outs, ctx_ref = refs[:size], refs[size]
    head = pl.program_id(0)
    count = qkv_ref.shape[1]
    rows = count // size
    half = rows // 2
    for k in range(size):
        outs[k][heads * half :] = extra_ref[...]

    def gather(i, carry):
        start = pl.multiple_of(i * span, span)
        here = pl.ds(start, span)
        picked = nn(slots_by_tokens(wide_ref, start, span, count), qkv_ref[0]).astype(BF16)
        slots_ref[0, here] = picked
        first = picked[:, :PAIR]
        probs = softmax_of(first, picked[:, PAIR:], mask_ref[0, here])
        ctx_ref[here] = upper_half(by_cluster(nn, probs.astype(BF16), first)).astype(BF16)
        return carry

    lax.fori_loop(0, count // span, gather, 0)
    at = pl.ds(pl.multiple_of(head * half, half), half)
    for k in range(size):
        given = nn(tokens_by_slots(order_ref, k * rows, rows, count), ctx_ref[...])
        outs[k][at] = (pltpu.roll(given[:half], HD, 1) + given[half:]).astype(BF16)


def backward_kernel(size, span, order_ref, wide_ref, mask_ref, slots_ref, turned_ref, *refs):
    g_refs, outs = refs[:size], refs[size : 2 * size]
    mine_ref, other_ref, bias_ref, gctx_ref, grad_ref, tok_ref, pack_ref, sem = refs[2 * size :]
    count = slots_ref.shape[1]
    rows = count // size
    half = rows // 2
    for k in range(size):
        packed = g_refs[k][...].astype(F32)
        gctx_ref[k * rows : k * rows + half] = upper_half(pltpu.roll(packed, HD, 1)).astype(BF16)
        gctx_ref[k * rows + half : (k + 1) * rows] = upper_half(packed).astype(BF16)

    def gather(i, sums):
        start = pl.multiple_of(i * span, span)
        here = pl.ds(start, span)
        grad_ctx = nn(slots_by_tokens(wide_ref, start, span, count), gctx_ref[...]).astype(BF16)
        part = slots_ref[0, here]
        first, second = part[:, :PAIR], part[:, PAIR:]
        probs = softmax_of(first, second, mask_ref[0, here])
        grad_prob = by_cluster(nt, grad_ctx, first)
        inner = jnp.sum(probs * grad_prob, axis=1, keepdims=True)
        grad_scores = (probs * (grad_prob - inner)).astype(BF16)
        grad_query = by_cluster(nn, grad_scores, second) * HD ** (-0.5)
        grad_key = by_cluster(tn, grad_scores, first) * HD ** (-0.5)
        grad_value = by_cluster(tn, probs.astype(BF16), grad_ctx)
        lane = lax.broadcasted_iota(jnp.int32, (span, PAIR), 1)
        grad_qv = jnp.where(lane < HD, grad_query, grad_value).astype(BF16)
        grad_ref[here, :PAIR] = grad_qv
        grad_ref[here, PAIR:] = jnp.where(lane < HD, grad_key, 0.0).astype(BF16)
        return sums + jnp.sum(grad_qv.astype(F32), axis=0, keepdims=True)

    bias_ref[...] = lax.fori_loop(0, count // span, gather, jnp.zeros((1, PAIR), F32))
    block = rows + half

    def give(k, carry):
        given = nn(tokens_by_slots(order_ref, k * rows, rows, count), grad_ref[...])
        low = given.astype(BF16)
        tok_ref[pl.ds(pl.multiple_of(k * rows, rows), rows)] = low
        at = pl.multiple_of(k * block, half)
        pack_ref[pl.ds(at, rows)] = low[:, :PAIR]
        pack_ref[pl.ds(at + rows, half)] = (given[:half, PAIR:] + pltpu.roll(given[half:, PAIR:], HD, 1)).astype(BF16)
        return carry

    lax.fori_loop(0, size, give, 0)
    leaving = [
        pltpu.make_async_copy(pack_ref.at[pl.ds(k * block, block)], outs[k], sem.at[k]) for k in range(size)
    ]
    for copy in leaving:
        copy.start()
    cut = turned_ref.shape[0] // 2
    mine_ref[...] = nn(turned_ref[:cut], tok_ref[...]).astype(BF16)
    other_ref[...] = nn(turned_ref[cut:], tok_ref[...]).astype(BF16)
    for copy in leaving:
        copy.wait()


def row_stats(values_in):
    center = values_in - jnp.mean(values_in, axis=-1, keepdims=True)
    inverse = lax.rsqrt(jnp.mean(center * center, axis=-1, keepdims=True) + EPS)
    return center * inverse, inverse


def norm_back(cotangent, gain, hat, inverse):
    scaled = cotangent * gain
    return inverse * (
        scaled
        - jnp.mean(scaled, axis=-1, keepdims=True)
        - hat * jnp.mean(scaled * hat, axis=-1, keepdims=True)
    )


def column_sum(values_in):
    return jnp.sum(values_in, axis=0, keepdims=True)


def row_copies(ref, layout, blocks, start, lanes, held, sem):
    size, groups, shard = layout
    if groups == 1:
        shard = held.shape[0]

    def rows_of(group, k):
        at = (group * size + blocks[k]) * shard
        return pl.ds(at if isinstance(at, int) else pl.multiple_of(at, shard), shard)

    return [
        pltpu.make_async_copy(
            ref.at[rows_of(group, k), pl.ds(start, lanes)],
            held.at[pl.ds(group * shard, shard), pl.ds(k * lanes, lanes)],
            sem,
        )
        for group in range(groups)
        for k in range(size)
    ]


def all_of(held, sem):
    return pltpu.make_async_copy(held, held, sem)


def layer_kernel(heads, layout, scal_ref, x_ref, og_ref, vec_ref, ff_ref, *refs):
    size = layout[0]
    recv_refs, refs = refs[: 2 * size], refs[2 * size :]
    layer_ref, sum_ref, small_ref, grads_out = refs[:4]
    gctx_refs = refs[4 : 4 + size]
    (
        wup_ref, wdn_ref, wo_ref, act_ref, slope_ref, total_ref, gup_ref, nlow_ref, plow_ref, slow_ref, ctx_ref,
        nturn_ref, pturn_ref, stage_ref, sem, out_sem,
    ) = refs[4 + size :]
    rows, width = x_ref.shape
    hidden = wup_ref.shape[1] // size
    head_lanes = wo_ref.shape[1] // size
    block = 2 * hidden + head_lanes
    rank = scal_ref[0]

    for kind, (start, lanes, held) in enumerate(
        ((2 * hidden, head_lanes, wo_ref), (0, hidden, wup_ref), (hidden, hidden, wdn_ref))
    ):
        for copy in row_copies(ff_ref, layout, range(size), start, lanes, held, sem.at[kind]):
            copy.start()

    half = rows // 2
    lower = lax.broadcasted_iota(jnp.int32, (half, PAIR), 1) < HD

    def piece(k, h):
        if h >= heads:
            return jnp.zeros((half, PAIR), F32)
        if h == heads - 1:
            return recv_refs[size + k][:half].astype(F32)
        return recv_refs[k][h * half : (h + 1) * half].astype(F32)

    for k in range(size):
        for h in range(0, heads, 2):
            first, second = piece(k, h), piece(k, h + 1)
            lanes = slice(k * head_lanes + h * HD, k * head_lanes + h * HD + PAIR)
            ctx_ref[:half, lanes] = jnp.where(lower, first, pltpu.roll(second, HD, 1)).astype(BF16)
            ctx_ref[half:, lanes] = jnp.where(lower, pltpu.roll(first, HD, 1), second).astype(BF16)
    row = lax.broadcasted_iota(jnp.int32, (width, width), 0)
    same = one_hot(row == lax.broadcasted_iota(jnp.int32, (width, width), 1))
    all_of(wo_ref, sem.at[0]).wait()
    summed = x_ref[...].astype(F32) + nt(ctx_ref[...], wo_ref[...]) + vec_ref[0:1]
    hat1, inverse1 = row_stats(summed)
    normed = hat1 * vec_ref[1:2] + vec_ref[2:3]
    nlow_ref[...] = normed.astype(BF16)
    total_ref[...] = normed + vec_ref[3:4]
    curve = (2.0 / 3.141592653589793) ** 0.5
    cut = hidden // PAIR
    biases = []
    for k in range(size):
        parts = recv_refs[k][(heads - 1) * half :].astype(F32)
        bias = parts[:cut] + parts[cut : 2 * cut] + parts[2 * cut : 3 * cut]
        biases.append(jnp.concatenate([bias[i : i + 1] for i in range(cut)], axis=1))
        small_ref[8 + k : 9 + k] = biases[-1]
    all_of(wup_ref, sem.at[1]).wait()
    all_of(wdn_ref, sem.at[2]).wait()

    def span(k):
        return pl.ds(pl.multiple_of(k * hidden, hidden), hidden)

    def forward(k, carry):
        lanes = span(k)
        up = nn(nlow_ref[...], wup_ref[:, lanes]) + small_ref[pl.ds(8 + k, 1)]
        square = up * up
        tanh = jnp.tanh(up * (curve + (0.044715 * curve) * square))
        gate = 0.5 + 0.5 * tanh
        act_ref[:, lanes] = (up * gate).astype(BF16)
        slope_ref[:, lanes] = gate + (0.5 * up) * (1.0 - tanh * tanh) * (curve + (3 * 0.044715 * curve) * square)
        total_ref[...] += nt(act_ref[:, lanes], wdn_ref[:, lanes])
        return carry

    lax.fori_loop(0, size, forward, 0)
    nturn_ref[...] = nt(same, nlow_ref[...]).astype(BF16)
    hat2, inverse2 = row_stats(total_ref[...])
    gain2 = vec_ref[4:5]
    layer_ref[...] = (hat2 * gain2 + vec_ref[5:6]).astype(BF16)
    cot = og_ref[...].astype(F32)
    grad_pre = norm_back(cot, gain2, hat2, inverse2)
    plow_ref[...] = grad_pre.astype(BF16)
    pturn_ref[...] = nt(same, plow_ref[...]).astype(BF16)
    small_ref[3:4] = column_sum(grad_pre)
    small_ref[4:5] = column_sum(cot * hat2)
    small_ref[5:6] = column_sum(cot)
    small_ref[6:8] = jnp.zeros((2, width), F32)
    total_ref[...] = grad_pre

    def leave(k):
        at = pl.multiple_of(k * block, block)
        return pltpu.make_async_copy(stage_ref, grads_out.at[:, pl.ds(at, 2 * hidden)], out_sem.at[0])

    def backward(k, carry):
        lanes = span(k)
        grad_up = (nn(plow_ref[...], wdn_ref[:, lanes]) * slope_ref[:, lanes]).astype(BF16)
        gup_ref[...] = grad_up
        small_ref[pl.ds(8 + lax.rem(rank - k + size, size), 1)] = column_sum(grad_up.astype(F32))
        total_ref[...] += nt(gup_ref[...], wup_ref[:, lanes])

        @pl.when(k > 0)
        def _():
            leave(k - 1).wait()

        stage_ref[:, :hidden] = nn(nturn_ref[...], gup_ref[...]).astype(BF16)
        stage_ref[:, hidden:] = nn(pturn_ref[...], act_ref[:, lanes]).astype(BF16)
        leave(k).start()
        return carry

    lax.fori_loop(0, size, backward, 0)
    grad_normed = total_ref[...]
    small_ref[1:2] = column_sum(grad_normed * hat1)
    small_ref[2:3] = column_sum(grad_normed)
    grad_summed = norm_back(grad_normed, vec_ref[1:2], hat1, inverse1)
    small_ref[0:1] = column_sum(grad_summed)
    sum_ref[...] = grad_summed
    slow_ref[...] = grad_summed.astype(BF16)
    grad_ctx = nn(slow_ref[...], wo_ref[...])
    for k in range(size):
        for h in range(0, heads, 2):
            lanes = slice(k * head_lanes + h * HD, k * head_lanes + h * HD + PAIR)
            top, bottom = grad_ctx[:half, lanes], grad_ctx[half:, lanes]
            gctx_refs[k][h * half : (h + 1) * half] = jnp.where(lower, top, pltpu.roll(bottom, HD, 1)).astype(BF16)
            if h + 1 < heads:
                gctx_refs[k][(h + 1) * half : (h + 2) * half] = jnp.where(
                    lower, pltpu.roll(top, HD, 1), bottom
                ).astype(BF16)
    leave(size - 1).wait()
    nturn_ref[...] = nt(same, slow_ref[...]).astype(BF16)
    leaving = []
    for k in range(size):
        kept = stage_ref.at[:, pl.ds(k * head_lanes, head_lanes)]
        stage_ref[:, k * head_lanes : (k + 1) * head_lanes] = nn(
            nturn_ref[...], ctx_ref[:, k * head_lanes : (k + 1) * head_lanes]
        ).astype(BF16)
        leaving.append(
            pltpu.make_async_copy(kept, grads_out.at[:, pl.ds(k * block + 2 * hidden, head_lanes)], out_sem.at[1 + k])
        )
        leaving[-1].start()
    for copy in leaving:
        copy.wait()


def flip_kernel(pick_ref, left_ref, turned_ref):
    turned_ref[...] = nt(pick_ref[...], left_ref[...]).astype(BF16)


def finish_kernel(head, layout, scal_ref, acc_ref, w_ref, *refs):
    size = layout[0]
    out_ref, held_ref, grads_ref, sem = refs[-4:]
    g_refs = refs[:size]
    rows = acc_ref.shape[0]
    half = rows // 2
    for copy in row_copies(w_ref, layout, range(size), head * WIDE, WIDE, held_ref, sem):
        copy.start()
    lower = lax.broadcasted_iota(jnp.int32, (half, PAIR), 1) < HD
    for k in range(size):
        at = k * WIDE
        grads_ref[:, at : at + PAIR] = g_refs[k][:rows]
        packed = g_refs[k][rows:].astype(F32)
        grads_ref[:half, at + PAIR : at + WIDE] = jnp.where(lower, packed, 0.0).astype(BF16)
        grads_ref[half:, at + PAIR : at + WIDE] = jnp.where(lower, pltpu.roll(packed, HD, 1), 0.0).astype(BF16)
    all_of(held_ref, sem).wait()
    out_ref[...] = acc_ref[...] + nt(grads_ref[...], held_ref[...])


def cost(micros, exps=0):
    return pl.CostEstimate(flops=int(micros * PEAK_PER_MICRO), bytes_accessed=0, transcendentals=int(exps))


def head_spec(shape, head):
    return pl.BlockSpec((1,) + shape, lambda i: (head,) + (0,) * len(shape))


def full(shape):
    return pl.BlockSpec(tuple(shape), lambda i: (0,) * len(shape))


def held():
    return pl.BlockSpec(memory_space=pl.ANY)


def scalars_spec():
    return pl.BlockSpec(memory_space=pltpu.SMEM)


def shape_of(shape, dtype=BF16):
    return jax.ShapeDtypeStruct(tuple(shape), dtype)


def call(kernel, name, in_specs, out_specs, out_shape, scratch, estimate, mib, grid=(1,), after=()):
    count = len(in_specs)

    def body(*refs):
        kernel(*refs[:count], *refs[count + len(after) :])

    run = pl.pallas_call(
        body,
        grid=grid,
        in_specs=list(in_specs) + [held()] * len(after),
        out_specs=out_specs,
        out_shape=out_shape,
        scratch_shapes=scratch,
        compiler_params=pltpu.CompilerParams(vmem_limit_bytes=mib * 1024 * 1024),
        name=name,
        cost_estimate=estimate,
    )
    return lambda *args: run(*args, *after)


def prepare(query, key, value, out, up, down_t, heads):
    shard, hidden = up.shape
    lanes = 2 * hidden + -(-out.shape[0] // CL) * CL
    args = (query, key, value, out, up, down_t)
    shapes = [shape_of((shard, heads * WIDE)), shape_of((shard, lanes))]
    return call(
        prepare_kernel, "prepare", [full(a.shape) for a in args], [full(s.shape) for s in shapes], shapes, [],
        cost(1), 60,
    )(*args)


def unmix(grads, local_width):
    shard = grads.shape[0]
    shapes = [shape_of((shard, local_width), F32)] * 3
    return call(
        unmix_kernel, "unmix", [full(grads.shape)], [full(s.shape) for s in shapes], shapes, [],
        cost(1), 16,
    )(grads)


def slot_tokens(seqs, scalars, clusters, balance):
    heads, count = clusters.shape[0], clusters.shape[2]
    row = pl.BlockSpec((1, 1, count), lambda h: (h, 0, 0))
    wide = pl.BlockSpec((1, count, CL), lambda h: (h, 0, 0))
    return call(
        functools.partial(order_kernel, seqs), "slot_tokens",
        [scalars_spec(), row, full(balance.shape)], [row, wide, wide],
        [shape_of((heads, 1, count), F32), shape_of((heads, count, CL), F32), shape_of((heads, count, CL))],
        [pltpu.VMEM((8, count), BF16)],
        cost(10), 16, grid=(heads,),
    )(scalars, clusters, balance)


def project(size, heads, step, scalars, weights, biases, pieces, held_before):
    rows, width = pieces[0].shape
    shapes = [shape_of((size * rows, width)), shape_of((heads, size * rows, WIDE))]
    first = 3 + len(pieces)
    return pl.pallas_call(
        functools.partial(project_kernel, size, heads, step),
        grid=(1,),
        in_specs=[scalars_spec(), full(weights.shape), full(biases.shape)]
        + [held()] * (len(pieces) + len(held_before)),
        out_specs=[held()] * 2,
        out_shape=shapes,
        scratch_shapes=[
            pltpu.VMEM((rows, width), BF16),
            pltpu.VMEM((heads, rows, WIDE), BF16),
            pltpu.SemaphoreType.DMA(()),
            pltpu.SemaphoreType.DMA((heads + 1,)),
        ],
        input_output_aliases={first: 0, first + 1: 1} if step else {},
        compiler_params=pltpu.CompilerParams(vmem_limit_bytes=24 * 1024 * 1024),
        name="project",
        cost_estimate=cost(2),
    )(scalars, weights, biases, *pieces, *held_before)


def attend(size, first, heads, order, wide, mask, qkv, extra, after):
    count = qkv.shape[1]
    half = count // size // 2
    row = pl.BlockSpec((1, 1, count), lambda h: (h + first, 0, 0))
    block = pl.BlockSpec((1, count, WIDE), lambda h: (h + first, 0, 0))
    column = pl.BlockSpec((1, count, CL), lambda h: (h + first, 0, 0))
    shapes = [shape_of((heads, count, WIDE))] + [shape_of((heads * half + extra.shape[0], PAIR))] * size
    return call(
        functools.partial(forward_kernel, size, heads, count // 2), "attend",
        [row, column, column, block, full(extra.shape)],
        [pl.BlockSpec((1, count, WIDE), lambda h: (h, 0, 0))] + [full(s.shape) for s in shapes[1:]], shapes,
        [pltpu.VMEM((count, PAIR), BF16)],
        cost(6.5 * heads), 60, grid=(heads,), after=after,
    )(order, wide, mask, qkv, extra)


def attend_back(size, head, order, wide, mask, slots, place, turned_x, grad_context, after):
    count = slots.shape[1]
    rows = count // size
    cut = turned_x.shape[0] // 2
    shapes = (
        [shape_of((rows + rows // 2, PAIR))] * size + [shape_of((cut, WIDE))] * 2 + [shape_of((1, PAIR), F32)]
    )
    return call(
        functools.partial(backward_kernel, size, count // 2), "attend_back",
        [head_spec((1, count), head), head_spec((count, CL), head), head_spec((count, CL), head)]
        + [head_spec((count, WIDE), place), full(turned_x.shape)]
        + [pl.BlockSpec((rows // 2, PAIR), lambda i: (head, 0))] * size,
        [held()] * size + [full(s.shape) for s in shapes[size:]], shapes,
        [pltpu.VMEM((count, PAIR), BF16), pltpu.VMEM((count, WIDE), BF16), pltpu.VMEM((count, WIDE), BF16)]
        + [pltpu.VMEM((size * (rows + rows // 2), PAIR), BF16), pltpu.SemaphoreType.DMA((size,))],
        cost(3), 40, after=after,
    )(order, wide, mask, slots, turned_x, *grad_context)


def layer(heads, layout, hidden, scalars, inputs, out_grad, vectors, received, ff):
    size = layout[0]
    rows, width = inputs.shape
    block = ff.shape[1]
    head_lanes = block - 2 * hidden
    shapes = [
        shape_of((rows, width)),
        shape_of((rows, width), F32),
        shape_of((8 + size, width), F32),
        shape_of((width, size * block)),
    ] + [shape_of((heads * (rows // 2), PAIR))] * size
    args = (inputs, out_grad, vectors)

    def kept(shape, dtype=BF16):
        return pltpu.VMEM(shape, dtype)

    return call(
        functools.partial(layer_kernel, heads, layout), "layer",
        [scalars_spec()] + [full(a.shape) for a in args] + [held()] + [full(r.shape) for r in received],
        [full(s.shape) if i != 3 else held() for i, s in enumerate(shapes)], shapes,
        [
            kept((width, size * hidden)),
            kept((width, size * hidden)),
            kept((width, size * head_lanes)),
            kept((rows, size * hidden)),
            kept((rows, size * hidden), F32),
            kept((rows, width), F32),
            kept((rows, hidden)),
            kept((rows, width)),
            kept((rows, width)),
            kept((rows, width)),
            kept((rows, size * head_lanes)),
            kept((width, rows)),
            kept((width, rows)),
            kept((width, 2 * hidden)),
            pltpu.SemaphoreType.DMA((3,)),
            pltpu.SemaphoreType.DMA((1 + size,)),
        ],
        cost(33), 58,
    )(scalars, *args, ff, *received)


def flip(size, pick, left):
    count, width = left.shape
    rows = count // size
    return call(
        flip_kernel, "flip",
        [full(pick.shape), pl.BlockSpec((rows, width), lambda i: (i, 0))],
        pl.BlockSpec((width, rows), lambda i: (0, i)), shape_of((width, count)), [],
        cost(0.05), 16, grid=(size,),
    )(pick, left)


def finish(head, layout, scalars, total, weights, grads, after):
    size = layout[0]
    rows, width = total.shape
    return call(
        functools.partial(finish_kernel, head, layout), "finish",
        [scalars_spec(), full(total.shape), held()] + [full(g.shape) for g in grads],
        full(total.shape), shape_of(total.shape, F32),
        [
            pltpu.VMEM((width, size * WIDE), BF16),
            pltpu.VMEM((rows, size * WIDE), BF16),
            pltpu.SemaphoreType.DMA(()),
        ],
        cost(1), 24, after=after,
    )(scalars, total, weights, *grads)


def shift(values, size, k):
    return lax.ppermute(values, "tensor", [(i, (i + k) % size) for i in range(size)])


def exchange(parts, size):
    return [parts[0]] + [shift(parts[size - k], size, k) for k in range(1, size)]


def line_step(up, down, k, size):
    return (
        lax.ppermute(up, "tensor", [(i, i + 1) for i in range(k - 1, size - 1)]),
        lax.ppermute(down, "tensor", [(i + 1, i) for i in range(0, size - k)]),
    )


def gather_line(own, size):
    ups, downs = [own], [own]
    for k in range(1, size):
        up, down = line_step(ups[-1], downs[-1], k, size)
        ups.append(up)
        downs.append(down)
    return ups[1:], downs[1:]


def swap(values, axis, bit):
    return lax.ppermute(values, axis, [(i, i ^ bit) for i in range(lax.axis_size(axis))])


def bits_of(size):
    return [1 << b for b in range(size.bit_length() - 1)]


def add_low(left, right):
    return (left.astype(F32) + right.astype(F32)).astype(BF16)


def halves(mine, arrived):
    cut = mine.shape[0] // 2
    return add_low(mine[:cut], arrived[:cut]), add_low(mine[cut:], arrived[cut:])


def total_of(parts):
    result = parts[0].astype(F32)
    for part in parts[1:]:
        result = result + part.astype(F32)
    return result


def tie(*groups):
    return lax.optimization_barrier(groups)


def local(
    inputs, out_grad, seq_lengths, balance, clusters, query_weight, query_bias, key_weight,
    value_weight, value_bias, out_weight, out_bias, norm1_gain, norm1_bias, up_weight, up_bias,
    down_weight, down_bias, norm2_gain, norm2_bias,
):
    dp = ("chip", "core")
    rows, width = inputs.shape
    size = lax.axis_size("tensor")
    chips = lax.axis_size("chip")
    rank, chip, core = (lax.axis_index(axis) for axis in ("tensor", "chip", "core"))
    shard = query_weight.shape[0]
    local_width = query_weight.shape[1]
    heads = clusters.shape[1]
    seqs = seq_lengths.shape[1]
    bits = bits_of(chips)

    bounds = jnp.cumsum(seq_lengths[0])
    scalars = jnp.concatenate([jnp.stack([rank, core, jnp.int32(rows)]), bounds]).astype(jnp.int32)
    direct = shard % 16 == 0
    layout = (size, 2 * chips if direct else 1, shard)
    hidden = up_weight.shape[1]

    def whole(near):
        rows_in = lax.all_gather(near, dp, axis=0, tiled=True)
        if direct:
            return rows_in
        lanes = near.shape[1]
        return rows_in.reshape(2 * chips, size, shard, lanes).transpose(1, 0, 2, 3).reshape(size * width, lanes)

    head_weights, ff_own = prepare(
        query_weight, key_weight, value_weight, out_weight, up_weight, down_weight.T, heads
    )
    ups, downs = gather_line(inputs, size)
    ff_ups, ff_downs = [ff_own], [ff_own]
    for k in range(1, size):
        if k == size - 1:
            ff_ups[-1], ff_downs[-1], ups[0], downs[0] = tie(ff_ups[-1], ff_downs[-1], ups[0], downs[0])
        one_up, one_down = line_step(ff_ups[-1], ff_downs[-1], k, size)
        ff_ups.append(one_up)
        ff_downs.append(one_down)
    near = jnp.concatenate(
        [ff_own] + [jnp.where(rank >= k, ff_ups[k], ff_downs[size - k]) for k in range(1, size)], axis=0
    )
    own_qkv = lax.all_gather(head_weights, dp, axis=0, tiled=True)
    near, own_qkv = tie(near, own_qkv)
    ff = whole(near)
    blank = jnp.zeros((heads, HD), F32)
    head_biases = jnp.concatenate(
        [query_bias.reshape(heads, HD), value_bias.reshape(heads, HD), blank, blank], axis=-1
    ).reshape(1, heads * WIDE)
    terms, rest = [], up_bias
    for _ in range(3):
        term = lax.reduce_precision(rest, 8, 7)
        terms.append(term.astype(BF16))
        rest = rest - term
    extra = jnp.concatenate(terms).reshape(-1, PAIR)
    extra = jnp.pad(extra, ((0, -extra.shape[0] % 16), (0, 0)))
    vectors = jnp.stack([out_bias, norm1_gain, norm1_bias, down_bias, norm2_gain, norm2_bias])

    def row_pick(order_bits):
        place = jnp.arange(width, dtype=jnp.int32)
        block = place // shard
        away = jnp.zeros_like(block)
        for depth, bit in enumerate(order_bits):
            away = away + ((block >> (len(order_bits) - 1 - depth)) & 1) * bit
        near = chip ^ away
        owner = near * 2 + (core ^ (block // chips))
        return one_hot((owner * shard + place % shard)[:, None] == place[None, :])

    pick = row_pick(bits)
    order, wide, mask = slot_tokens(seqs, scalars, clusters[0][:, None, :], balance)
    whole_rows = []
    for step in range(size):
        pieces = [ups[step - 1], downs[step - 1]] if step else [inputs]
        whole_rows = project(size, heads, step, scalars, own_qkv, head_biases, pieces, whole_rows)
    x_all, qkv = whole_rows
    later_weights, qkv = tie(head_weights, qkv)
    later_near = jnp.concatenate([later_weights] + [shift(later_weights, size, k) for k in range(1, size)], axis=0)

    kept_a, *context_a = attend(size, 0, heads - 1, order, wide, mask, qkv, extra, [])
    context_a, later_near = tie(context_a, later_near)
    later = whole(later_near)
    received = exchange(context_a, size)
    kept_b, *context_b = attend(size, heads - 1, 1, order, wide, mask, qkv, extra[:16], [context_a[0]])
    received, context_b = tie(received, context_b)
    received = received + exchange(context_b, size)
    slots = [(kept_a, h) for h in range(heads - 1)] + [(kept_b, 0)]
    turned_x = flip(size, pick, x_all)
    layer_out, grad_summed, small, grads, *grad_ctx = layer(
        heads, layout, hidden, scalars, inputs, out_grad, vectors, received, ff
    )
    arrived = exchange(grad_ctx, size)
    grads, later = tie(grads, later)
    grads = lax.psum_scatter(grads, dp, scatter_dimension=0, tiled=True)

    backs, head_mine, head_other, bias_sums = [], [], [], []
    for h in range(heads):
        after = backs[h - 2][1:] if h >= 2 else []
        outs = attend_back(size, h, order, wide, mask, *slots[h], turned_x, arrived, after)
        backs.append(exchange(outs[:size], size))
        head_mine.append(outs[size])
        head_other.append(outs[size + 1])
        bias_sums.append(outs[size + 2])
        if h < len(bits_of(size)):
            small = small + swap(small, "tensor", bits_of(size)[h])
            arrived, small = tie(arrived, small)
    backs[heads - 2], head_other = tie(backs[heads - 2], head_other)
    mine = jnp.concatenate(head_mine, axis=1)
    far = swap(jnp.concatenate(head_other, axis=1), "core", 1)
    sums = jnp.concatenate([small, jnp.pad(jnp.concatenate(bias_sums, axis=0), ((0, 0), (0, width - PAIR)))], axis=0)
    sums = sums + swap(sums, "core", 1)
    grad_inputs = grad_summed
    for h in range(heads - 1):
        grad_inputs = finish(h, layout, scalars, grad_inputs, later, backs[h], [])
    for bit in bits:
        mine, sent = halves(mine, far)
        far = swap(sent, "chip", bit)
        sums = sums + swap(sums, "chip", bit)
    head_sum = add_low(mine, far)
    bias = sums[small.shape[0] :]
    grad_query_bias = bias[:, :HD].reshape(local_width)
    grad_value_bias = bias[:, HD:PAIR].reshape(local_width)
    grad_up_bias = lax.dynamic_index_in_dim(sums, 8 + rank, 0, keepdims=False)
    lanes = grads.shape[1] // size
    parts = [grads[:, k * lanes : (k + 1) * lanes] for k in range(size)]
    parts, grad_inputs, back_last, head_sum = tie(parts, grad_inputs, backs[heads - 1], head_sum)
    backs[heads - 1] = back_last
    moved = exchange(parts, size)
    grad_query_weight, grad_key_weight, grad_value_weight = unmix(head_sum, local_width)
    grads = total_of(moved)
    grad_inputs = finish(heads - 1, layout, scalars, grad_inputs, later, backs[heads - 1], [])
    grad_up_weight = grads[:, :hidden]
    grad_down_weight = grads[:, hidden : 2 * hidden].T
    grad_out_weight = grads[:, 2 * hidden : 2 * hidden + local_width].T
    return (
        layer_out, grad_inputs, grad_query_weight, grad_query_bias, grad_key_weight, grad_value_weight,
        grad_value_bias, grad_out_weight, sums[0], sums[1], sums[2], grad_up_weight, grad_up_bias,
        grad_down_weight, sums[3], sums[4], sums[5],
    )


def solution(mesh):
    devices = mesh.devices
    split = Mesh(devices.reshape(devices.shape[0] // 2, 2, devices.shape[1]), ("chip", "core", "tensor"))
    dp = ("chip", "core")
    rows, weight, turned_weight, vector, same = (
        P(dp + ("tensor",), None),
        P(dp, "tensor"),
        P("tensor", dp),
        P("tensor"),
        P(),
    )
    in_specs = (
        rows, rows, P(dp, None), P(dp, None), P(dp, "tensor", None), weight, vector, weight, weight,
        vector, turned_weight, same, same, same, weight, vector, turned_weight, same, same, same,
    )
    out_specs = (
        rows, rows, weight, vector, weight, weight, vector, turned_weight, same, same, same, weight, vector,
        turned_weight, same, same, same,
    )
    return jax.shard_map(local, mesh=split, in_specs=in_specs, out_specs=out_specs, check_vma=False)
```

```python
import functools

import jax
import jax.numpy as jnp
from jax import lax
from jax.experimental import pallas as pl
from jax.experimental.pallas import tpu as pltpu
from jax.sharding import Mesh, PartitionSpec as P

HD = 64
CL = 128
PAIR = 2 * HD
WIDE = 4 * HD
F32 = jnp.float32
BF16 = jnp.bfloat16
EPS = 1e-06
PEAK_PER_MICRO = 1.15e9


def nn(left, right):
    return jnp.dot(left, right, preferred_element_type=F32)


def nt(left, right):
    return lax.dot_general(left, right, (((1,), (1,)), ((), ())), preferred_element_type=F32)


def tn(left, right):
    return lax.dot_general(left, right, (((0,), (0,)), ((), ())), preferred_element_type=F32)


def one_hot(hits):
    return jnp.where(hits, 1.0, 0.0).astype(BF16)


def head_lane(shape, dim, part):
    lane = lax.broadcasted_iota(jnp.int32, shape, dim)
    column = (lane // WIDE) * HD + lane % HD
    return jnp.where((lane % WIDE) // HD == part, column, -1)


def prepare_kernel(q_ref, k_ref, v_ref, o_ref, up_ref, dn_ref, heads_ref, ff_ref):
    shape = (q_ref.shape[1], heads_ref.shape[1])
    column = lax.broadcasted_iota(jnp.int32, shape, 0)
    total = jnp.zeros(heads_ref.shape, F32)
    for part, ref in ((0, q_ref), (1, v_ref), (2, k_ref)):
        total = total + nn(ref[...], one_hot(head_lane(shape, 1, part) == column))
    heads_ref[...] = total.astype(BF16)
    hidden = up_ref.shape[1]
    ff_ref[:, :hidden] = up_ref[...]
    ff_ref[:, hidden : 2 * hidden] = dn_ref[...]
    shape = (ff_ref.shape[1] - 2 * hidden, o_ref.shape[0])
    spread = one_hot(lax.broadcasted_iota(jnp.int32, shape, 0) == lax.broadcasted_iota(jnp.int32, shape, 1))
    padded = nn(spread, o_ref[...]).astype(BF16)
    rows = o_ref.shape[1]
    same = lax.broadcasted_iota(jnp.int32, (rows, rows), 0) == lax.broadcasted_iota(jnp.int32, (rows, rows), 1)
    ff_ref[:, 2 * hidden :] = nt(one_hot(same), padded).astype(BF16)


def unmix_kernel(grads_ref, q_ref, k_ref, v_ref):
    shape = (q_ref.shape[1], grads_ref.shape[1])
    column = lax.broadcasted_iota(jnp.int32, shape, 0)
    for part, ref in ((0, q_ref), (1, v_ref), (2, k_ref)):
        ref[...] = nt(grads_ref[...], one_hot(head_lane(shape, 1, part) == column))


def column_of(row):
    return jnp.transpose(jnp.broadcast_to(row, (CL, CL)))


def order_kernel(seqs, scal_ref, clusters_ref, balance_ref, order_ref, wide_ref, mask_ref, table_ref):
    count = balance_ref.shape[1]
    step = 2 * CL
    rows = scal_ref[2]
    balance = balance_ref[...]
    high = balance // HD
    low = balance - high * HD
    pick = lax.broadcasted_iota(jnp.int32, (8, count), 0)
    table = jnp.where(pick == 0, high, jnp.where(pick == 1, low, 0)).astype(F32).astype(BF16)
    chosen = clusters_ref[0]
    table_ref[...] = table

    def pick_block(i, total):
        start = pl.multiple_of(i * step, step)
        place = lax.broadcasted_iota(jnp.int32, (step, count), 0) + start
        return total + nn(table_ref[:, pl.ds(start, step)], one_hot(place == chosen))

    total = lax.fori_loop(0, count // step, pick_block, jnp.zeros((8, count), F32))
    token = (total[0:1] * float(HD) + total[1:2]).astype(jnp.int32)
    segment = jnp.zeros_like(token)
    for s in range(seqs):
        segment = segment + jnp.where(token >= scal_ref[3 + s], 1, 0)
    segment = segment.astype(F32)
    from_own = scal_ref[0] * rows - (token // rows) * rows
    from_own = jnp.where(from_own < 0, from_own + count, from_own)
    order = (from_own + token % rows).astype(F32)
    order_ref[0] = order
    for at in range(0, count, CL):
        wide_ref[0, at : at + CL] = column_of(order[:, at : at + CL])
        row = segment[:, at : at + CL]
        mask_ref[0, at : at + CL] = jnp.where(column_of(row) == row, 0.0, -1e30).astype(BF16)


def slots_by_tokens(wide_ref, start, span, count):
    lane = lax.broadcasted_iota(jnp.int32, (span, CL), 1).astype(F32)
    gap = wide_ref[0, pl.ds(start, span)] - lane
    return jnp.concatenate([one_hot(gap == float(j)) for j in range(0, count, CL)], axis=1)


def tokens_by_slots(order_ref, start, span, count):
    row = order_ref[0] - jnp.asarray(start, F32)
    return one_hot(lax.broadcasted_iota(jnp.int32, (span, count), 0).astype(F32) == row)


def by_cluster(product, left, right):
    return jnp.concatenate(
        [product(left[at : at + CL], right[at : at + CL]) for at in range(0, left.shape[0], CL)], axis=0
    )


def softmax_of(first, second, mask):
    scores = by_cluster(nt, first, second) * HD ** (-0.5) + mask.astype(F32)
    raised = jnp.exp(scores - jnp.max(scores, axis=1, keepdims=True))
    return raised * (1.0 / jnp.sum(raised, axis=1, keepdims=True))


def upper_half(values):
    lane = lax.broadcasted_iota(jnp.int32, values.shape, 1)
    return jnp.where(lane >= HD, values, 0.0)


def project_kernel(size, heads, step, scal_ref, w_ref, b_ref, *refs):
    pieces = refs[: 1 if step == 0 else 2]
    x_out, qkv_out, x_ref, qkv_ref, sem, out_sem = refs[-6:]
    rows = x_ref.shape[0]
    rank = scal_ref[0]

    def block(piece, k):
        incoming = pltpu.make_async_copy(piece, x_ref, sem)
        incoming.start()
        incoming.wait()
        place = pl.ds(k * rows, rows)
        leaving = [pltpu.make_async_copy(x_ref, x_out.at[place], out_sem.at[heads])]
        leaving[0].start()
        for h in range(heads):
            lanes = slice(h * WIDE, (h + 1) * WIDE)
            qkv_ref[h] = (nn(x_ref[...], w_ref[:, lanes]) + b_ref[:, lanes]).astype(BF16)
            leaving.append(pltpu.make_async_copy(qkv_ref.at[h], qkv_out.at[h, place], out_sem.at[h]))
            leaving[-1].start()
        for copy in leaving:
            copy.wait()

    if step == 0:
        block(pieces[0], 0)
        return

    @pl.when(rank >= step)
    def _():
        block(pieces[0], step)

    @pl.when(rank < size - step)
    def _():
        block(pieces[1], size - step)


def forward_kernel(size, heads, span, order_ref, wide_ref, mask_ref, qkv_ref, extra_ref, slots_ref, *refs):
    outs, ctx_ref = refs[:size], refs[size]
    head = pl.program_id(0)
    count = qkv_ref.shape[1]
    rows = count // size
    half = rows // 2
    for k in range(size):
        outs[k][heads * half :] = extra_ref[...]

    def gather(i, carry):
        start = pl.multiple_of(i * span, span)
        here = pl.ds(start, span)
        picked = nn(slots_by_tokens(wide_ref, start, span, count), qkv_ref[0]).astype(BF16)
        slots_ref[0, here] = picked
        first = picked[:, :PAIR]
        probs = softmax_of(first, picked[:, PAIR:], mask_ref[0, here])
        ctx_ref[here] = upper_half(by_cluster(nn, probs.astype(BF16), first)).astype(BF16)
        return carry

    lax.fori_loop(0, count // span, gather, 0)
    at = pl.ds(pl.multiple_of(head * half, half), half)
    for k in range(size):
        given = nn(tokens_by_slots(order_ref, k * rows, rows, count), ctx_ref[...])
        outs[k][at] = (pltpu.roll(given[:half], HD, 1) + given[half:]).astype(BF16)


def backward_kernel(size, span, order_ref, wide_ref, mask_ref, slots_ref, turned_ref, *refs):
    g_refs, outs = refs[:size], refs[size : 2 * size]
    mine_ref, other_ref, bias_ref, gctx_ref, grad_ref, tok_ref = refs[2 * size :]
    count = slots_ref.shape[1]
    rows = count // size
    half = rows // 2
    for k in range(size):
        packed = g_refs[k][...].astype(F32)
        gctx_ref[k * rows : k * rows + half] = upper_half(pltpu.roll(packed, HD, 1)).astype(BF16)
        gctx_ref[k * rows + half : (k + 1) * rows] = upper_half(packed).astype(BF16)

    def gather(i, sums):
        start = pl.multiple_of(i * span, span)
        here = pl.ds(start, span)
        grad_ctx = nn(slots_by_tokens(wide_ref, start, span, count), gctx_ref[...]).astype(BF16)
        part = slots_ref[0, here]
        first, second = part[:, :PAIR], part[:, PAIR:]
        probs = softmax_of(first, second, mask_ref[0, here])
        grad_prob = by_cluster(nt, grad_ctx, first)
        inner = jnp.sum(probs * grad_prob, axis=1, keepdims=True)
        grad_scores = (probs * (grad_prob - inner)).astype(BF16)
        grad_query = by_cluster(nn, grad_scores, second) * HD ** (-0.5)
        grad_key = by_cluster(tn, grad_scores, first) * HD ** (-0.5)
        grad_value = by_cluster(tn, probs.astype(BF16), grad_ctx)
        lane = lax.broadcasted_iota(jnp.int32, (span, PAIR), 1)
        grad_qv = jnp.where(lane < HD, grad_query, grad_value).astype(BF16)
        grad_ref[here, :PAIR] = grad_qv
        grad_ref[here, PAIR:] = jnp.where(lane < HD, grad_key, 0.0).astype(BF16)
        return sums + jnp.sum(grad_qv.astype(F32), axis=0, keepdims=True)

    bias_ref[...] = lax.fori_loop(0, count // span, gather, jnp.zeros((1, PAIR), F32))
    for k in range(size):
        given = nn(tokens_by_slots(order_ref, k * rows, rows, count), grad_ref[...])
        low = given.astype(BF16)
        tok_ref[k * rows : (k + 1) * rows] = low
        outs[k][:rows] = low[:, :PAIR]
        outs[k][rows:] = (given[:half, PAIR:] + pltpu.roll(given[half:, PAIR:], HD, 1)).astype(BF16)
    cut = turned_ref.shape[0] // 2
    mine_ref[...] = nn(turned_ref[:cut], tok_ref[...]).astype(BF16)
    other_ref[...] = nn(turned_ref[cut:], tok_ref[...]).astype(BF16)


def row_stats(values_in):
    center = values_in - jnp.mean(values_in, axis=-1, keepdims=True)
    inverse = lax.rsqrt(jnp.mean(center * center, axis=-1, keepdims=True) + EPS)
    return center * inverse, inverse


def norm_back(cotangent, gain, hat, inverse):
    scaled = cotangent * gain
    return inverse * (
        scaled
        - jnp.mean(scaled, axis=-1, keepdims=True)
        - hat * jnp.mean(scaled * hat, axis=-1, keepdims=True)
    )


def column_sum(values_in):
    return jnp.sum(values_in, axis=0, keepdims=True)


def row_copies(ref, layout, blocks, start, lanes, held, sem):
    size, groups, shard = layout
    if groups == 1:
        shard = held.shape[0]

    def rows_of(group, k):
        at = (group * size + blocks[k]) * shard
        return pl.ds(at if isinstance(at, int) else pl.multiple_of(at, shard), shard)

    return [
        pltpu.make_async_copy(
            ref.at[rows_of(group, k), pl.ds(start, lanes)],
            held.at[pl.ds(group * shard, shard), pl.ds(k * lanes, lanes)],
            sem,
        )
        for group in range(groups)
        for k in range(size)
    ]


def all_of(held, sem):
    return pltpu.make_async_copy(held, held, sem)


def layer_kernel(heads, layout, scal_ref, x_ref, og_ref, vec_ref, ff_ref, *refs):
    size = layout[0]
    recv_refs, refs = refs[: 2 * size], refs[2 * size :]
    layer_ref, sum_ref, small_ref, grads_out = refs[:4]
    gctx_refs = refs[4 : 4 + size]
    (
        wup_ref, wdn_ref, wo_ref, act_ref, slope_ref, total_ref, gup_ref, nlow_ref, plow_ref, slow_ref, ctx_ref,
        nturn_ref, pturn_ref, stage_ref, sem, out_sem,
    ) = refs[4 + size :]
    rows, width = x_ref.shape
    hidden = wup_ref.shape[1] // size
    head_lanes = wo_ref.shape[1] // size
    block = 2 * hidden + head_lanes
    rank = scal_ref[0]

    for kind, (start, lanes, held) in enumerate(
        ((2 * hidden, head_lanes, wo_ref), (0, hidden, wup_ref), (hidden, hidden, wdn_ref))
    ):
        for copy in row_copies(ff_ref, layout, range(size), start, lanes, held, sem.at[kind]):
            copy.start()

    half = rows // 2
    lower = lax.broadcasted_iota(jnp.int32, (half, PAIR), 1) < HD

    def piece(k, h):
        if h >= heads:
            return jnp.zeros((half, PAIR), F32)
        if h == heads - 1:
            return recv_refs[size + k][:half].astype(F32)
        return recv_refs[k][h * half : (h + 1) * half].astype(F32)

    for k in range(size):
        for h in range(0, heads, 2):
            first, second = piece(k, h), piece(k, h + 1)
            lanes = slice(k * head_lanes + h * HD, k * head_lanes + h * HD + PAIR)
            ctx_ref[:half, lanes] = jnp.where(lower, first, pltpu.roll(second, HD, 1)).astype(BF16)
            ctx_ref[half:, lanes] = jnp.where(lower, pltpu.roll(first, HD, 1), second).astype(BF16)
    row = lax.broadcasted_iota(jnp.int32, (width, width), 0)
    same = one_hot(row == lax.broadcasted_iota(jnp.int32, (width, width), 1))
    all_of(wo_ref, sem.at[0]).wait()
    summed = x_ref[...].astype(F32) + nt(ctx_ref[...], wo_ref[...]) + vec_ref[0:1]
    hat1, inverse1 = row_stats(summed)
    normed = hat1 * vec_ref[1:2] + vec_ref[2:3]
    nlow_ref[...] = normed.astype(BF16)
    total_ref[...] = normed + vec_ref[3:4]
    curve = (2.0 / 3.141592653589793) ** 0.5
    cut = hidden // PAIR
    biases = []
    for k in range(size):
        parts = recv_refs[k][(heads - 1) * half :].astype(F32)
        bias = parts[:cut] + parts[cut : 2 * cut] + parts[2 * cut : 3 * cut]
        biases.append(jnp.concatenate([bias[i : i + 1] for i in range(cut)], axis=1))
        small_ref[8 + k : 9 + k] = biases[-1]
    all_of(wup_ref, sem.at[1]).wait()
    all_of(wdn_ref, sem.at[2]).wait()

    def span(k):
        return pl.ds(pl.multiple_of(k * hidden, hidden), hidden)

    def forward(k, carry):
        lanes = span(k)
        up = nn(nlow_ref[...], wup_ref[:, lanes]) + small_ref[pl.ds(8 + k, 1)]
        square = up * up
        tanh = jnp.tanh(up * (curve + (0.044715 * curve) * square))
        gate = 0.5 + 0.5 * tanh
        act_ref[:, lanes] = (up * gate).astype(BF16)
        slope_ref[:, lanes] = gate + (0.5 * up) * (1.0 - tanh * tanh) * (curve + (3 * 0.044715 * curve) * square)
        total_ref[...] += nt(act_ref[:, lanes], wdn_ref[:, lanes])
        return carry

    lax.fori_loop(0, size, forward, 0)
    nturn_ref[...] = nt(same, nlow_ref[...]).astype(BF16)
    hat2, inverse2 = row_stats(total_ref[...])
    gain2 = vec_ref[4:5]
    layer_ref[...] = (hat2 * gain2 + vec_ref[5:6]).astype(BF16)
    cot = og_ref[...].astype(F32)
    grad_pre = norm_back(cot, gain2, hat2, inverse2)
    plow_ref[...] = grad_pre.astype(BF16)
    pturn_ref[...] = nt(same, plow_ref[...]).astype(BF16)
    small_ref[3:4] = column_sum(grad_pre)
    small_ref[4:5] = column_sum(cot * hat2)
    small_ref[5:6] = column_sum(cot)
    small_ref[6:8] = jnp.zeros((2, width), F32)
    total_ref[...] = grad_pre

    def leave(k):
        at = pl.multiple_of(k * block, block)
        return pltpu.make_async_copy(stage_ref, grads_out.at[:, pl.ds(at, 2 * hidden)], out_sem.at[0])

    def backward(k, carry):
        lanes = span(k)
        grad_up = (nn(plow_ref[...], wdn_ref[:, lanes]) * slope_ref[:, lanes]).astype(BF16)
        gup_ref[...] = grad_up
        small_ref[pl.ds(8 + lax.rem(rank - k + size, size), 1)] = column_sum(grad_up.astype(F32))
        total_ref[...] += nt(gup_ref[...], wup_ref[:, lanes])

        @pl.when(k > 0)
        def _():
            leave(k - 1).wait()

        stage_ref[:, :hidden] = nn(nturn_ref[...], gup_ref[...]).astype(BF16)
        stage_ref[:, hidden:] = nn(pturn_ref[...], act_ref[:, lanes]).astype(BF16)
        leave(k).start()
        return carry

    lax.fori_loop(0, size, backward, 0)
    grad_normed = total_ref[...]
    small_ref[1:2] = column_sum(grad_normed * hat1)
    small_ref[2:3] = column_sum(grad_normed)
    grad_summed = norm_back(grad_normed, vec_ref[1:2], hat1, inverse1)
    small_ref[0:1] = column_sum(grad_summed)
    sum_ref[...] = grad_summed
    slow_ref[...] = grad_summed.astype(BF16)
    grad_ctx = nn(slow_ref[...], wo_ref[...])
    for k in range(size):
        for h in range(0, heads, 2):
            lanes = slice(k * head_lanes + h * HD, k * head_lanes + h * HD + PAIR)
            top, bottom = grad_ctx[:half, lanes], grad_ctx[half:, lanes]
            gctx_refs[k][h * half : (h + 1) * half] = jnp.where(lower, top, pltpu.roll(bottom, HD, 1)).astype(BF16)
            if h + 1 < heads:
                gctx_refs[k][(h + 1) * half : (h + 2) * half] = jnp.where(
                    lower, pltpu.roll(top, HD, 1), bottom
                ).astype(BF16)
    leave(size - 1).wait()
    nturn_ref[...] = nt(same, slow_ref[...]).astype(BF16)
    leaving = []
    for k in range(size):
        kept = stage_ref.at[:, pl.ds(k * head_lanes, head_lanes)]
        stage_ref[:, k * head_lanes : (k + 1) * head_lanes] = nn(
            nturn_ref[...], ctx_ref[:, k * head_lanes : (k + 1) * head_lanes]
        ).astype(BF16)
        leaving.append(
            pltpu.make_async_copy(kept, grads_out.at[:, pl.ds(k * block + 2 * hidden, head_lanes)], out_sem.at[1 + k])
        )
        leaving[-1].start()
    for copy in leaving:
        copy.wait()


def total_kernel(hidden, *refs):
    parts, (up_ref, down_ref, out_ref, square_ref) = refs[:-4], refs[-4:]
    rows = up_ref.shape[0]
    total = parts[0][...].astype(F32)
    for part in parts[1:]:
        total = total + part[...].astype(F32)
    up_ref[...] = total[:, :hidden]
    down_ref[...] = total[:, hidden : 2 * hidden]
    square_ref[...] = jnp.zeros(square_ref.shape, F32)
    square_ref[:rows] = total[:, 2 * hidden :]
    turned = jnp.transpose(square_ref[...])
    out_ref[...] = turned[: out_ref.shape[0], :rows]


def flip_kernel(pick_ref, left_ref, turned_ref):
    turned_ref[...] = nt(pick_ref[...], left_ref[...]).astype(BF16)


def finish_kernel(head, layout, scal_ref, acc_ref, w_ref, *refs):
    size = layout[0]
    out_ref, held_ref, grads_ref, sem = refs[-4:]
    g_refs = refs[:size]
    rows = acc_ref.shape[0]
    half = rows // 2
    for copy in row_copies(w_ref, layout, range(size), head * WIDE, WIDE, held_ref, sem):
        copy.start()
    lower = lax.broadcasted_iota(jnp.int32, (half, PAIR), 1) < HD
    for k in range(size):
        at = k * WIDE
        grads_ref[:, at : at + PAIR] = g_refs[k][:rows]
        packed = g_refs[k][rows:].astype(F32)
        grads_ref[:half, at + PAIR : at + WIDE] = jnp.where(lower, packed, 0.0).astype(BF16)
        grads_ref[half:, at + PAIR : at + WIDE] = jnp.where(lower, pltpu.roll(packed, HD, 1), 0.0).astype(BF16)
    all_of(held_ref, sem).wait()
    out_ref[...] = acc_ref[...] + nt(grads_ref[...], held_ref[...])


def cost(micros, exps=0):
    return pl.CostEstimate(flops=int(micros * PEAK_PER_MICRO), bytes_accessed=0, transcendentals=int(exps))


def head_spec(shape, head):
    return pl.BlockSpec((1,) + shape, lambda i: (head,) + (0,) * len(shape))


def full(shape):
    return pl.BlockSpec(tuple(shape), lambda i: (0,) * len(shape))


def held():
    return pl.BlockSpec(memory_space=pl.ANY)


def scalars_spec():
    return pl.BlockSpec(memory_space=pltpu.SMEM)


def shape_of(shape, dtype=BF16):
    return jax.ShapeDtypeStruct(tuple(shape), dtype)


def call(kernel, name, in_specs, out_specs, out_shape, scratch, estimate, mib, grid=(1,), after=()):
    count = len(in_specs)

    def body(*refs):
        kernel(*refs[:count], *refs[count + len(after) :])

    run = pl.pallas_call(
        body,
        grid=grid,
        in_specs=list(in_specs) + [held()] * len(after),
        out_specs=out_specs,
        out_shape=out_shape,
        scratch_shapes=scratch,
        compiler_params=pltpu.CompilerParams(vmem_limit_bytes=mib * 1024 * 1024),
        name=name,
        cost_estimate=estimate,
    )
    return lambda *args: run(*args, *after)


def prepare(query, key, value, out, up, down_t, heads):
    shard, hidden = up.shape
    lanes = 2 * hidden + -(-out.shape[0] // CL) * CL
    args = (query, key, value, out, up, down_t)
    shapes = [shape_of((shard, heads * WIDE)), shape_of((shard, lanes))]
    return call(
        prepare_kernel, "prepare", [full(a.shape) for a in args], [full(s.shape) for s in shapes], shapes, [],
        cost(1), 60,
    )(*args)


def unmix(grads, local_width):
    shard = grads.shape[0]
    shapes = [shape_of((shard, local_width), F32)] * 3
    return call(
        unmix_kernel, "unmix", [full(grads.shape)], [full(s.shape) for s in shapes], shapes, [],
        cost(1), 16,
    )(grads)


def slot_tokens(seqs, scalars, clusters, balance):
    heads, count = clusters.shape[0], clusters.shape[2]
    row = pl.BlockSpec((1, 1, count), lambda h: (h, 0, 0))
    wide = pl.BlockSpec((1, count, CL), lambda h: (h, 0, 0))
    return call(
        functools.partial(order_kernel, seqs), "slot_tokens",
        [scalars_spec(), row, full(balance.shape)], [row, wide, wide],
        [shape_of((heads, 1, count), F32), shape_of((heads, count, CL), F32), shape_of((heads, count, CL))],
        [pltpu.VMEM((8, count), BF16)],
        cost(10), 16, grid=(heads,),
    )(scalars, clusters, balance)


def project(size, heads, step, scalars, weights, biases, pieces, held_before):
    rows, width = pieces[0].shape
    shapes = [shape_of((size * rows, width)), shape_of((heads, size * rows, WIDE))]
    first = 3 + len(pieces)
    return pl.pallas_call(
        functools.partial(project_kernel, size, heads, step),
        grid=(1,),
        in_specs=[scalars_spec(), full(weights.shape), full(biases.shape)]
        + [held()] * (len(pieces) + len(held_before)),
        out_specs=[held()] * 2,
        out_shape=shapes,
        scratch_shapes=[
            pltpu.VMEM((rows, width), BF16),
            pltpu.VMEM((heads, rows, WIDE), BF16),
            pltpu.SemaphoreType.DMA(()),
            pltpu.SemaphoreType.DMA((heads + 1,)),
        ],
        input_output_aliases={first: 0, first + 1: 1} if step else {},
        compiler_params=pltpu.CompilerParams(vmem_limit_bytes=24 * 1024 * 1024),
        name="project",
        cost_estimate=cost(2),
    )(scalars, weights, biases, *pieces, *held_before)


def attend(size, first, heads, order, wide, mask, qkv, extra, after):
    count = qkv.shape[1]
    half = count // size // 2
    row = pl.BlockSpec((1, 1, count), lambda h: (h + first, 0, 0))
    block = pl.BlockSpec((1, count, WIDE), lambda h: (h + first, 0, 0))
    column = pl.BlockSpec((1, count, CL), lambda h: (h + first, 0, 0))
    shapes = [shape_of((heads, count, WIDE))] + [shape_of((heads * half + extra.shape[0], PAIR))] * size
    return call(
        functools.partial(forward_kernel, size, heads, count // 2), "attend",
        [row, column, column, block, full(extra.shape)],
        [pl.BlockSpec((1, count, WIDE), lambda h: (h, 0, 0))] + [full(s.shape) for s in shapes[1:]], shapes,
        [pltpu.VMEM((count, PAIR), BF16)],
        cost(6.5 * heads), 60 if heads == 1 else 40, grid=(heads,), after=after,
    )(order, wide, mask, qkv, extra)


def attend_back(size, head, order, wide, mask, slots, place, turned_x, grad_context, after):
    count = slots.shape[1]
    rows = count // size
    cut = turned_x.shape[0] // 2
    shapes = (
        [shape_of((rows + rows // 2, PAIR))] * size + [shape_of((cut, WIDE))] * 2 + [shape_of((1, PAIR), F32)]
    )
    return call(
        functools.partial(backward_kernel, size, count // 2), "attend_back",
        [head_spec((1, count), head), head_spec((count, CL), head), head_spec((count, CL), head)]
        + [head_spec((count, WIDE), place), full(turned_x.shape)]
        + [pl.BlockSpec((rows // 2, PAIR), lambda i: (head, 0))] * size,
        [full(s.shape) for s in shapes], shapes,
        [pltpu.VMEM((count, PAIR), BF16), pltpu.VMEM((count, WIDE), BF16), pltpu.VMEM((count, WIDE), BF16)],
        cost(3), 40, after=after,
    )(order, wide, mask, slots, turned_x, *grad_context)


def layer(heads, layout, hidden, scalars, inputs, out_grad, vectors, received, ff):
    size = layout[0]
    rows, width = inputs.shape
    block = ff.shape[1]
    head_lanes = block - 2 * hidden
    shapes = [
        shape_of((rows, width)),
        shape_of((rows, width), F32),
        shape_of((8 + size, width), F32),
        shape_of((width, size * block)),
    ] + [shape_of((heads * (rows // 2), PAIR))] * size
    args = (inputs, out_grad, vectors)

    def kept(shape, dtype=BF16):
        return pltpu.VMEM(shape, dtype)

    return call(
        functools.partial(layer_kernel, heads, layout), "layer",
        [scalars_spec()] + [full(a.shape) for a in args] + [held()] + [full(r.shape) for r in received],
        [full(s.shape) if i != 3 else held() for i, s in enumerate(shapes)], shapes,
        [
            kept((width, size * hidden)),
            kept((width, size * hidden)),
            kept((width, size * head_lanes)),
            kept((rows, size * hidden)),
            kept((rows, size * hidden), F32),
            kept((rows, width), F32),
            kept((rows, hidden)),
            kept((rows, width)),
            kept((rows, width)),
            kept((rows, width)),
            kept((rows, size * head_lanes)),
            kept((width, rows)),
            kept((width, rows)),
            kept((width, 2 * hidden)),
            pltpu.SemaphoreType.DMA((3,)),
            pltpu.SemaphoreType.DMA((1 + size,)),
        ],
        cost(33), 58,
    )(scalars, *args, ff, *received)


def totals(hidden, local_width, parts):
    rows, lanes = parts[0].shape
    shapes = [shape_of((rows, hidden), F32), shape_of((rows, hidden), F32), shape_of((local_width, rows), F32)]
    return call(
        functools.partial(total_kernel, hidden), "totals",
        [full(part.shape) for part in parts], [full(s.shape) for s in shapes], shapes,
        [pltpu.VMEM((-(-rows // CL) * CL, lanes - 2 * hidden), F32)],
        cost(1), 32,
    )(*parts)


def flip(size, pick, left):
    count, width = left.shape
    rows = count // size
    return call(
        flip_kernel, "flip",
        [full(pick.shape), pl.BlockSpec((rows, width), lambda i: (i, 0))],
        pl.BlockSpec((width, rows), lambda i: (0, i)), shape_of((width, count)), [],
        cost(0.05), 16, grid=(size,),
    )(pick, left)


def finish(head, layout, scalars, total, weights, grads, after):
    size = layout[0]
    rows, width = total.shape
    return call(
        functools.partial(finish_kernel, head, layout), "finish",
        [scalars_spec(), full(total.shape), held()] + [full(g.shape) for g in grads],
        full(total.shape), shape_of(total.shape, F32),
        [
            pltpu.VMEM((width, size * WIDE), BF16),
            pltpu.VMEM((rows, size * WIDE), BF16),
            pltpu.SemaphoreType.DMA(()),
        ],
        cost(1), 24, after=after,
    )(scalars, total, weights, *grads)


def shift(values, size, k):
    return lax.ppermute(values, "tensor", [(i, (i + k) % size) for i in range(size)])


def exchange(parts, size):
    return [parts[0]] + [shift(parts[size - k], size, k) for k in range(1, size)]


def line_step(up, down, k, size):
    return (
        lax.ppermute(up, "tensor", [(i, i + 1) for i in range(k - 1, size - 1)]),
        lax.ppermute(down, "tensor", [(i + 1, i) for i in range(0, size - k)]),
    )


def gather_line(own, size):
    ups, downs = [own], [own]
    for k in range(1, size):
        up, down = line_step(ups[-1], downs[-1], k, size)
        ups.append(up)
        downs.append(down)
    return ups[1:], downs[1:]


def swap(values, axis, bit):
    return lax.ppermute(values, axis, [(i, i ^ bit) for i in range(lax.axis_size(axis))])


def bits_of(size):
    return [1 << b for b in range(size.bit_length() - 1)]


def add_low(left, right):
    return (left.astype(F32) + right.astype(F32)).astype(BF16)


def halves(mine, arrived):
    cut = mine.shape[0] // 2
    return add_low(mine[:cut], arrived[:cut]), add_low(mine[cut:], arrived[cut:])


def tie(*groups):
    return lax.optimization_barrier(groups)


def local(
    inputs, out_grad, seq_lengths, balance, clusters, query_weight, query_bias, key_weight,
    value_weight, value_bias, out_weight, out_bias, norm1_gain, norm1_bias, up_weight, up_bias,
    down_weight, down_bias, norm2_gain, norm2_bias,
):
    dp = ("chip", "core")
    rows, width = inputs.shape
    size = lax.axis_size("tensor")
    chips = lax.axis_size("chip")
    rank, chip, core = (lax.axis_index(axis) for axis in ("tensor", "chip", "core"))
    shard = query_weight.shape[0]
    local_width = query_weight.shape[1]
    heads = clusters.shape[1]
    seqs = seq_lengths.shape[1]
    bits = bits_of(chips)

    bounds = jnp.cumsum(seq_lengths[0])
    scalars = jnp.concatenate([jnp.stack([rank, core, jnp.int32(rows)]), bounds]).astype(jnp.int32)
    direct = shard % 16 == 0
    layout = (size, 2 * chips if direct else 1, shard)
    hidden = up_weight.shape[1]

    def whole(near):
        rows_in = lax.all_gather(near, dp, axis=0, tiled=True)
        if direct:
            return rows_in
        lanes = near.shape[1]
        return rows_in.reshape(2 * chips, size, shard, lanes).transpose(1, 0, 2, 3).reshape(size * width, lanes)

    head_weights, ff_own = prepare(
        query_weight, key_weight, value_weight, out_weight, up_weight, down_weight.T, heads
    )
    ups, downs = gather_line(inputs, size)
    ff_ups, ff_downs = [ff_own], [ff_own]
    for k in range(1, size):
        if k == size - 1:
            ff_ups[-1], ff_downs[-1], ups[0], downs[0] = tie(ff_ups[-1], ff_downs[-1], ups[0], downs[0])
        one_up, one_down = line_step(ff_ups[-1], ff_downs[-1], k, size)
        ff_ups.append(one_up)
        ff_downs.append(one_down)
    near = jnp.concatenate(
        [ff_own] + [jnp.where(rank >= k, ff_ups[k], ff_downs[size - k]) for k in range(1, size)], axis=0
    )
    own_qkv = lax.all_gather(head_weights, dp, axis=0, tiled=True)
    near, own_qkv = tie(near, own_qkv)
    ff = whole(near)
    blank = jnp.zeros((heads, HD), F32)
    head_biases = jnp.concatenate(
        [query_bias.reshape(heads, HD), value_bias.reshape(heads, HD), blank, blank], axis=-1
    ).reshape(1, heads * WIDE)
    terms, rest = [], up_bias
    for _ in range(3):
        term = lax.reduce_precision(rest, 8, 7)
        terms.append(term.astype(BF16))
        rest = rest - term
    extra = jnp.concatenate(terms).reshape(-1, PAIR)
    extra = jnp.pad(extra, ((0, -extra.shape[0] % 16), (0, 0)))
    vectors = jnp.stack([out_bias, norm1_gain, norm1_bias, down_bias, norm2_gain, norm2_bias])

    def row_pick(order_bits):
        place = jnp.arange(width, dtype=jnp.int32)
        block = place // shard
        away = jnp.zeros_like(block)
        for depth, bit in enumerate(order_bits):
            away = away + ((block >> (len(order_bits) - 1 - depth)) & 1) * bit
        near = chip ^ away
        owner = near * 2 + (core ^ (block // chips))
        return one_hot((owner * shard + place % shard)[:, None] == place[None, :])

    pick = row_pick(bits)
    order, wide, mask = slot_tokens(seqs, scalars, clusters[0][:, None, :], balance)
    whole_rows = []
    for step in range(size):
        pieces = [ups[step - 1], downs[step - 1]] if step else [inputs]
        whole_rows = project(size, heads, step, scalars, own_qkv, head_biases, pieces, whole_rows)
    x_all, qkv = whole_rows
    later_weights, qkv = tie(head_weights, qkv)
    later_near = jnp.concatenate([later_weights] + [shift(later_weights, size, k) for k in range(1, size)], axis=0)

    kept_a, *context_a = attend(size, 0, heads - 1, order, wide, mask, qkv, extra, [])
    context_a, later_near = tie(context_a, later_near)
    later = whole(later_near)
    received = exchange(context_a, size)
    kept_b, *context_b = attend(size, heads - 1, 1, order, wide, mask, qkv, extra[:16], [context_a[0]])
    received, context_b = tie(received, context_b)
    received = received + exchange(context_b, size)
    slots = [(kept_a, h) for h in range(heads - 1)] + [(kept_b, 0)]
    turned_x = flip(size, pick, x_all)
    layer_out, grad_summed, small, grads, *grad_ctx = layer(
        heads, layout, hidden, scalars, inputs, out_grad, vectors, received, ff
    )
    arrived = exchange(grad_ctx, size)
    grads, later = tie(grads, later)
    grads = lax.psum_scatter(grads, dp, scatter_dimension=0, tiled=True)

    backs, head_mine, head_other, bias_sums = [], [], [], []
    for h in range(heads):
        after = backs[h - 2][1:] if h >= 2 else []
        outs = attend_back(size, h, order, wide, mask, *slots[h], turned_x, arrived, after)
        backs.append(exchange(outs[:size], size))
        head_mine.append(outs[size])
        head_other.append(outs[size + 1])
        bias_sums.append(outs[size + 2])
        if h < len(bits_of(size)):
            small = small + swap(small, "tensor", bits_of(size)[h])
            arrived, small = tie(arrived, small)
    backs[heads - 2], head_other = tie(backs[heads - 2], head_other)
    mine = jnp.concatenate(head_mine, axis=1)
    far = swap(jnp.concatenate(head_other, axis=1), "core", 1)
    sums = jnp.concatenate([small, jnp.pad(jnp.concatenate(bias_sums, axis=0), ((0, 0), (0, width - PAIR)))], axis=0)
    sums = sums + swap(sums, "core", 1)
    grad_inputs = grad_summed
    for h in range(heads - 1):
        grad_inputs = finish(h, layout, scalars, grad_inputs, later, backs[h], [])
    for bit in bits:
        mine, sent = halves(mine, far)
        far = swap(sent, "chip", bit)
        sums = sums + swap(sums, "chip", bit)
    head_sum = add_low(mine, far)
    bias = sums[small.shape[0] :]
    grad_query_bias = bias[:, :HD].reshape(local_width)
    grad_value_bias = bias[:, HD:PAIR].reshape(local_width)
    grad_up_bias = lax.dynamic_index_in_dim(sums, 8 + rank, 0, keepdims=False)
    lanes = grads.shape[1] // size
    parts = [grads[:, k * lanes : (k + 1) * lanes] for k in range(size)]
    parts, grad_inputs, back_last, head_sum = tie(parts, grad_inputs, backs[heads - 1], head_sum)
    backs[heads - 1] = back_last
    moved = exchange(parts, size)
    grad_query_weight, grad_key_weight, grad_value_weight = unmix(head_sum, local_width)
    grad_up_weight, grad_down_weight, grad_out_weight = totals(hidden, local_width, moved)
    grad_inputs = finish(heads - 1, layout, scalars, grad_inputs, later, backs[heads - 1], [])
    grad_down_weight = grad_down_weight.T
    return (
        layer_out, grad_inputs, grad_query_weight, grad_query_bias, grad_key_weight, grad_value_weight,
        grad_value_bias, grad_out_weight, sums[0], sums[1], sums[2], grad_up_weight, grad_up_bias,
        grad_down_weight, sums[3], sums[4], sums[5],
    )


def solution(mesh):
    devices = mesh.devices
    split = Mesh(devices.reshape(devices.shape[0] // 2, 2, devices.shape[1]), ("chip", "core", "tensor"))
    dp = ("chip", "core")
    rows, weight, turned_weight, vector, same = (
        P(dp + ("tensor",), None),
        P(dp, "tensor"),
        P("tensor", dp),
        P("tensor"),
        P(),
    )
    in_specs = (
        rows, rows, P(dp, None), P(dp, None), P(dp, "tensor", None), weight, vector, weight, weight,
        vector, turned_weight, same, same, same, weight, vector, turned_weight, same, same, same,
    )
    out_specs = (
        rows, rows, weight, vector, weight, weight, vector, turned_weight, same, same, same, weight, vector,
        turned_weight, same, same, same,
    )
    return jax.shard_map(local, mesh=split, in_specs=in_specs, out_specs=out_specs, check_vma=False)
```
